32 devices in a mesh: groups: 2 (over y), wide: 4 (over z), narrow: 4 (over x, core).
Axes of the slice: x: 2, y: 2, z: 4, core: 2. Of those that a mesh axis runs over, the one named last changes fastest.
Arguments:
- hidden: bfloat16 [4096, 4096], P(('groups', 'wide')), parts along dimension 0, may hold values from -16 to 16
- w_qkv: bfloat16 [4096, 3, 2048], P('wide', None, 'narrow'), may hold values from -0.09375 to 0.09375
- w_out: bfloat16 [2048, 4096], P(None, 'wide'), may hold values from -0.125 to 0.125
- seg_ids: int32 [4096], P('groups'), parts along dimension 0, may hold values from 0 to 3, never falling along the last dimension, each value on 1 to 1024 neighbouring positions
- shift_heads: int32 [16], replicated, may hold values from 0 to 1, as said below
Outputs:
- layer_out: bfloat16 [4096, 4096], P(('groups', 'wide', 'narrow')), parts along dimension 0
The draws below stay inside these ranges and needn't reach their ends.
There are 2 independent parts, one for each index of `groups`. The reference program is written for one: setup_inputs(seed, part) draws one part's arguments, and reference() takes and returns one part's arrays. A program takes and returns all parts, laid end to end along the dimension named above; an argument that names none is the same for every part. Nothing has to cross between parts.
Inputs may be any that keep to these rules, and one draw needn't show every extreme that they name: `shift_heads`: exactly half of the heads are marked with 1, the others with 0. `seg_ids`: never falls along the window; every number occurs on 1 to 1024 consecutive tokens, one on exactly that many.
All inputs are finite; a program needn't handle non-finite values.
Results may differ from the reference program's by a relative error of at most 0.012.
Values may be sent and summed in bfloat16 or wider, within the bound.
A program may use at most 128 MiB of HBM per device.

```python
import math
import jax
import jax.numpy as jnp
import numpy as np
from jax import lax

D = 4096
HEAD_DIM = 128
HEADS = 16
GROUP = 512
SHIFT = 256
TOK_DEV = 512
TOKENS = 2048
N_WIDE = 4


def draw_hidden(key, part):
    first_key = jax.random.fold_in(jax.random.fold_in(key, 11), 0)
    result = jnp.clip(jax.random.normal(first_key, (TOKENS, D), jnp.float32), -6.0, 6.0)
    return result.astype(jnp.bfloat16)


def draw_shift_heads(key, part):
    order = jax.random.permutation(jax.random.fold_in(key, 23), HEADS)
    return (order < HEADS // 2).astype(jnp.int32)


def levels(own_key, extent, cuts, least, largest):
    def one(dim, parts):
        steps = jax.random.uniform(jax.random.fold_in(jax.random.fold_in(own_key, 6), dim), (parts,), jnp.float32, least / len(cuts), largest / len(cuts))
        return jnp.repeat(jnp.exp(steps), extent[dim] // parts).reshape((-1,) + (1,) * (len(extent) - dim - 1))

    loudness = one(*cuts[0])
    for cut in cuts[1:]:
        loudness = loudness * one(*cut)
    return loudness


def split_up(number_of, total, most, lean):
    loads = [(1 << 20) // math.isqrt(standing ** lean) + 1 for standing in range(2, number_of + 1)]
    surplus, holding = total - most - (number_of - 1), [1] * (number_of - 1)
    while surplus > 0:
        candidates = [i for i in range(number_of - 1) if holding[i] < most]
        mass, left = sum([loads[i] for i in candidates]), surplus
        for i in candidates:
            more = min(most - holding[i], max(1, left * loads[i] // mass), surplus)
            holding[i] = holding[i] + more
            surplus = surplus - more
    return np.array([most] + holding)


def uneven_parts(key, count, total, limit, slope):
    if count == 2:
        one = jax.random.randint(key, (), max(1, total - limit), min(limit, total - 1) + 1)
        return jnp.stack([one, total - one])
    sizes = jnp.asarray(split_up(count, total, limit, slope), jnp.int32)
    couples = (count - 1) // 2
    giver, taker = sizes[1:1 + 2 * couples:2], sizes[2:2 + 2 * couples:2]
    slack = jnp.minimum(giver - 1, limit - taker)
    passed = jax.random.randint(jax.random.fold_in(key, 1), (couples,), 0, 1 << 20) % (slack + 1)
    sizes = sizes.at[1:1 + 2 * couples:2].set(giver - passed).at[2:2 + 2 * couples:2].set(taker + passed)
    return sizes[jax.random.permutation(jax.random.fold_in(key, 2), count)]


def centred(own_key, extent, spread, bound, cuts=(), kind=jnp.bfloat16):
    factor_of = levels(own_key, extent, cuts, -0.22, 0.18) if cuts else 1.0
    values = jax.random.normal(own_key, extent, jnp.float32) * spread * factor_of
    return jnp.minimum(jnp.maximum(values, -bound), bound).astype(kind)


def setup_inputs(seed: int = 0, part: int = 0) -> dict:
    keys = jax.random.split(jax.random.key(seed), 6)
    own_keys = jax.random.split(jax.random.fold_in(keys[5], part), 6)
    hidden = draw_hidden(jax.random.fold_in(jax.random.fold_in(keys[5], part), 71), part)
    w_qkv = centred(keys[1], (D, 3, HEADS * HEAD_DIM), D ** -0.5, 0.09375, ((0, 4), (2, 4)))
    w_out = centred(keys[2], (HEADS * HEAD_DIM, D), (HEADS * HEAD_DIM) ** -0.5, 0.125, ((1, 4),))
    seg_ids = jnp.searchsorted(jnp.cumsum(uneven_parts(own_keys[3], N_WIDE, TOKENS, 2 * TOK_DEV, 2)), jnp.arange(TOKENS), side="right").astype(jnp.int32)
    shift_heads = draw_shift_heads(jax.random.fold_in(keys[5], 71), part)
    return dict(hidden=hidden, w_qkv=w_qkv, w_out=w_out, seg_ids=seg_ids, shift_heads=shift_heads)


masked_out = -1e+30

def attend(query_rows, key_rows, value_rows, allowed):
    scores = jnp.einsum('ihd,jhd->hij', query_rows.astype(jnp.float32), key_rows.astype(jnp.float32)) * (1.0 / math.sqrt(HEAD_DIM))
    scores = jnp.where(allowed, scores, masked_out)
    row_max = lax.optimization_barrier(jnp.max(scores, axis=-1, keepdims=True))
    exponent = jnp.exp(scores - row_max)
    weights = (exponent / lax.optimization_barrier(jnp.sum(exponent, axis=-1, keepdims=True))).astype(jnp.bfloat16)
    combined = jnp.einsum('hij,jhd->ihd', weights.astype(jnp.float32), value_rows.astype(jnp.float32))
    return combined.astype(jnp.bfloat16)

def reference(hidden, w_qkv, w_out, seg_ids, shift_heads):
    width = HEADS * HEAD_DIM
    projected = jnp.dot(hidden, w_qkv.reshape(D, 3 * width), preferred_element_type=jnp.float32).astype(jnp.bfloat16)
    projected = projected.reshape(TOKENS, 3, HEADS, HEAD_DIM)
    shifted = shift_heads > 0
    moved_qkv = jnp.where(shifted[None, None, :, None], jnp.roll(projected, -SHIFT, axis=0), projected)
    seg_heads = jnp.where(shifted[:, None], jnp.roll(seg_ids, -SHIFT)[None, :], seg_ids[None, :])
    groups_all = TOKENS // GROUP
    blocks = moved_qkv.reshape(groups_all, GROUP, 3, HEADS, HEAD_DIM)
    block_segs = seg_heads.reshape(HEADS, groups_all, GROUP).transpose(1, 0, 2)
    positions = jnp.arange(GROUP, dtype=jnp.int32)
    causal = positions[:, None] >= positions[None, :]

    def one_group(inputs):
        block_qkv, block_seg = inputs
        allowed = causal[None] & (block_seg[:, :, None] == block_seg[:, None, :])
        return attend(block_qkv[:, 0], block_qkv[:, 1], block_qkv[:, 2], allowed)
    rolled_out = lax.map(one_group, (blocks, block_segs)).reshape(TOKENS, HEADS, HEAD_DIM)
    attended = jnp.where(shifted[None, :, None], jnp.roll(rolled_out, SHIFT, axis=0), rolled_out)
    return jnp.dot(attended.reshape(TOKENS, width), w_out, preferred_element_type=jnp.float32).astype(jnp.bfloat16)
```

```python
import functools
import math

import jax
import jax.numpy as jnp
from jax import lax
from jax.experimental import pallas as pl
from jax.experimental.pallas import tpu as pltpu
from jax.sharding import PartitionSpec as P

HEAD_DIM = 128
GROUP = 512
SHIFT = 256

masked_out = -1e30
MESH = pl.DeviceIdType.MESH
ROWS = 128
WO_CHUNKS = 4
DIRECT = 5


def layer_kernel(
    n, narrow, chunks, wo_chunks,
    hidden_ref, wq_ref, wo_ref, segq_ref, segk_ref, out_ref,
    wbuf, acc, wo_buf, q_buf, kv_buf, att, part, pair_in, pair_sum, far_in,
    own_sem,
    qs_r, qs_l, qr, qs_y, qr_y,
    os_r, os_l, o_r, os_y, or_y,
    kv_sem, pair_s, pair_r, far_s, far_r,
):
    me = lax.axis_index("wide")
    y = lax.axis_index("groups")
    spot = lax.axis_index("narrow")
    other = 1 - y
    across_n = narrow // 2
    high, low = spot // 2, lax.rem(spot, 2)
    depth = wq_ref.shape[1]
    half = wbuf.shape[3]
    tok = hidden_ref.shape[0]
    rows = depth // chunks
    steps = (n - 1) * chunks
    wo_rows = wo_buf.shape[2] // wo_chunks
    cols = wo_buf.shape[3]
    blocks = tok // SHIFT
    per_half = half // HEAD_DIM
    has_left, has_right = me > 0, me < n - 1
    right, left = {"wide": me + 1}, {"wide": me - 1}
    after, before = {"wide": lax.rem(me + 1, n)}, {"wide": lax.rem(me + n - 1, n)}
    opposite = {"groups": other}
    pair = {"narrow": high * 2 + 1 - low}
    far = [{"narrow": lax.rem(high + d, across_n) * 2 + low} for d in range(1, across_n)]
    far_from = [{"narrow": lax.rem(high + across_n - d, across_n) * 2 + low} for d in range(1, across_n)]

    barrier = pltpu.get_barrier_semaphore()
    greeted = [after, before, opposite, pair] + far
    for device in greeted:
        pl.semaphore_signal(barrier, inc=1, device_id=device, device_id_type=MESH)

    def w_at(shard, part_of, c):
        start = pl.multiple_of(shard * depth + c * rows, rows)
        return wbuf.at[part_of, :, pl.ds(start, rows)]

    def wq_own(c):
        return wq_ref.at[
            :, pl.ds(pl.multiple_of(c * rows, rows), rows), pl.ds(pl.multiple_of(y * half, half), half)
        ]

    def o_at(shard, part_of, c):
        return wo_buf.at[shard, part_of, pl.ds(pl.multiple_of(c * wo_rows, wo_rows), wo_rows)]

    def wo_own(c):
        return wo_ref.at[spot, y, pl.ds(pl.multiple_of(c * wo_rows, wo_rows), wo_rows)]

    def remote(src, dst, send, recv, device):
        return pltpu.make_async_remote_copy(
            src_ref=src, dst_ref=dst, send_sem=send, recv_sem=recv,
            device_id=device, device_id_type=MESH,
        )

    def q_right(shard, c, src=None):
        dst = w_at(shard, y, c)
        return remote(dst if src is None else src, dst, qs_r.at[shard, c], qr.at[shard, c], right)

    def q_left(shard, c, src=None):
        dst = w_at(shard, y, c)
        return remote(dst if src is None else src, dst, qs_l.at[shard, c], qr.at[shard, c], left)

    def q_across(shard, c, part_of):
        ref = w_at(shard, part_of, c)
        return remote(ref, ref, qs_y.at[shard, c], qr_y.at[shard, c], opposite)

    def o_right(shard, c, src=None):
        dst = o_at(shard, y, c)
        return remote(dst if src is None else src, dst, os_r.at[shard, c], o_r.at[shard, c], right)

    def o_left(shard, c, src=None):
        dst = o_at(shard, y, c)
        return remote(dst if src is None else src, dst, os_l.at[shard, c], o_r.at[shard, c], left)

    def o_across(shard, c, part_of):
        ref = o_at(shard, part_of, c)
        return remote(ref, ref, os_y.at[shard, c], or_y.at[shard, c], opposite)

    own = [
        pltpu.make_async_copy(
            wq_ref.at[:, :, pl.ds(h * half, half)],
            wbuf.at[h, :, pl.ds(pl.multiple_of(me * depth, depth), depth)],
            own_sem.at[h],
        )
        for h in range(2)
    ]
    own.append(pltpu.make_async_copy(wo_ref.at[spot], wo_buf.at[me], own_sem.at[2]))
    for copy in own:
        copy.start()
    pl.semaphore_wait(barrier, len(greeted))

    @pl.loop(0, chunks)
    def _(c):
        @pl.when(has_right)
        def _():
            q_right(me, c, wq_own(c)).start()

        @pl.when(has_left)
        def _():
            q_left(me, c, wq_own(c)).start()

    acc[...] = jnp.zeros_like(acc)
    own[0].wait()
    own[1].wait()

    def add(shard, part_of, c):
        start = pl.multiple_of(shard * depth + c * rows, rows)
        piece = hidden_ref[:, pl.ds(start, rows)]
        for i in range(3):
            acc[part_of, i] += jnp.dot(
                piece, wbuf[part_of, i, pl.ds(start, rows)], preferred_element_type=jnp.float32
            )

    @pl.loop(0, 2 * chunks)
    def _(i):
        add(me, i // chunks, lax.rem(i, chunks))

    def add_across(t):
        s, c = t // chunks, lax.rem(t, chunks)
        for there, shard in ((me - 1 - s >= 0, me - 1 - s), (me + 1 + s <= n - 1, me + 1 + s)):
            @pl.when(there)
            def _():
                q_across(shard, c, other).wait_recv()
                add(shard, other, c)

    def send_own_wo():
        @pl.loop(0, wo_chunks)
        def _(c):
            @pl.when(has_right)
            def _():
                o_right(me, c, wo_own(c)).start()

            @pl.when(has_left)
            def _():
                o_left(me, c, wo_own(c)).start()

    @pl.loop(0, steps)
    def _(t):
        s, c = t // chunks, lax.rem(t, chunks)

        @pl.when(t == steps - chunks)
        def _():
            send_own_wo()

        @pl.when(me - 1 - s >= 0)
        def _():
            q_right(me - 1 - s, c).wait_recv()

            @pl.when(has_right)
            def _():
                q_right(me - 1 - s, c).start()

            q_across(me - 1 - s, c, y).start()

        @pl.when(me + 1 + s <= n - 1)
        def _():
            q_left(me + 1 + s, c).wait_recv()

            @pl.when(has_left)
            def _():
                q_left(me + 1 + s, c).start()

            q_across(me + 1 + s, c, y).start()

        for there, shard in ((me - 1 - s >= 0, me - 1 - s), (me + 1 + s <= n - 1, me + 1 + s)):
            @pl.when(there)
            def _():
                add(shard, y, c)

        @pl.when(t > 0)
        def _():
            add_across(t - 1)

    add_across(steps - 1)
    for h in range(2):
        q_buf[h] = acc[h, 0].astype(jnp.bfloat16)
        for i in range(2):
            kv_buf[h, i, SHIFT:] = acc[h, 1 + i].astype(jnp.bfloat16)

    kv_copy = remote(
        kv_buf.at[:, :, pl.ds(tok, SHIFT)], kv_buf.at[:, :, pl.ds(0, SHIFT)],
        kv_sem.at[0], kv_sem.at[1], after,
    )
    kv_copy.start()

    causal = lax.broadcasted_iota(jnp.int32, (SHIFT, 2 * SHIFT), 1) <= (
        lax.broadcasted_iota(jnp.int32, (SHIFT, 2 * SHIFT), 0) + SHIFT
    )

    def attend(h, b):
        lanes = slice((h % per_half) * HEAD_DIM, (h % per_half + 1) * HEAD_DIM)
        mine, seen = slice(b * SHIFT, (b + 1) * SHIFT), slice(b * SHIFT, (b + 2) * SHIFT)
        keys, values = kv_buf.at[h // per_half, 0], kv_buf.at[h // per_half, 1]
        scores = lax.dot_general(
            q_buf[h // per_half, mine, lanes], keys[seen, lanes], (((1,), (1,)), ((), ())),
            preferred_element_type=jnp.float32,
        ) * (1.0 / math.sqrt(HEAD_DIM))
        allowed = causal & (segq_ref[mine, :] == segk_ref[h, b])
        scores = jnp.where(allowed, scores, masked_out)
        exponent = jnp.exp(scores - jnp.max(scores, axis=-1, keepdims=True))
        weights = exponent / jnp.sum(exponent, axis=-1, keepdims=True)
        att[mine, h * HEAD_DIM : (h + 1) * HEAD_DIM] = jnp.dot(
            weights.astype(jnp.bfloat16), values[seen, lanes], preferred_element_type=jnp.float32
        ).astype(jnp.bfloat16)

    least = jnp.minimum(me, n - 1 - me)

    def block_of(k):
        turn = (k + 1) // 2
        near = jnp.where(lax.rem(k, 2) == 1, me - turn, me + turn)
        rest = jnp.where(me > least, me - (k - least), me + (k - least))
        return jnp.where(k <= 2 * least, near, rest)

    def pass_on(k):
        shard = block_of(k)

        @pl.loop(0, wo_chunks)
        def _(c):
            o_right(shard, c).wait_recv()

            @pl.when(jnp.logical_and(shard < me, has_right))
            def _():
                o_right(shard, c).start()

            @pl.when(jnp.logical_and(shard > me, has_left))
            def _():
                o_left(shard, c).start()

            o_across(shard, c, y).start()

    def pair_copy(shard, a):
        return remote(
            part.at[shard, a * 2 + 1 - low], pair_in.at[shard, a],
            pair_s.at[shard, a], pair_r.at[shard, a], pair,
        )

    def far_copy(shard, d):
        a = lax.rem(high + d, across_n)
        return remote(
            pair_sum.at[shard, a], far_in.at[shard, d - 1],
            far_s.at[shard, d - 1], far_r.at[shard, d - 1], far[d - 1],
        )

    def far_arrival(shard, d):
        return remote(
            pair_sum.at[shard, high], far_in.at[shard, d - 1],
            far_s.at[shard, d - 1], far_r.at[shard, d - 1], far_from[d - 1],
        )

    def multiply(k):
        shard = block_of(k)
        width = att.shape[1] // 2
        share = tok // narrow
        for p in range(narrow):
            a_rows = att[p * share : (p + 1) * share, :]
            total = jnp.dot(a_rows[:, :width], wo_buf[shard, 0], preferred_element_type=jnp.float32)
            total += jnp.dot(a_rows[:, width:], wo_buf[shard, 1], preferred_element_type=jnp.float32)
            part[shard, p] = total.astype(jnp.bfloat16)
        for a in range(across_n):
            pair_copy(shard, a).start()

    def sum_pair(k):
        shard = block_of(k)
        for a in range(across_n):
            pair_copy(shard, a).wait_recv()
            total = part[shard, a * 2 + low].astype(jnp.float32) + pair_in[shard, a].astype(jnp.float32)
            pair_sum[shard, a] = total.astype(jnp.bfloat16)
        for d in range(1, across_n):
            far_copy(shard, d).start()

    def finish(k):
        shard = block_of(k)
        total = part[shard, high * 2 + low].astype(jnp.float32) + pair_in[shard, high].astype(jnp.float32)
        for d in range(1, across_n):
            far_arrival(shard, d).wait_recv()
            total += far_in[shard, d - 1].astype(jnp.float32)
        out_ref[:, pl.ds(pl.multiple_of(shard * cols, cols), cols)] = total.astype(out_ref.dtype)

    heads = 2 * per_half
    for b in range(1, blocks):
        for h in range(heads):
            attend(h, b)
    pass_on(1)
    pass_on(2)
    kv_copy.wait_recv()
    for h in range(heads):
        attend(h, 0)
    own[2].wait()
    multiply(0)

    @pl.loop(1, n)
    def _(k):
        @pl.when(k > 2)
        def _():
            pass_on(k)

        sum_pair(k - 1)

        @pl.when(k > 1)
        def _():
            finish(k - 2)

        shard = block_of(k)

        @pl.loop(0, wo_chunks)
        def _(c):
            o_across(shard, c, other).wait_recv()

        multiply(k)

    sum_pair(n - 1)
    finish(n - 2)
    finish(n - 1)

    kv_copy.wait_send()

    @pl.loop(0, n)
    def _(shard):
        for a in range(across_n):
            pair_copy(shard, a).wait_send()
        for d in range(1, across_n):
            far_copy(shard, d).wait_send()
        goes_right = jnp.logical_and(shard <= me, has_right)
        goes_left = jnp.logical_and(shard >= me, has_left)
        for count, to_right, to_left, to_other in (
            (chunks, q_right, q_left, q_across), (wo_chunks, o_right, o_left, o_across)
        ):
            @pl.loop(0, count)
            def _(c):
                @pl.when(goes_right)
                def _():
                    to_right(shard, c).wait_send()

                @pl.when(goes_left)
                def _():
                    to_left(shard, c).wait_send()

                @pl.when(shard != me)
                def _():
                    to_other(shard, c, y).wait_send()


def layer(hidden, wq, wo, seg_q, seg_k):
    n, narrow = lax.axis_size("wide"), lax.axis_size("narrow")
    tok, width = hidden.shape
    half = wq.shape[2] // 2
    chunks = max(1, wq.shape[1] // ROWS)
    wo_chunks = WO_CHUNKS
    cols = wo.shape[3]
    share = tok // narrow
    vmem = pl.BlockSpec(memory_space=pltpu.VMEM)
    hbm = pl.BlockSpec(memory_space=pl.ANY)
    dma = pltpu.SemaphoreType.DMA
    bf16 = jnp.bfloat16
    return pl.pallas_call(
        functools.partial(layer_kernel, n, narrow, chunks, wo_chunks),
        out_shape=jax.ShapeDtypeStruct((share, n * cols), bf16),
        in_specs=[vmem, hbm, hbm, vmem, vmem],
        out_specs=vmem,
        scratch_shapes=[
            pltpu.VMEM((2, 3, width, half), bf16),
            pltpu.VMEM((2, 3, tok, half), jnp.float32),
            pltpu.VMEM((n,) + wo.shape[1:], bf16),
            pltpu.VMEM((2, tok, half), bf16),
            pltpu.VMEM((2, 2, tok + SHIFT, half), bf16),
            pltpu.VMEM((tok, 2 * half), bf16),
            pltpu.VMEM((n, narrow, share, cols), bf16),
            pltpu.VMEM((n, narrow // 2, share, cols), bf16),
            pltpu.VMEM((n, narrow // 2, share, cols), bf16),
            pltpu.VMEM((n, max(1, narrow // 2 - 1), share, cols), bf16),
            dma((3,)),
        ]
        + [dma((n, chunks))] * 5
        + [dma((n, wo_chunks))] * 5
        + [dma((2,))]
        + [dma((n, narrow // 2))] * 2
        + [dma((n, max(1, narrow // 2 - 1)))] * 2,
        compiler_params=pltpu.CompilerParams(
            collective_id=0, has_side_effects=True, vmem_limit_bytes=58 * 1024 * 1024
        ),
    )(hidden, wq, wo, seg_q, seg_k)


def per_device(hidden, w_qkv, w_out, seg_ids, shift_heads):
    tok_rows = hidden.shape[0]
    local_f = w_qkv.shape[2]
    heads_here = local_f // HEAD_DIM
    blocks = tok_rows // SHIFT
    narrow = lax.axis_size("narrow")
    first_tok = lax.axis_index("wide") * tok_rows
    shifted = lax.dynamic_slice_in_dim(shift_heads, lax.axis_index("narrow") * heads_here, heads_here) > 0

    doubled = jnp.concatenate([seg_ids[-SHIFT:], seg_ids], 0)
    seg_here = lax.dynamic_slice_in_dim(doubled, first_tok, tok_rows + SHIFT)
    seg_q = seg_here[SHIFT:, None]
    windows = jnp.stack([seg_here[b * SHIFT : (b + 2) * SHIFT] for b in range(blocks)])
    odd = (jnp.arange(blocks) % 2 == 1)[None, :, None]
    reaches = (shifted[:, None, None] != odd) | (jnp.arange(2 * SHIFT) >= SHIFT)[None, None, :]
    seg_k = jnp.where(reaches, windows[None], -1)[:, :, None, :]

    wq = w_qkv.transpose(1, 0, 2)
    wo = w_out.reshape(narrow, 2, local_f // 2, -1)
    return layer(hidden, wq, wo, seg_q, seg_k)


def hub_kernel(
    chunks, wo_chunks, direct,
    hidden_ref, wq_ref, wo_ref, segq_ref, segk_ref, out_ref,
    wbuf, hid, acc, q_buf, kv_buf, att, wo_buf, stage,
    own_sem, he_s, he_r, hx_s, hx_r, hc_s, hc_r,
    wm_s, wm_r, we_s, we_r, wy_s, wy_r, kv_sem,
    om_s, om_r, oe_s, oe_r, oy_s, oy_r,
    ax_s, ax_r, ac_s, ac_r, res_s, res_r,
):
    n, narrow = lax.axis_size("wide"), lax.axis_size("narrow")
    me = lax.axis_index("wide")
    y = lax.axis_index("groups")
    spot = lax.axis_index("narrow")
    opp = 1 - y
    side = me // (n // 2)
    inner, outer = n // 2 - 1 + side, side * (n - 1)
    far_inner, far_outer = n - 1 - inner, n - 1 - outer
    is_inner, is_outer = me == inner, me == outer
    high, low = spot // 2, lax.rem(spot, 2)
    core_n, x_n = high * 2 + 1 - low, (1 - high) * 2 + low
    diag_n = (1 - high) * 2 + 1 - low
    depth = wq_ref.shape[1]
    tok = hidden_ref.shape[0]
    half = wbuf.shape[3]
    rows = depth // chunks
    pair_rows = 2 * rows
    pairs = chunks // 2
    quarter = tok // narrow
    span = 2 * tok
    blocks = span // SHIFT
    own_pos = 1 - side
    own_row = pl.multiple_of(own_pos * tok, tok)
    far_row = pl.multiple_of(side * tok, tok)
    wo_half, wo_cols = wo_buf.shape[2], wo_buf.shape[3]
    wo_rows = wo_half // wo_chunks
    cols = wo_ref.shape[1]
    per_half = half // HEAD_DIM
    heads = 2 * per_half
    to_core, to_x, to_y = {"narrow": core_n}, {"narrow": x_n}, {"groups": opp}
    to_far, to_inner = {"wide": far_inner}, {"wide": inner}

    def remote(src, dst, send, recv, device):
        return pltpu.make_async_remote_copy(
            src_ref=src, dst_ref=dst, send_sem=send, recv_sem=recv,
            device_id=device, device_id_type=MESH,
        )

    def w_at(shard, part, c):
        start = pl.multiple_of(shard * depth + c * rows, rows)
        return wbuf.at[part, :, pl.ds(start, rows)]

    def wq_at(part, c):
        return wq_ref.at[
            :, pl.ds(pl.multiple_of(c * rows, rows), rows), pl.ds(pl.multiple_of(part * half, half), half)
        ]

    def o_at(shard, part, c):
        return wo_buf.at[shard, part, pl.ds(pl.multiple_of(c * wo_rows, wo_rows), wo_rows)]

    def wo_at(part, c):
        start = pl.multiple_of(part * wo_half + c * wo_rows, wo_rows)
        return wo_ref.at[pl.ds(start, wo_rows), pl.ds(pl.multiple_of(spot * wo_cols, wo_cols), wo_cols)]

    def h_at(row_n, k):
        start = pl.multiple_of(far_row + row_n * quarter, quarter)
        return hid.at[pl.ds(start, quarter), pl.ds(pl.multiple_of(k * depth, depth), depth)]

    def h_end(k):
        src = hidden_ref.at[
            pl.ds(pl.multiple_of(spot * quarter, quarter), quarter), pl.ds(pl.multiple_of(k * depth, depth), depth)
        ]
        return remote(src, h_at(spot, k), he_s.at[k], he_r.at[k], to_inner)

    def h_x(k, row_n):
        return remote(h_at(row_n, k), h_at(row_n, k), hx_s.at[k], hx_r.at[k], to_x)

    def h_core(j, k, row_n):
        return remote(h_at(row_n, k), h_at(row_n, k), hc_s.at[j, k], hc_r.at[j, k], to_core)

    def w_end(j, c):
        part = y if j == 0 else opp
        return remote(wq_at(part, c), w_at(outer, part, c), we_s.at[j, c], we_r.at[j, c], to_inner)

    def w_mid_send(s, c):
        if s == 0:
            return remote(wq_at(y, c), w_at(inner, y, c), wm_s.at[s, c], wm_r.at[s, c], to_far)
        return remote(w_at(outer, y, c), w_at(outer, y, c), wm_s.at[s, c], wm_r.at[s, c], to_far)

    def far_shard(s):
        return jnp.where(s == 0, far_inner, far_outer)

    def w_mid_recv(s, c):
        ref = w_at(far_shard(s), y, c)
        return remote(ref, ref, wm_s.at[s, c], wm_r.at[s, c], to_far)

    def y_shard(s):
        return jnp.where(s == 2, outer, far_shard(s))

    def w_y(s, c, part):
        ref = w_at(y_shard(s), part, c)
        return remote(ref, ref, wy_s.at[s, c], wy_r.at[s, c], to_y)

    def o_end(j, c):
        part = y if j == 0 else opp
        return remote(wo_at(part, c), o_at(outer, part, c), oe_s.at[j, c], oe_r.at[j, c], to_inner)

    def o_mid_send(s, c):
        if s == 0:
            return remote(wo_at(y, c), o_at(inner, y, c), om_s.at[s, c], om_r.at[s, c], to_far)
        return remote(o_at(outer, y, c), o_at(outer, y, c), om_s.at[s, c], om_r.at[s, c], to_far)

    def o_mid_recv(s, c):
        ref = o_at(far_shard(s), y, c)
        return remote(ref, ref, om_s.at[s, c], om_r.at[s, c], to_far)

    def o_y(s, c, part):
        ref = o_at(far_shard(s), part, c)
        return remote(ref, ref, oy_s.at[s, c], oy_r.at[s, c], to_y)

    def att_at(row_n, b):
        return att.at[row_n, pl.ds(b * SHIFT, SHIFT)]

    def att_x(b, row_n):
        return remote(att_at(row_n, b), att_at(row_n, b), ax_s.at[b], ax_r.at[b], to_x)

    def att_core(j, b, row_n):
        return remote(att_at(row_n, b), att_at(row_n, b), ac_s.at[j, b], ac_r.at[j, b], to_core)

    def res_cols(shard, row_n):
        return pl.ds(pl.multiple_of(shard * cols + row_n * wo_cols, wo_cols), wo_cols)

    def result(shard, pos, to_n):
        return remote(
            stage.at[shard, pl.ds(pos * tok + to_n * quarter, quarter)],
            out_ref.at[:, res_cols(shard, spot)],
            res_s.at[shard, pos, to_n], res_r.at[shard, spot],
            {"wide": side * (n // 2) + pos, "narrow": to_n},
        )

    def result_arrival(shard, from_n):
        ref = out_ref.at[:, res_cols(shard, from_n)]
        return remote(ref, ref, res_s.at[shard, 0, 0], res_r.at[shard, from_n], to_core)

    kv_copy = remote(
        kv_buf.at[:, :, pl.ds(span, SHIFT)], kv_buf.at[:, :, pl.ds(0, SHIFT)],
        kv_sem.at[0], kv_sem.at[1], to_far,
    )

    barrier = pltpu.get_barrier_semaphore()

    @pl.when(is_outer)
    def _():
        for p in range(narrow):
            pl.semaphore_signal(barrier, inc=1, device_id={"wide": inner, "narrow": p}, device_id_type=MESH)
        pl.semaphore_wait(barrier, narrow)

        @pl.loop(0, n)
        def _(k):
            h_end(k).start()

        @pl.loop(0, chunks)
        def _(c):
            w_end(0, c).start()

        @pl.loop(0, direct)
        def _(c):
            w_end(1, c).start()

        for j in range(2):
            @pl.loop(0, wo_chunks)
            def _(c):
                o_end(j, c).start()

        @pl.loop(0, n)
        def _(k):
            h_end(k).wait_send()

        @pl.loop(0, chunks)
        def _(c):
            w_end(0, c).wait_send()

        @pl.loop(0, direct)
        def _(c):
            w_end(1, c).wait_send()

        for j in range(2):
            @pl.loop(0, wo_chunks)
            def _(c):
                o_end(j, c).wait_send()

        @pl.loop(0, n)
        def _(shard):
            for p in range(narrow):
                result_arrival(shard, p).wait_recv()

    @pl.when(is_inner)
    def _():
        own = [
            pltpu.make_async_copy(
                wq_ref.at[:, :, pl.ds(h * half, half)],
                wbuf.at[h, :, pl.ds(pl.multiple_of(inner * depth, depth), depth)],
                own_sem.at[h],
            )
            for h in range(2)
        ]
        own.append(pltpu.make_async_copy(hidden_ref, hid.at[pl.ds(own_row, tok)], own_sem.at[2]))
        own += [
            pltpu.make_async_copy(
                wo_ref.at[pl.ds(h * wo_half, wo_half), pl.ds(pl.multiple_of(spot * wo_cols, wo_cols), wo_cols)],
                wo_buf.at[inner, h],
                own_sem.at[3 + h],
            )
            for h in range(2)
        ]
        for copy in own:
            copy.start()
        peers = [{"narrow": core_n}, {"narrow": x_n}, {"narrow": diag_n}, to_y, to_far]
        peers += [{"wide": outer, "narrow": p} for p in range(narrow)]
        for device in peers:
            pl.semaphore_signal(barrier, inc=1, device_id=device, device_id_type=MESH)
        pl.semaphore_wait(barrier, len(peers))

        @pl.loop(0, chunks)
        def _(c):
            w_mid_send(0, c).start()

        acc[...] = jnp.zeros_like(acc)

        def add(row, size, shard, part, p):
            start = pl.multiple_of(shard * depth + p * pair_rows, pair_rows)
            piece = hid[pl.ds(row, size), pl.ds(start, pair_rows)]
            for i in range(3):
                acc[part, i, pl.ds(row, size)] += jnp.dot(
                    piece, wbuf[part, i, pl.ds(start, pair_rows)], preferred_element_type=jnp.float32
                )

        for copy in own[:3]:
            copy.wait()

        @pl.loop(0, 2 * pairs)
        def _(u):
            add(own_row, tok, inner, u // pairs, lax.rem(u, pairs))

        late = 3 * pairs // 4
        catch_up = 2 * pairs + 2 * late

        @pl.loop(0, 2 * chunks)
        def _(t):
            s, c = t // chunks, lax.rem(t, chunks)
            w_mid_recv(s, c).wait_recv()
            w_y(s, c, y).start()

            first = chunks - 2

            @pl.when(jnp.logical_and(t >= first, t < first + chunks))
            def _():
                w_end(0, t - first).wait_recv()
                w_mid_send(1, t - first).start()

            @pl.when(t == first + chunks)
            def _():
                @pl.loop(0, wo_chunks)
                def _(k):
                    o_mid_send(0, k).start()

            @pl.when(jnp.logical_and(t >= 2, t < 2 + n))
            def _():
                h_end(t - 2).wait_recv()
                h_x(t - 2, spot).start()
                h_core(0, t - 2, spot).start()

            @pl.when(jnp.logical_and(t >= 4, t < 4 + n))
            def _():
                h_x(t - 4, x_n).wait_recv()
                h_core(1, t - 4, x_n).start()

            @pl.when(t == chunks)
            def _():
                @pl.loop(0, n)
                def _(k):
                    h_core(0, k, core_n).wait_recv()
                    h_core(1, k, diag_n).wait_recv()

            @pl.when(t >= 2)
            def _():
                w_y((t - 2) // chunks, lax.rem(t - 2, chunks), opp).wait_recv()
                even = lax.rem(t, 2) == 0
                last = jnp.where(even, t - 1, t - 2)

                @pl.when(last >= 1)
                def _():
                    shard = far_shard(last // chunks)
                    part = jnp.where(even, y, opp)
                    p = lax.rem(last, chunks) // 2
                    add(own_row, tok, shard, part, p)

                    @pl.when(t >= chunks)
                    def _():
                        add(far_row, tok, shard, part, p)

            @pl.when(t >= chunks)
            def _():
                @pl.when(lax.rem(t, 2) == 1)
                def _():
                    @pl.loop(0, 2)
                    def _(k):
                        add(pl.multiple_of(k * tok, tok), tok, outer, y, (t - chunks - 1) // 2)

                u0 = 2 * (t - chunks)

                @pl.loop(u0, jnp.minimum(u0 + 2, catch_up))
                def _(u):
                    own_done = u < 2 * pairs
                    v = u - 2 * pairs
                    shard = jnp.where(own_done, inner, far_inner)
                    part = jnp.where(own_done, u // pairs, jnp.where(v < late, y, opp))
                    p = jnp.where(own_done, lax.rem(u, pairs), lax.rem(v + 2 * late, late))
                    add(far_row, tok, shard, part, p)

        @pl.loop(direct, chunks)
        def _(c):
            w_y(2, c, y).start()

        def add_all(shard, part, p):
            add(0, span, shard, part, p)

        add_all(far_outer, y, pairs - 1)

        @pl.loop(0, 2)
        def _(k):
            w_y(1, chunks - 2 + k, opp).wait_recv()

        add_all(far_outer, opp, pairs - 1)

        @pl.loop(0, pairs)
        def _(p):
            for k in range(2):
                c = 2 * p + k

                @pl.when(c < direct)
                def _():
                    w_end(1, c).wait_recv()

                @pl.when(c >= direct)
                def _():
                    w_y(2, c, opp).wait_recv()

            add_all(outer, opp, p)

        for h in range(2):
            for i in range(2):
                kv_buf[h, i, SHIFT:] = acc[h, 1 + i].astype(jnp.bfloat16)
        kv_copy.start()
        for h in range(2):
            q_buf[h] = acc[h, 0].astype(jnp.bfloat16)

        causal = lax.broadcasted_iota(jnp.int32, (SHIFT, 2 * SHIFT), 1) <= (
            lax.broadcasted_iota(jnp.int32, (SHIFT, 2 * SHIFT), 0) + SHIFT
        )

        def attend(b):
            for h in range(heads):
                lanes = slice((h % per_half) * HEAD_DIM, (h % per_half + 1) * HEAD_DIM)
                mine, seen = slice(b * SHIFT, (b + 1) * SHIFT), slice(b * SHIFT, (b + 2) * SHIFT)
                keys, values = kv_buf.at[h // per_half, 0], kv_buf.at[h // per_half, 1]
                scores = lax.dot_general(
                    q_buf[h // per_half, mine, lanes], keys[seen, lanes], (((1,), (1,)), ((), ())),
                    preferred_element_type=jnp.float32,
                ) * (1.0 / math.sqrt(HEAD_DIM))
                allowed = causal & (segq_ref[mine, :] == segk_ref[h, b])
                scores = jnp.where(allowed, scores, masked_out)
                exponent = jnp.exp(scores - jnp.max(scores, axis=-1, keepdims=True))
                weights = exponent / jnp.sum(exponent, axis=-1, keepdims=True)
                att[spot, mine, h * HEAD_DIM : (h + 1) * HEAD_DIM] = jnp.dot(
                    weights.astype(jnp.bfloat16), values[seen, lanes], preferred_element_type=jnp.float32
                ).astype(jnp.bfloat16)
            att_x(b, spot).start()
            att_core(0, b, spot).start()

        def relay(b):
            att_x(b, x_n).wait_recv()
            att_core(1, b, x_n).start()

        def gathered(b):
            att_core(0, b, core_n).wait_recv()
            att_core(1, b, diag_n).wait_recv()

        def multiply(shard, b):
            total = None
            for p in range(narrow):
                a_cols = att.shape[2]
                start = (p % (narrow // 2)) * a_cols
                term = jnp.dot(
                    att[p, b * SHIFT : (b + 1) * SHIFT],
                    wo_buf[shard, p // (narrow // 2), start : start + a_cols],
                    preferred_element_type=jnp.float32,
                )
                total = term if total is None else total + term
            done = total.astype(jnp.bfloat16)
            stage[shard, b * SHIFT : (b + 1) * SHIFT] = done
            pos = b * SHIFT // tok
            for k in range(SHIFT // quarter):
                to_n = b * SHIFT % tok // quarter + k
                here = jnp.logical_and(pos == own_pos, spot == to_n)

                @pl.when(here)
                def _():
                    out_ref[:, res_cols(shard, spot)] = done[k * quarter : (k + 1) * quarter]

                @pl.when(jnp.logical_not(here))
                def _():
                    result(shard, pos, to_n).start()

        @pl.loop(0, wo_chunks)
        def _(c):
            o_mid_recv(0, c).wait_recv()
            o_y(0, c, y).start()

        def forward_wo(c):
            o_end(0, c).wait_recv()
            o_mid_send(1, c).start()

        attend(1)
        for c in range(0, wo_chunks // 2):
            forward_wo(c)
        attend(2)
        relay(1)
        for c in range(wo_chunks // 2, wo_chunks):
            forward_wo(c)
        attend(3)
        relay(2)
        for copy in own[3:]:
            copy.wait()
        gathered(1)
        multiply(inner, 1)
        relay(3)
        gathered(2)
        multiply(inner, 2)
        gathered(3)
        multiply(inner, 3)
        kv_copy.wait_recv()
        attend(0)

        @pl.loop(0, wo_chunks)
        def _(c):
            o_y(0, c, opp).wait_recv()

        for b in range(1, blocks):
            multiply(far_inner, b)
        relay(0)

        @pl.loop(0, wo_chunks)
        def _(c):
            o_mid_recv(1, c).wait_recv()
            o_y(1, c, y).start()

        gathered(0)
        multiply(inner, 0)
        multiply(far_inner, 0)

        @pl.loop(0, wo_chunks)
        def _(c):
            o_end(1, c).wait_recv()

        for b in range(blocks):
            multiply(outer, b)

        @pl.loop(0, wo_chunks)
        def _(c):
            o_y(1, c, opp).wait_recv()

        for b in range(blocks):
            multiply(far_outer, b)

        @pl.loop(0, n)
        def _(shard):
            for p in range(narrow):
                @pl.when(spot != p)
                def _():
                    result_arrival(shard, p).wait_recv()

        @pl.loop(0, n)
        def _(k):
            h_x(k, spot).wait_send()
            h_core(0, k, spot).wait_send()
            h_core(1, k, x_n).wait_send()

        @pl.loop(0, chunks)
        def _(c):
            w_mid_send(0, c).wait_send()
            w_mid_send(1, c).wait_send()
            w_y(0, c, y).wait_send()
            w_y(1, c, y).wait_send()

        @pl.loop(direct, chunks)
        def _(c):
            w_y(2, c, y).wait_send()

        kv_copy.wait_send()

        @pl.loop(0, wo_chunks)
        def _(c):
            o_mid_send(0, c).wait_send()
            o_mid_send(1, c).wait_send()
            o_y(0, c, y).wait_send()
            o_y(1, c, y).wait_send()

        for b in range(blocks):
            att_x(b, spot).wait_send()
            att_core(0, b, spot).wait_send()
            att_core(1, b, x_n).wait_send()

        @pl.loop(0, n)
        def _(shard):
            for pos in range(2):
                for to_n in range(narrow):
                    @pl.when(jnp.logical_not(jnp.logical_and(pos == own_pos, spot == to_n)))
                    def _():
                        result(shard, pos, to_n).wait_send()


def hub_layer(hidden, wq, wo, seg_q, seg_k):
    n, narrow = lax.axis_size("wide"), lax.axis_size("narrow")
    tok, width = hidden.shape
    half = wq.shape[2] // 2
    chunks = wq.shape[1] // ROWS
    wo_chunks = WO_CHUNKS
    direct = DIRECT
    cols = wo.shape[1]
    wo_half, wo_cols = wo.shape[0] // 2, cols // narrow
    quarter, span = tok // narrow, 2 * tok
    blocks = span // SHIFT
    vmem = pl.BlockSpec(memory_space=pltpu.VMEM)
    hbm = pl.BlockSpec(memory_space=pl.ANY)
    dma = pltpu.SemaphoreType.DMA
    bf16 = jnp.bfloat16
    return pl.pallas_call(
        functools.partial(hub_kernel, chunks, wo_chunks, direct),
        out_shape=jax.ShapeDtypeStruct((quarter, n * cols), bf16),
        in_specs=[hbm, hbm, hbm, vmem, vmem],
        out_specs=vmem,
        scratch_shapes=[
            pltpu.VMEM((2, 3, width, half), bf16),
            pltpu.VMEM((span, width), bf16),
            pltpu.VMEM((2, 3, span, half), jnp.float32),
            pltpu.VMEM((2, span, half), bf16),
            pltpu.VMEM((2, 2, span + SHIFT, half), bf16),
            pltpu.VMEM((narrow, span, 2 * half), bf16),
            pltpu.VMEM((n, 2, wo_half, wo_cols), bf16),
            pltpu.VMEM((n, span, wo_cols), bf16),
            dma((5,)),
        ]
        + [dma((n,))] * 4
        + [dma((2, n))] * 2
        + [dma((2, chunks))] * 4
        + [dma((3, chunks))] * 2
        + [dma((2,))]
        + [dma((2, wo_chunks))] * 6
        + [dma((blocks,))] * 2
        + [dma((2, blocks))] * 2
        + [dma((n, 2, narrow)), dma((n, narrow))],
        compiler_params=pltpu.CompilerParams(
            collective_id=0, has_side_effects=True, vmem_limit_bytes=58 * 1024 * 1024
        ),
    )(hidden, wq, wo, seg_q, seg_k)


def hub_per_device(hidden, w_qkv, w_out, seg_ids, shift_heads):
    n = lax.axis_size("wide")
    heads_here = w_qkv.shape[2] // HEAD_DIM
    span = hidden.shape[0] * n // 2
    blocks = span // SHIFT
    first_tok = lax.axis_index("wide") // (n // 2) * span
    shifted = lax.dynamic_slice_in_dim(shift_heads, lax.axis_index("narrow") * heads_here, heads_here) > 0

    doubled = jnp.concatenate([seg_ids[-SHIFT:], seg_ids], 0)
    seg_here = lax.dynamic_slice_in_dim(doubled, first_tok, span + SHIFT)
    seg_q = seg_here[SHIFT:, None]
    windows = jnp.stack([seg_here[b * SHIFT : (b + 2) * SHIFT] for b in range(blocks)])
    odd = (jnp.arange(blocks) % 2 == 1)[None, :, None]
    reaches = (shifted[:, None, None] != odd) | (jnp.arange(2 * SHIFT) >= SHIFT)[None, None, :]
    seg_k = jnp.where(reaches, windows[None], -1)[:, :, None, :]
    return hub_layer(hidden, w_qkv.transpose(1, 0, 2), w_out, seg_q, seg_k)


def solution(mesh):
    placed = (
        P(("groups", "wide"), None),
        P("wide", None, "narrow"),
        P(None, "wide"),
        P("groups"),
        P(),
    )
    shape = mesh.shape
    hub = shape["groups"] == 2 and shape["wide"] == 4 and shape["narrow"] == 4
    return jax.shard_map(
        hub_per_device if hub else per_device,
        mesh=mesh,
        in_specs=placed,
        out_specs=P(("groups", "wide", "narrow"), None),
        check_vma=False,
    )
```

```python
import functools
import math

import jax
import jax.numpy as jnp
from jax import lax
from jax.experimental import pallas as pl
from jax.experimental.pallas import tpu as pltpu
from jax.sharding import PartitionSpec as P

HEAD_DIM = 128
GROUP = 512
SHIFT = 256

masked_out = -1e30
MESH = pl.DeviceIdType.MESH
ROWS = 128
WO_CHUNKS = 4
HUB_ROWS = 256
DIRECT = 1


def layer_kernel(
    n, narrow, chunks, wo_chunks,
    hidden_ref, wq_ref, wo_ref, segq_ref, segk_ref, out_ref,
    wbuf, acc, wo_buf, q_buf, kv_buf, att, part, pair_in, pair_sum, far_in,
    own_sem,
    qs_r, qs_l, qr, qs_y, qr_y,
    os_r, os_l, o_r, os_y, or_y,
    kv_sem, pair_s, pair_r, far_s, far_r,
):
    me = lax.axis_index("wide")
    y = lax.axis_index("groups")
    spot = lax.axis_index("narrow")
    other = 1 - y
    across_n = narrow // 2
    high, low = spot // 2, lax.rem(spot, 2)
    depth = wq_ref.shape[1]
    half = wbuf.shape[3]
    tok = hidden_ref.shape[0]
    rows = depth // chunks
    steps = (n - 1) * chunks
    wo_rows = wo_buf.shape[2] // wo_chunks
    cols = wo_buf.shape[3]
    blocks = tok // SHIFT
    per_half = half // HEAD_DIM
    has_left, has_right = me > 0, me < n - 1
    right, left = {"wide": me + 1}, {"wide": me - 1}
    after, before = {"wide": lax.rem(me + 1, n)}, {"wide": lax.rem(me + n - 1, n)}
    opposite = {"groups": other}
    pair = {"narrow": high * 2 + 1 - low}
    far = [{"narrow": lax.rem(high + d, across_n) * 2 + low} for d in range(1, across_n)]
    far_from = [{"narrow": lax.rem(high + across_n - d, across_n) * 2 + low} for d in range(1, across_n)]

    barrier = pltpu.get_barrier_semaphore()
    greeted = [after, before, opposite, pair] + far
    for device in greeted:
        pl.semaphore_signal(barrier, inc=1, device_id=device, device_id_type=MESH)

    def w_at(shard, part_of, c):
        start = pl.multiple_of(shard * depth + c * rows, rows)
        return wbuf.at[part_of, :, pl.ds(start, rows)]

    def wq_own(c):
        return wq_ref.at[
            :, pl.ds(pl.multiple_of(c * rows, rows), rows), pl.ds(pl.multiple_of(y * half, half), half)
        ]

    def o_at(shard, part_of, c):
        return wo_buf.at[shard, part_of, pl.ds(pl.multiple_of(c * wo_rows, wo_rows), wo_rows)]

    def wo_own(c):
        return wo_ref.at[spot, y, pl.ds(pl.multiple_of(c * wo_rows, wo_rows), wo_rows)]

    def remote(src, dst, send, recv, device):
        return pltpu.make_async_remote_copy(
            src_ref=src, dst_ref=dst, send_sem=send, recv_sem=recv,
            device_id=device, device_id_type=MESH,
        )

    def q_right(shard, c, src=None):
        dst = w_at(shard, y, c)
        return remote(dst if src is None else src, dst, qs_r.at[shard, c], qr.at[shard, c], right)

    def q_left(shard, c, src=None):
        dst = w_at(shard, y, c)
        return remote(dst if src is None else src, dst, qs_l.at[shard, c], qr.at[shard, c], left)

    def q_across(shard, c, part_of):
        ref = w_at(shard, part_of, c)
        return remote(ref, ref, qs_y.at[shard, c], qr_y.at[shard, c], opposite)

    def o_right(shard, c, src=None):
        dst = o_at(shard, y, c)
        return remote(dst if src is None else src, dst, os_r.at[shard, c], o_r.at[shard, c], right)

    def o_left(shard, c, src=None):
        dst = o_at(shard, y, c)
        return remote(dst if src is None else src, dst, os_l.at[shard, c], o_r.at[shard, c], left)

    def o_across(shard, c, part_of):
        ref = o_at(shard, part_of, c)
        return remote(ref, ref, os_y.at[shard, c], or_y.at[shard, c], opposite)

    own = [
        pltpu.make_async_copy(
            wq_ref.at[:, :, pl.ds(h * half, half)],
            wbuf.at[h, :, pl.ds(pl.multiple_of(me * depth, depth), depth)],
            own_sem.at[h],
        )
        for h in range(2)
    ]
    own.append(pltpu.make_async_copy(wo_ref.at[spot], wo_buf.at[me], own_sem.at[2]))
    for copy in own:
        copy.start()
    pl.semaphore_wait(barrier, len(greeted))

    @pl.loop(0, chunks)
    def _(c):
        @pl.when(has_right)
        def _():
            q_right(me, c, wq_own(c)).start()

        @pl.when(has_left)
        def _():
            q_left(me, c, wq_own(c)).start()

    acc[...] = jnp.zeros_like(acc)
    own[0].wait()
    own[1].wait()

    def add(shard, part_of, c):
        start = pl.multiple_of(shard * depth + c * rows, rows)
        piece = hidden_ref[:, pl.ds(start, rows)]
        for i in range(3):
            acc[part_of, i] += jnp.dot(
                piece, wbuf[part_of, i, pl.ds(start, rows)], preferred_element_type=jnp.float32
            )

    @pl.loop(0, 2 * chunks)
    def _(i):
        add(me, i // chunks, lax.rem(i, chunks))

    def add_across(t):
        s, c = t // chunks, lax.rem(t, chunks)
        for there, shard in ((me - 1 - s >= 0, me - 1 - s), (me + 1 + s <= n - 1, me + 1 + s)):
            @pl.when(there)
            def _():
                q_across(shard, c, other).wait_recv()
                add(shard, other, c)

    def send_own_wo():
        @pl.loop(0, wo_chunks)
        def _(c):
            @pl.when(has_right)
            def _():
                o_right(me, c, wo_own(c)).start()

            @pl.when(has_left)
            def _():
                o_left(me, c, wo_own(c)).start()

    @pl.loop(0, steps)
    def _(t):
        s, c = t // chunks, lax.rem(t, chunks)

        @pl.when(t == steps - chunks)
        def _():
            send_own_wo()

        @pl.when(me - 1 - s >= 0)
        def _():
            q_right(me - 1 - s, c).wait_recv()

            @pl.when(has_right)
            def _():
                q_right(me - 1 - s, c).start()

            q_across(me - 1 - s, c, y).start()

        @pl.when(me + 1 + s <= n - 1)
        def _():
            q_left(me + 1 + s, c).wait_recv()

            @pl.when(has_left)
            def _():
                q_left(me + 1 + s, c).start()

            q_across(me + 1 + s, c, y).start()

        for there, shard in ((me - 1 - s >= 0, me - 1 - s), (me + 1 + s <= n - 1, me + 1 + s)):
            @pl.when(there)
            def _():
                add(shard, y, c)

        @pl.when(t > 0)
        def _():
            add_across(t - 1)

    add_across(steps - 1)
    for h in range(2):
        q_buf[h] = acc[h, 0].astype(jnp.bfloat16)
        for i in range(2):
            kv_buf[h, i, SHIFT:] = acc[h, 1 + i].astype(jnp.bfloat16)

    kv_copy = remote(
        kv_buf.at[:, :, pl.ds(tok, SHIFT)], kv_buf.at[:, :, pl.ds(0, SHIFT)],
        kv_sem.at[0], kv_sem.at[1], after,
    )
    kv_copy.start()

    causal = lax.broadcasted_iota(jnp.int32, (SHIFT, 2 * SHIFT), 1) <= (
        lax.broadcasted_iota(jnp.int32, (SHIFT, 2 * SHIFT), 0) + SHIFT
    )

    def attend(h, b):
        lanes = slice((h % per_half) * HEAD_DIM, (h % per_half + 1) * HEAD_DIM)
        mine, seen = slice(b * SHIFT, (b + 1) * SHIFT), slice(b * SHIFT, (b + 2) * SHIFT)
        keys, values = kv_buf.at[h // per_half, 0], kv_buf.at[h // per_half, 1]
        scores = lax.dot_general(
            q_buf[h // per_half, mine, lanes], keys[seen, lanes], (((1,), (1,)), ((), ())),
            preferred_element_type=jnp.float32,
        ) * (1.0 / math.sqrt(HEAD_DIM))
        allowed = causal & (segq_ref[mine, :] == segk_ref[h, b])
        scores = jnp.where(allowed, scores, masked_out)
        exponent = jnp.exp(scores - jnp.max(scores, axis=-1, keepdims=True))
        weights = exponent / jnp.sum(exponent, axis=-1, keepdims=True)
        att[mine, h * HEAD_DIM : (h + 1) * HEAD_DIM] = jnp.dot(
            weights.astype(jnp.bfloat16), values[seen, lanes], preferred_element_type=jnp.float32
        ).astype(jnp.bfloat16)

    least = jnp.minimum(me, n - 1 - me)

    def block_of(k):
        turn = (k + 1) // 2
        near = jnp.where(lax.rem(k, 2) == 1, me - turn, me + turn)
        rest = jnp.where(me > least, me - (k - least), me + (k - least))
        return jnp.where(k <= 2 * least, near, rest)

    def pass_on(k):
        shard = block_of(k)

        @pl.loop(0, wo_chunks)
        def _(c):
            o_right(shard, c).wait_recv()

            @pl.when(jnp.logical_and(shard < me, has_right))
            def _():
                o_right(shard, c).start()

            @pl.when(jnp.logical_and(shard > me, has_left))
            def _():
                o_left(shard, c).start()

            o_across(shard, c, y).start()

    def pair_copy(shard, a):
        return remote(
            part.at[shard, a * 2 + 1 - low], pair_in.at[shard, a],
            pair_s.at[shard, a], pair_r.at[shard, a], pair,
        )

    def far_copy(shard, d):
        a = lax.rem(high + d, across_n)
        return remote(
            pair_sum.at[shard, a], far_in.at[shard, d - 1],
            far_s.at[shard, d - 1], far_r.at[shard, d - 1], far[d - 1],
        )

    def far_arrival(shard, d):
        return remote(
            pair_sum.at[shard, high], far_in.at[shard, d - 1],
            far_s.at[shard, d - 1], far_r.at[shard, d - 1], far_from[d - 1],
        )

    def multiply(k):
        shard = block_of(k)
        width = att.shape[1] // 2
        share = tok // narrow
        for p in range(narrow):
            a_rows = att[p * share : (p + 1) * share, :]
            total = jnp.dot(a_rows[:, :width], wo_buf[shard, 0], preferred_element_type=jnp.float32)
            total += jnp.dot(a_rows[:, width:], wo_buf[shard, 1], preferred_element_type=jnp.float32)
            part[shard, p] = total.astype(jnp.bfloat16)
        for a in range(across_n):
            pair_copy(shard, a).start()

    def sum_pair(k):
        shard = block_of(k)
        for a in range(across_n):
            pair_copy(shard, a).wait_recv()
            total = part[shard, a * 2 + low].astype(jnp.float32) + pair_in[shard, a].astype(jnp.float32)
            pair_sum[shard, a] = total.astype(jnp.bfloat16)
        for d in range(1, across_n):
            far_copy(shard, d).start()

    def finish(k):
        shard = block_of(k)
        total = part[shard, high * 2 + low].astype(jnp.float32) + pair_in[shard, high].astype(jnp.float32)
        for d in range(1, across_n):
            far_arrival(shard, d).wait_recv()
            total += far_in[shard, d - 1].astype(jnp.float32)
        out_ref[:, pl.ds(pl.multiple_of(shard * cols, cols), cols)] = total.astype(out_ref.dtype)

    heads = 2 * per_half
    for b in range(1, blocks):
        for h in range(heads):
            attend(h, b)
    pass_on(1)
    pass_on(2)
    kv_copy.wait_recv()
    for h in range(heads):
        attend(h, 0)
    own[2].wait()
    multiply(0)

    @pl.loop(1, n)
    def _(k):
        @pl.when(k > 2)
        def _():
            pass_on(k)

        sum_pair(k - 1)

        @pl.when(k > 1)
        def _():
            finish(k - 2)

        shard = block_of(k)

        @pl.loop(0, wo_chunks)
        def _(c):
            o_across(shard, c, other).wait_recv()

        multiply(k)

    sum_pair(n - 1)
    finish(n - 2)
    finish(n - 1)

    kv_copy.wait_send()

    @pl.loop(0, n)
    def _(shard):
        for a in range(across_n):
            pair_copy(shard, a).wait_send()
        for d in range(1, across_n):
            far_copy(shard, d).wait_send()
        goes_right = jnp.logical_and(shard <= me, has_right)
        goes_left = jnp.logical_and(shard >= me, has_left)
        for count, to_right, to_left, to_other in (
            (chunks, q_right, q_left, q_across), (wo_chunks, o_right, o_left, o_across)
        ):
            @pl.loop(0, count)
            def _(c):
                @pl.when(goes_right)
                def _():
                    to_right(shard, c).wait_send()

                @pl.when(goes_left)
                def _():
                    to_left(shard, c).wait_send()

                @pl.when(shard != me)
                def _():
                    to_other(shard, c, y).wait_send()


def layer(hidden, wq, wo, seg_q, seg_k):
    n, narrow = lax.axis_size("wide"), lax.axis_size("narrow")
    tok, width = hidden.shape
    half = wq.shape[2] // 2
    chunks = max(1, wq.shape[1] // ROWS)
    wo_chunks = WO_CHUNKS
    cols = wo.shape[3]
    share = tok // narrow
    vmem = pl.BlockSpec(memory_space=pltpu.VMEM)
    hbm = pl.BlockSpec(memory_space=pl.ANY)
    dma = pltpu.SemaphoreType.DMA
    bf16 = jnp.bfloat16
    return pl.pallas_call(
        functools.partial(layer_kernel, n, narrow, chunks, wo_chunks),
        out_shape=jax.ShapeDtypeStruct((share, n * cols), bf16),
        in_specs=[vmem, hbm, hbm, vmem, vmem],
        out_specs=vmem,
        scratch_shapes=[
            pltpu.VMEM((2, 3, width, half), bf16),
            pltpu.VMEM((2, 3, tok, half), jnp.float32),
            pltpu.VMEM((n,) + wo.shape[1:], bf16),
            pltpu.VMEM((2, tok, half), bf16),
            pltpu.VMEM((2, 2, tok + SHIFT, half), bf16),
            pltpu.VMEM((tok, 2 * half), bf16),
            pltpu.VMEM((n, narrow, share, cols), bf16),
            pltpu.VMEM((n, narrow // 2, share, cols), bf16),
            pltpu.VMEM((n, narrow // 2, share, cols), bf16),
            pltpu.VMEM((n, max(1, narrow // 2 - 1), share, cols), bf16),
            dma((3,)),
        ]
        + [dma((n, chunks))] * 5
        + [dma((n, wo_chunks))] * 5
        + [dma((2,))]
        + [dma((n, narrow // 2))] * 2
        + [dma((n, max(1, narrow // 2 - 1)))] * 2,
        compiler_params=pltpu.CompilerParams(
            collective_id=0, has_side_effects=True, vmem_limit_bytes=58 * 1024 * 1024
        ),
    )(hidden, wq, wo, seg_q, seg_k)


def per_device(hidden, w_qkv, w_out, seg_ids, shift_heads):
    tok_rows = hidden.shape[0]
    local_f = w_qkv.shape[2]
    heads_here = local_f // HEAD_DIM
    blocks = tok_rows // SHIFT
    narrow = lax.axis_size("narrow")
    first_tok = lax.axis_index("wide") * tok_rows
    shifted = lax.dynamic_slice_in_dim(shift_heads, lax.axis_index("narrow") * heads_here, heads_here) > 0

    doubled = jnp.concatenate([seg_ids[-SHIFT:], seg_ids], 0)
    seg_here = lax.dynamic_slice_in_dim(doubled, first_tok, tok_rows + SHIFT)
    seg_q = seg_here[SHIFT:, None]
    windows = jnp.stack([seg_here[b * SHIFT : (b + 2) * SHIFT] for b in range(blocks)])
    odd = (jnp.arange(blocks) % 2 == 1)[None, :, None]
    reaches = (shifted[:, None, None] != odd) | (jnp.arange(2 * SHIFT) >= SHIFT)[None, None, :]
    seg_k = jnp.where(reaches, windows[None], -1)[:, :, None, :]

    wq = w_qkv.transpose(1, 0, 2)
    wo = w_out.reshape(narrow, 2, local_f // 2, -1)
    return layer(hidden, wq, wo, seg_q, seg_k)


def hub_kernel(
    row_chunks, direct,
    hidden_ref, wq_ref, wo_ref, seg_ref, shift_ref, out_ref,
    wbuf, hid, acc, q_buf, kv_buf, att, wo_buf, stage, seg_col,
    own_sem, he_s, he_r, hx_s, hx_r, hc_s, hc_r,
    wm_s, wm_r, we_s, we_r, wy_s, wy_r, kv_sem,
    om_s, om_r, oe_s, oe_r, oy_s, oy_r,
    ax_s, ax_r, ac_s, ac_r, res_s, res_r,
):
    n, narrow = lax.axis_size("wide"), lax.axis_size("narrow")
    me = lax.axis_index("wide")
    y = lax.axis_index("groups")
    spot = lax.axis_index("narrow")
    opp = 1 - y
    side = me // (n // 2)
    inner, outer = n // 2 - 1 + side, side * (n - 1)
    far_inner, far_outer = n - 1 - inner, n - 1 - outer
    is_inner, is_outer = me == inner, me == outer
    high, low = spot // 2, lax.rem(spot, 2)
    core_n, x_n = high * 2 + 1 - low, (1 - high) * 2 + low
    diag_n = (1 - high) * 2 + 1 - low
    depth = wq_ref.shape[1]
    tok = hidden_ref.shape[0]
    heads = wbuf.shape[0]
    chunks = 2 * row_chunks
    rows = depth // row_chunks
    wo_chunks = 4
    quarter = tok // narrow
    span = 2 * tok
    blocks = span // SHIFT
    own_pos = 1 - side
    own_row = pl.multiple_of(own_pos * tok, tok)
    far_row = pl.multiple_of(side * tok, tok)
    wo_half, wo_cols = wo_buf.shape[2], wo_buf.shape[3]
    wo_rows, wo_lanes = wo_half // 2, wo_cols // 2
    cols = wo_ref.shape[1]
    to_core, to_x, to_y = {"narrow": core_n}, {"narrow": x_n}, {"groups": opp}
    to_far, to_inner = {"wide": far_inner}, {"wide": inner}

    def remote(src, dst, send, recv, device):
        return pltpu.make_async_remote_copy(
            src_ref=src, dst_ref=dst, send_sem=send, recv_sem=recv,
            device_id=device, device_id_type=MESH,
        )

    def w_at(shard, part, c):
        start = pl.multiple_of(shard * depth + lax.rem(c, row_chunks) * rows, rows)
        return wbuf.at[c // row_chunks * 2 + part, :, pl.ds(start, rows)]

    def wq_at(part, c):
        start = pl.multiple_of(lax.rem(c, row_chunks) * rows, rows)
        lane = pl.multiple_of((c // row_chunks * 2 + part) * HEAD_DIM, HEAD_DIM)
        return wq_ref.at[:, pl.ds(start, rows), pl.ds(lane, HEAD_DIM)]

    def o_at(shard, part, c):
        start = pl.multiple_of(lax.rem(c, 2) * wo_rows, wo_rows)
        return wo_buf.at[shard, part, pl.ds(start, wo_rows), pl.ds(pl.multiple_of(c // 2 * wo_lanes, wo_lanes), wo_lanes)]

    def wo_at(part, c):
        start = pl.multiple_of(part * wo_half + lax.rem(c, 2) * wo_rows, wo_rows)
        lane = pl.multiple_of(spot * wo_cols + c // 2 * wo_lanes, wo_lanes)
        return wo_ref.at[pl.ds(start, wo_rows), pl.ds(lane, wo_lanes)]

    def h_at(row_n, k):
        start = pl.multiple_of(far_row + row_n * quarter, quarter)
        return hid.at[pl.ds(start, quarter), pl.ds(pl.multiple_of(k * depth, depth), depth)]

    def h_end(k):
        src = hidden_ref.at[
            pl.ds(pl.multiple_of(spot * quarter, quarter), quarter), pl.ds(pl.multiple_of(k * depth, depth), depth)
        ]
        return remote(src, h_at(spot, k), he_s.at[k], he_r.at[k], to_inner)

    def h_x(k, row_n):
        return remote(h_at(row_n, k), h_at(row_n, k), hx_s.at[k], hx_r.at[k], to_x)

    def h_core(j, k, row_n):
        return remote(h_at(row_n, k), h_at(row_n, k), hc_s.at[j, k], hc_r.at[j, k], to_core)

    def w_end(j, c):
        part = y if j == 0 else opp
        return remote(wq_at(part, c), w_at(outer, part, c), we_s.at[j, c], we_r.at[j, c], to_inner)

    def w_mid_send(s, c):
        if s == 0:
            return remote(wq_at(y, c), w_at(inner, y, c), wm_s.at[s, c], wm_r.at[s, c], to_far)
        return remote(w_at(outer, y, c), w_at(outer, y, c), wm_s.at[s, c], wm_r.at[s, c], to_far)

    def far_shard(s):
        return jnp.where(s == 0, far_inner, far_outer)

    def w_mid_recv(s, c):
        ref = w_at(far_shard(s), y, c)
        return remote(ref, ref, wm_s.at[s, c], wm_r.at[s, c], to_far)

    def y_shard(s):
        return jnp.where(s == 2, outer, far_shard(s))

    def w_y(s, c, part):
        ref = w_at(y_shard(s), part, c)
        return remote(ref, ref, wy_s.at[s, c], wy_r.at[s, c], to_y)

    def o_end(j, c):
        part = y if j == 0 else opp
        return remote(wo_at(part, c), o_at(outer, part, c), oe_s.at[j, c], oe_r.at[j, c], to_inner)

    def o_mid_send(s, c):
        if s == 0:
            return remote(wo_at(y, c), o_at(inner, y, c), om_s.at[s, c], om_r.at[s, c], to_far)
        return remote(o_at(outer, y, c), o_at(outer, y, c), om_s.at[s, c], om_r.at[s, c], to_far)

    def o_mid_recv(s, c):
        ref = o_at(far_shard(s), y, c)
        return remote(ref, ref, om_s.at[s, c], om_r.at[s, c], to_far)

    def o_y(s, c, part):
        ref = o_at(far_shard(s), part, c)
        return remote(ref, ref, oy_s.at[s, c], oy_r.at[s, c], to_y)

    def att_at(row_n, g, b):
        return att.at[row_n, g, pl.ds(pl.multiple_of(b * SHIFT, SHIFT), SHIFT)]

    def att_x(g, b, row_n):
        ref = att_at(row_n, g, b)
        return remote(ref, ref, ax_s.at[g, b], ax_r.at[g, b], to_x)

    def att_core(j, g, b, row_n):
        ref = att_at(row_n, g, b)
        return remote(ref, ref, ac_s.at[j, g, b], ac_r.at[j, g, b], to_core)

    shards = (inner, far_inner, outer, far_outer)
    slots = ((0, 0, wo_cols), (1, 0, wo_cols), (2, 0, wo_cols), (3, 0, wo_lanes), (3, wo_lanes, wo_lanes))

    def res_cols(slot, row_n):
        order, lane, size = slots[slot]
        return pl.ds(pl.multiple_of(shards[order] * cols + row_n * wo_cols + lane, size), size)

    def result(slot, pos, to_n):
        order, lane, size = slots[slot]
        return remote(
            stage.at[order, pl.ds(pl.multiple_of(pos * tok + to_n * quarter, quarter), quarter), lane : lane + size],
            out_ref.at[:, res_cols(slot, spot)],
            res_s.at[slot, pos, to_n], res_r.at[slot, spot],
            {"wide": side * (n // 2) + pos, "narrow": to_n},
        )

    def result_arrival(slot, from_n):
        ref = out_ref.at[:, res_cols(slot, from_n)]
        return remote(ref, ref, res_s.at[slot, 0, 0], res_r.at[slot, from_n], to_core)

    def kv_copy(g):
        return remote(
            kv_buf.at[pl.ds(2 * g, 2), :, pl.ds(span, SHIFT)], kv_buf.at[pl.ds(2 * g, 2), :, pl.ds(0, SHIFT)],
            kv_sem.at[0, g], kv_sem.at[1, g], to_far,
        )

    barrier = pltpu.get_barrier_semaphore()

    @pl.when(is_outer)
    def _():
        for p in range(narrow):
            pl.semaphore_signal(barrier, inc=1, device_id={"wide": inner, "narrow": p}, device_id_type=MESH)
        pl.semaphore_wait(barrier, narrow)

        @pl.loop(0, n)
        def _(k):
            h_end(k).start()

        def each_end(act):
            @pl.loop(0, row_chunks)
            def _(c):
                act(w_end(0, c))

            @pl.loop(0, direct)
            def _(c):
                act(w_end(1, c))

            @pl.loop(row_chunks, chunks)
            def _(c):
                act(w_end(0, c))

            @pl.loop(row_chunks, chunks)
            def _(c):
                act(w_end(1, c))

            for j in range(2):
                @pl.loop(0, wo_chunks)
                def _(c):
                    act(o_end(j, c))

        each_end(lambda copy: copy.start())

        @pl.loop(0, n)
        def _(k):
            h_end(k).wait_send()

        each_end(lambda copy: copy.wait_send())
        for slot in range(len(slots)):
            for p in range(narrow):
                result_arrival(slot, p).wait_recv()

    @pl.when(is_inner)
    def _():
        own = [
            pltpu.make_async_copy(
                wq_ref.at[:, :, pl.ds(h * HEAD_DIM, HEAD_DIM)],
                wbuf.at[h, :, pl.ds(pl.multiple_of(inner * depth, depth), depth)],
                own_sem.at[h],
            )
            for h in range(heads)
        ]
        own.append(pltpu.make_async_copy(hidden_ref, hid.at[pl.ds(own_row, tok)], own_sem.at[heads]))
        own += [
            pltpu.make_async_copy(
                wo_ref.at[pl.ds(h * wo_half, wo_half), pl.ds(pl.multiple_of(spot * wo_cols, wo_cols), wo_cols)],
                wo_buf.at[inner, h],
                own_sem.at[heads + 1 + h],
            )
            for h in range(2)
        ]
        for copy in own:
            copy.start()
        peers = [{"narrow": core_n}, {"narrow": x_n}, {"narrow": diag_n}, to_y, to_far]
        peers += [{"wide": outer, "narrow": p} for p in range(narrow)]
        for device in peers:
            pl.semaphore_signal(barrier, inc=1, device_id=device, device_id_type=MESH)
        pl.semaphore_wait(barrier, len(peers))

        @pl.loop(0, chunks)
        def _(c):
            w_mid_send(0, c).start()

        acc[...] = jnp.zeros_like(acc)
        seg_rows = seg_ref.shape[0]
        lanes = seg_ref.shape[1]
        seg_first = side * (span // lanes)
        for k in range(span // lanes):
            line = seg_ref[pl.ds(seg_first + k, 1), :]
            seg_col[k * lanes : (k + 1) * lanes, :] = jnp.broadcast_to(line, (lanes, lanes)).T

        def add(row, size, shard, part, c):
            start = pl.multiple_of(shard * depth + lax.rem(c, row_chunks) * rows, rows)
            head = c // row_chunks * 2 + part
            here = pl.ds(row, size)
            piece = hid[here, pl.ds(start, rows)]
            both = jnp.concatenate([wbuf[head, i, pl.ds(start, rows)] for i in range(2)], axis=1)
            found = jnp.dot(piece, both, preferred_element_type=jnp.float32)
            acc[head, 0, here] += found[:, :HEAD_DIM]
            acc[head, 1, here] += found[:, HEAD_DIM:]
            acc[head, 2, here] += jnp.dot(piece, wbuf[head, 2, pl.ds(start, rows)], preferred_element_type=jnp.float32)

        def add_all(shard, part, c):
            add(0, span, shard, part, c)

        def add_at(t, shard, part, c):
            @pl.when(t < chunks)
            def _():
                add(own_row, tok, shard, part, c)

            @pl.when(t >= chunks)
            def _():
                add_all(shard, part, c)

        for copy in own[: heads + 1]:
            copy.wait()

        @pl.loop(0, 2 * chunks)
        def _(u):
            add(own_row, tok, inner, u // chunks, lax.rem(u, chunks))

        lag = row_chunks
        lead = chunks - 2
        catch_up = 4 * chunks - lag

        @pl.loop(0, 2 * chunks)
        def _(t):
            s, c = t // chunks, lax.rem(t, chunks)
            w_mid_recv(s, c).wait_recv()
            w_y(s, c, y).start()

            early = jnp.logical_and(t >= lead, t < lead + row_chunks)
            later = jnp.logical_and(t >= lead + row_chunks + direct, t < lead + chunks + direct)
            q = jnp.where(t < lead + row_chunks, t - lead, t - lead - direct)

            @pl.when(jnp.logical_or(early, later))
            def _():
                w_end(0, q).wait_recv()
                w_mid_send(1, q).start()

            @pl.when(jnp.logical_and(early, q >= direct))
            def _():
                w_y(2, q, y).start()

            @pl.when(jnp.logical_and(t >= 1, t < 1 + n))
            def _():
                h_end(t - 1).wait_recv()
                h_x(t - 1, spot).start()
                h_core(0, t - 1, spot).start()

            @pl.when(jnp.logical_and(t >= 4, t < 4 + n))
            def _():
                h_x(t - 4, x_n).wait_recv()
                h_core(1, t - 4, x_n).start()

            @pl.when(t == chunks)
            def _():
                @pl.loop(0, n)
                def _(k):
                    h_core(0, k, core_n).wait_recv()
                    h_core(1, k, diag_n).wait_recv()

            add_at(t, far_shard(s), y, c)

            @pl.when(t >= lag)
            def _():
                v = t - lag
                w_y(v // chunks, lax.rem(v, chunks), opp).wait_recv()
                add_at(t, far_shard(v // chunks), opp, lax.rem(v, chunks))

            @pl.when(t >= chunks)
            def _():
                add_all(outer, y, t - chunks)
                u0 = 4 * (t - chunks)

                @pl.loop(u0, jnp.minimum(u0 + 4, catch_up))
                def _(u):
                    first = u < 2 * chunks
                    part = jnp.where(first, u // chunks, jnp.where(u < 3 * chunks, y, opp))
                    add(far_row, tok, jnp.where(first, inner, far_inner), part, lax.rem(u, chunks))

            @pl.when(t >= chunks + row_chunks)
            def _():
                k = t - chunks - row_chunks

                @pl.when(k < direct)
                def _():
                    w_end(1, k).wait_recv()

                @pl.when(k >= direct)
                def _():
                    w_y(2, k, opp).wait_recv()

                add_all(outer, opp, k)

        causal = lax.broadcasted_iota(jnp.int32, (SHIFT, 2 * SHIFT), 1) <= (
            lax.broadcasted_iota(jnp.int32, (SHIFT, 2 * SHIFT), 0) + SHIFT
        )
        per_block = SHIFT // lanes

        def seg_line(b):
            at = [lax.rem(seg_first + b * per_block + k + seg_rows, seg_rows) for k in range(per_block)]
            return jnp.concatenate([seg_ref[pl.ds(i, 1), :] for i in at], axis=1)

        def attend(g, b):
            mine, seen = slice(b * SHIFT, (b + 1) * SHIFT), slice(b * SHIFT, (b + 2) * SHIFT)
            seg_q = jnp.concatenate([seg_col[mine, :]] * (2 * per_block), axis=1)
            near, prior = seg_line(b), seg_line(b - 1)
            for k in range(2):
                h = 2 * g + k
                reach = shift_ref[spot * heads + h]
                if b % 2 == 1:
                    reach = 1 - reach
                seg_k = jnp.concatenate([prior * reach + (reach - 1), near], axis=1)
                scores = lax.dot_general(
                    q_buf[h, mine], kv_buf[h, 0, seen], (((1,), (1,)), ((), ())),
                    preferred_element_type=jnp.float32,
                ) * (1.0 / math.sqrt(HEAD_DIM))
                allowed = causal & (seg_q == seg_k)
                scores = jnp.where(allowed, scores, masked_out)
                exponent = jnp.exp(scores - jnp.max(scores, axis=-1, keepdims=True))
                weights = exponent / jnp.sum(exponent, axis=-1, keepdims=True)
                att[spot, g, mine, k * HEAD_DIM : (k + 1) * HEAD_DIM] = jnp.dot(
                    weights.astype(jnp.bfloat16), kv_buf[h, 1, seen], preferred_element_type=jnp.float32
                ).astype(jnp.bfloat16)
            att_x(g, b, spot).start()
            att_core(0, g, b, spot).start()

        def relay(g, b):
            att_x(g, b, x_n).wait_recv()
            att_core(1, g, b, x_n).start()

        def gathered(b):
            for g in range(2):
                att_core(0, g, b, core_n).wait_recv()
                att_core(1, g, b, diag_n).wait_recv()

        def settle(g):
            for h in (2 * g, 2 * g + 1):
                for i in range(2):
                    kv_buf[h, i, SHIFT:] = acc[h, 1 + i].astype(jnp.bfloat16)
            kv_copy(g).start()
            for h in (2 * g, 2 * g + 1):
                q_buf[h] = acc[h, 0].astype(jnp.bfloat16)

        def multiply(slot, b):
            order, lane, size = slots[slot]
            mine = pl.ds(pl.multiple_of(b * SHIFT, SHIFT), SHIFT)
            a_cols = att.shape[3]
            total = None
            for p in range(narrow):
                for g in range(2):
                    start = (p % (narrow // 2) * 2 + g) * a_cols
                    term = jnp.dot(
                        att[p, g, mine],
                        wo_buf[shards[order], p // (narrow // 2), start : start + a_cols, lane : lane + size],
                        preferred_element_type=jnp.float32,
                    )
                    total = term if total is None else total + term
            done = total.astype(jnp.bfloat16)
            stage[order, mine, lane : lane + size] = done
            pos = b // (blocks // 2)
            for k in range(SHIFT // quarter):
                to_n = lax.rem(b, blocks // 2) * (SHIFT // quarter) + k
                here = jnp.logical_and(pos == own_pos, spot == to_n)

                @pl.when(here)
                def _():
                    out_ref[:, res_cols(slot, spot)] = done[k * quarter : (k + 1) * quarter]

                @pl.when(jnp.logical_not(here))
                def _():
                    result(slot, pos, to_n).start()

        def multiply_these(slot, first, count):
            @pl.loop(0, count)
            def _(k):
                multiply(slot, lax.rem(first + k, blocks))

        def near_wo(c):
            o_mid_recv(0, c).wait_recv()
            o_y(0, c, y).start()

        def far_wo(c):
            o_mid_recv(1, c).wait_recv()
            o_y(1, c, y).start()

        def pass_wo(c):
            o_end(0, c).wait_recv()
            o_mid_send(1, c).start()

        def last_y(c):
            w_y(1, c, opp).wait_recv()
            add_all(far_outer, opp, c)

        def last_end(c):
            w_end(1, c).wait_recv()
            add_all(outer, opp, c)

        settle(0)

        @pl.loop(0, wo_chunks)
        def _(c):
            o_mid_send(0, c).start()

        attend(0, 1)
        last_y(row_chunks)
        attend(0, 2)
        last_y(row_chunks + 1)
        attend(0, 3)

        @pl.loop(row_chunks, chunks - 2)
        def _(c):
            last_end(c)

        relay(0, 1)
        relay(0, 2)
        last_y(row_chunks + 2)
        kv_copy(0).wait_recv()
        attend(0, 0)
        relay(0, 3)

        @pl.loop(chunks - 2, chunks)
        def _(c):
            last_end(c)

        near_wo(0)
        near_wo(1)
        last_y(row_chunks + 3)
        relay(0, 0)
        settle(1)
        near_wo(2)
        attend(1, 1)
        near_wo(3)
        pass_wo(0)
        attend(1, 2)
        pass_wo(1)
        attend(1, 3)
        pass_wo(2)
        pass_wo(3)
        for copy in own[heads + 1 :]:
            copy.wait()
        relay(1, 1)
        gathered(1)
        multiply(0, 1)
        relay(1, 2)
        gathered(2)
        multiply(0, 2)
        kv_copy(1).wait_recv()
        attend(1, 0)
        far_wo(0)
        relay(1, 3)
        gathered(3)
        multiply(0, 3)
        far_wo(1)

        @pl.loop(0, wo_chunks)
        def _(c):
            o_y(0, c, opp).wait_recv()

        multiply_these(1, 1, 3)
        far_wo(2)
        relay(1, 0)

        @pl.loop(0, wo_chunks)
        def _(c):
            o_end(1, c).wait_recv()

        multiply_these(2, 1, 3)
        far_wo(3)
        gathered(0)
        for slot in range(3):
            multiply(slot, 0)
        for k in range(2):
            for c in range(2 * k, 2 * k + 2):
                o_y(1, c, opp).wait_recv()
            multiply_these(3 + k, side * (blocks // 2), blocks)

        for slot in range(len(slots)):
            for p in range(narrow):
                @pl.when(spot != p)
                def _():
                    result_arrival(slot, p).wait_recv()

        @pl.loop(0, n)
        def _(k):
            h_x(k, spot).wait_send()
            h_core(0, k, spot).wait_send()
            h_core(1, k, x_n).wait_send()

        @pl.loop(0, chunks)
        def _(c):
            for s in range(2):
                w_mid_send(s, c).wait_send()
                w_y(s, c, y).wait_send()

        @pl.loop(direct, row_chunks)
        def _(c):
            w_y(2, c, y).wait_send()

        @pl.loop(0, wo_chunks)
        def _(c):
            for s in range(2):
                o_mid_send(s, c).wait_send()
                o_y(s, c, y).wait_send()

        for g in range(2):
            kv_copy(g).wait_send()

            @pl.loop(0, blocks)
            def _(b):
                att_x(g, b, spot).wait_send()
                att_core(0, g, b, spot).wait_send()
                att_core(1, g, b, x_n).wait_send()

        for slot in range(len(slots)):
            for pos in range(2):
                for to_n in range(narrow):
                    @pl.when(jnp.logical_not(jnp.logical_and(pos == own_pos, spot == to_n)))
                    def _():
                        result(slot, pos, to_n).wait_send()


def hub_layer(hidden, wq, wo, seg, shift_heads):
    n, narrow = lax.axis_size("wide"), lax.axis_size("narrow")
    tok, width = hidden.shape
    heads = wq.shape[2] // HEAD_DIM
    row_chunks = wq.shape[1] // HUB_ROWS
    chunks, wo_chunks = 2 * row_chunks, 4
    cols = wo.shape[1]
    wo_half, wo_cols = wo.shape[0] // 2, cols // narrow
    quarter, span = tok // narrow, 2 * tok
    blocks = span // SHIFT
    vmem = pl.BlockSpec(memory_space=pltpu.VMEM)
    smem = pl.BlockSpec(memory_space=pltpu.SMEM)
    hbm = pl.BlockSpec(memory_space=pl.ANY)
    dma = pltpu.SemaphoreType.DMA
    bf16 = jnp.bfloat16
    return pl.pallas_call(
        functools.partial(hub_kernel, row_chunks, DIRECT),
        out_shape=jax.ShapeDtypeStruct((quarter, n * cols), bf16),
        in_specs=[hbm, hbm, hbm, vmem, smem],
        out_specs=vmem,
        scratch_shapes=[
            pltpu.VMEM((heads, 3, width, HEAD_DIM), bf16),
            pltpu.VMEM((span, width), bf16),
            pltpu.VMEM((heads, 3, span, HEAD_DIM), jnp.float32),
            pltpu.VMEM((heads, span, HEAD_DIM), bf16),
            pltpu.VMEM((heads, 2, span + SHIFT, HEAD_DIM), bf16),
            pltpu.VMEM((narrow, 2, span, 2 * HEAD_DIM), bf16),
            pltpu.VMEM((n, 2, wo_half, wo_cols), bf16),
            pltpu.VMEM((n, span, wo_cols), bf16),
            pltpu.VMEM((span, seg.shape[1]), jnp.int32),
            dma((heads + 3,)),
        ]
        + [dma((n,))] * 4
        + [dma((2, n))] * 2
        + [dma((2, chunks))] * 4
        + [dma((3, chunks))] * 2
        + [dma((2, 2))]
        + [dma((2, wo_chunks))] * 6
        + [dma((2, blocks))] * 2
        + [dma((2, 2, blocks))] * 2
        + [dma((5, 2, narrow)), dma((5, narrow))],
        compiler_params=pltpu.CompilerParams(
            collective_id=0, has_side_effects=True, vmem_limit_bytes=58 * 1024 * 1024
        ),
    )(hidden, wq, wo, seg, shift_heads)


def hub_per_device(hidden, w_qkv, w_out, seg_ids, shift_heads):
    return hub_layer(hidden, w_qkv.transpose(1, 0, 2), w_out, seg_ids.reshape(-1, 128), shift_heads)


def solution(mesh):
    placed = (
        P(("groups", "wide"), None),
        P("wide", None, "narrow"),
        P(None, "wide"),
        P("groups"),
        P(),
    )
    shape = mesh.shape
    hub = shape["groups"] == 2 and shape["wide"] == 4 and shape["narrow"] == 4
    return jax.shard_map(
        hub_per_device if hub else per_device,
        mesh=mesh,
        in_specs=placed,
        out_specs=P(("groups", "wide", "narrow"), None),
        check_vma=False,
    )
```

```python
import functools
import math

import jax
import jax.numpy as jnp
from jax import lax
from jax.experimental import pallas as pl
from jax.experimental.pallas import tpu as pltpu
from jax.sharding import PartitionSpec as P

HEAD_DIM = 128
GROUP = 512
SHIFT = 256

masked_out = -1e30
MESH = pl.DeviceIdType.MESH
ROWS = 128
WO_CHUNKS = 4
HUB_ROWS = 256
DIRECT = 2


def layer_kernel(
    n, narrow, chunks, wo_chunks,
    hidden_ref, wq_ref, wo_ref, segq_ref, segk_ref, out_ref,
    wbuf, acc, wo_buf, q_buf, kv_buf, att, part, pair_in, pair_sum, far_in,
    own_sem,
    qs_r, qs_l, qr, qs_y, qr_y,
    os_r, os_l, o_r, os_y, or_y,
    kv_sem, pair_s, pair_r, far_s, far_r,
):
    me = lax.axis_index("wide")
    y = lax.axis_index("groups")
    spot = lax.axis_index("narrow")
    other = 1 - y
    across_n = narrow // 2
    high, low = spot // 2, lax.rem(spot, 2)
    depth = wq_ref.shape[1]
    half = wbuf.shape[3]
    tok = hidden_ref.shape[0]
    rows = depth // chunks
    steps = (n - 1) * chunks
    wo_rows = wo_buf.shape[2] // wo_chunks
    cols = wo_buf.shape[3]
    blocks = tok // SHIFT
    per_half = half // HEAD_DIM
    has_left, has_right = me > 0, me < n - 1
    right, left = {"wide": me + 1}, {"wide": me - 1}
    after, before = {"wide": lax.rem(me + 1, n)}, {"wide": lax.rem(me + n - 1, n)}
    opposite = {"groups": other}
    pair = {"narrow": high * 2 + 1 - low}
    far = [{"narrow": lax.rem(high + d, across_n) * 2 + low} for d in range(1, across_n)]
    far_from = [{"narrow": lax.rem(high + across_n - d, across_n) * 2 + low} for d in range(1, across_n)]

    barrier = pltpu.get_barrier_semaphore()
    greeted = [after, before, opposite, pair] + far
    for device in greeted:
        pl.semaphore_signal(barrier, inc=1, device_id=device, device_id_type=MESH)

    def w_at(shard, part_of, c):
        start = pl.multiple_of(shard * depth + c * rows, rows)
        return wbuf.at[part_of, :, pl.ds(start, rows)]

    def wq_own(c):
        return wq_ref.at[
            :, pl.ds(pl.multiple_of(c * rows, rows), rows), pl.ds(pl.multiple_of(y * half, half), half)
        ]

    def o_at(shard, part_of, c):
        return wo_buf.at[shard, part_of, pl.ds(pl.multiple_of(c * wo_rows, wo_rows), wo_rows)]

    def wo_own(c):
        return wo_ref.at[spot, y, pl.ds(pl.multiple_of(c * wo_rows, wo_rows), wo_rows)]

    def remote(src, dst, send, recv, device):
        return pltpu.make_async_remote_copy(
            src_ref=src, dst_ref=dst, send_sem=send, recv_sem=recv,
            device_id=device, device_id_type=MESH,
        )

    def q_right(shard, c, src=None):
        dst = w_at(shard, y, c)
        return remote(dst if src is None else src, dst, qs_r.at[shard, c], qr.at[shard, c], right)

    def q_left(shard, c, src=None):
        dst = w_at(shard, y, c)
        return remote(dst if src is None else src, dst, qs_l.at[shard, c], qr.at[shard, c], left)

    def q_across(shard, c, part_of):
        ref = w_at(shard, part_of, c)
        return remote(ref, ref, qs_y.at[shard, c], qr_y.at[shard, c], opposite)

    def o_right(shard, c, src=None):
        dst = o_at(shard, y, c)
        return remote(dst if src is None else src, dst, os_r.at[shard, c], o_r.at[shard, c], right)

    def o_left(shard, c, src=None):
        dst = o_at(shard, y, c)
        return remote(dst if src is None else src, dst, os_l.at[shard, c], o_r.at[shard, c], left)

    def o_across(shard, c, part_of):
        ref = o_at(shard, part_of, c)
        return remote(ref, ref, os_y.at[shard, c], or_y.at[shard, c], opposite)

    own = [
        pltpu.make_async_copy(
            wq_ref.at[:, :, pl.ds(h * half, half)],
            wbuf.at[h, :, pl.ds(pl.multiple_of(me * depth, depth), depth)],
            own_sem.at[h],
        )
        for h in range(2)
    ]
    own.append(pltpu.make_async_copy(wo_ref.at[spot], wo_buf.at[me], own_sem.at[2]))
    for copy in own:
        copy.start()
    pl.semaphore_wait(barrier, len(greeted))

    @pl.loop(0, chunks)
    def _(c):
        @pl.when(has_right)
        def _():
            q_right(me, c, wq_own(c)).start()

        @pl.when(has_left)
        def _():
            q_left(me, c, wq_own(c)).start()

    acc[...] = jnp.zeros_like(acc)
    own[0].wait()
    own[1].wait()

    def add(shard, part_of, c):
        start = pl.multiple_of(shard * depth + c * rows, rows)
        piece = hidden_ref[:, pl.ds(start, rows)]
        for i in range(3):
            acc[part_of, i] += jnp.dot(
                piece, wbuf[part_of, i, pl.ds(start, rows)], preferred_element_type=jnp.float32
            )

    @pl.loop(0, 2 * chunks)
    def _(i):
        add(me, i // chunks, lax.rem(i, chunks))

    def add_across(t):
        s, c = t // chunks, lax.rem(t, chunks)
        for there, shard in ((me - 1 - s >= 0, me - 1 - s), (me + 1 + s <= n - 1, me + 1 + s)):
            @pl.when(there)
            def _():
                q_across(shard, c, other).wait_recv()
                add(shard, other, c)

    def send_own_wo():
        @pl.loop(0, wo_chunks)
        def _(c):
            @pl.when(has_right)
            def _():
                o_right(me, c, wo_own(c)).start()

            @pl.when(has_left)
            def _():
                o_left(me, c, wo_own(c)).start()

    @pl.loop(0, steps)
    def _(t):
        s, c = t // chunks, lax.rem(t, chunks)

        @pl.when(t == steps - chunks)
        def _():
            send_own_wo()

        @pl.when(me - 1 - s >= 0)
        def _():
            q_right(me - 1 - s, c).wait_recv()

            @pl.when(has_right)
            def _():
                q_right(me - 1 - s, c).start()

            q_across(me - 1 - s, c, y).start()

        @pl.when(me + 1 + s <= n - 1)
        def _():
            q_left(me + 1 + s, c).wait_recv()

            @pl.when(has_left)
            def _():
                q_left(me + 1 + s, c).start()

            q_across(me + 1 + s, c, y).start()

        for there, shard in ((me - 1 - s >= 0, me - 1 - s), (me + 1 + s <= n - 1, me + 1 + s)):
            @pl.when(there)
            def _():
                add(shard, y, c)

        @pl.when(t > 0)
        def _():
            add_across(t - 1)

    add_across(steps - 1)
    for h in range(2):
        q_buf[h] = acc[h, 0].astype(jnp.bfloat16)
        for i in range(2):
            kv_buf[h, i, SHIFT:] = acc[h, 1 + i].astype(jnp.bfloat16)

    kv_copy = remote(
        kv_buf.at[:, :, pl.ds(tok, SHIFT)], kv_buf.at[:, :, pl.ds(0, SHIFT)],
        kv_sem.at[0], kv_sem.at[1], after,
    )
    kv_copy.start()

    causal = lax.broadcasted_iota(jnp.int32, (SHIFT, 2 * SHIFT), 1) <= (
        lax.broadcasted_iota(jnp.int32, (SHIFT, 2 * SHIFT), 0) + SHIFT
    )

    def attend(h, b):
        lanes = slice((h % per_half) * HEAD_DIM, (h % per_half + 1) * HEAD_DIM)
        mine, seen = slice(b * SHIFT, (b + 1) * SHIFT), slice(b * SHIFT, (b + 2) * SHIFT)
        keys, values = kv_buf.at[h // per_half, 0], kv_buf.at[h // per_half, 1]
        scores = lax.dot_general(
            q_buf[h // per_half, mine, lanes], keys[seen, lanes], (((1,), (1,)), ((), ())),
            preferred_element_type=jnp.float32,
        ) * (1.0 / math.sqrt(HEAD_DIM))
        allowed = causal & (segq_ref[mine, :] == segk_ref[h, b])
        scores = jnp.where(allowed, scores, masked_out)
        exponent = jnp.exp(scores - jnp.max(scores, axis=-1, keepdims=True))
        weights = exponent / jnp.sum(exponent, axis=-1, keepdims=True)
        att[mine, h * HEAD_DIM : (h + 1) * HEAD_DIM] = jnp.dot(
            weights.astype(jnp.bfloat16), values[seen, lanes], preferred_element_type=jnp.float32
        ).astype(jnp.bfloat16)

    least = jnp.minimum(me, n - 1 - me)

    def block_of(k):
        turn = (k + 1) // 2
        near = jnp.where(lax.rem(k, 2) == 1, me - turn, me + turn)
        rest = jnp.where(me > least, me - (k - least), me + (k - least))
        return jnp.where(k <= 2 * least, near, rest)

    def pass_on(k):
        shard = block_of(k)

        @pl.loop(0, wo_chunks)
        def _(c):
            o_right(shard, c).wait_recv()

            @pl.when(jnp.logical_and(shard < me, has_right))
            def _():
                o_right(shard, c).start()

            @pl.when(jnp.logical_and(shard > me, has_left))
            def _():
                o_left(shard, c).start()

            o_across(shard, c, y).start()

    def pair_copy(shard, a):
        return remote(
            part.at[shard, a * 2 + 1 - low], pair_in.at[shard, a],
            pair_s.at[shard, a], pair_r.at[shard, a], pair,
        )

    def far_copy(shard, d):
        a = lax.rem(high + d, across_n)
        return remote(
            pair_sum.at[shard, a], far_in.at[shard, d - 1],
            far_s.at[shard, d - 1], far_r.at[shard, d - 1], far[d - 1],
        )

    def far_arrival(shard, d):
        return remote(
            pair_sum.at[shard, high], far_in.at[shard, d - 1],
            far_s.at[shard, d - 1], far_r.at[shard, d - 1], far_from[d - 1],
        )

    def multiply(k):
        shard = block_of(k)
        width = att.shape[1] // 2
        share = tok // narrow
        for p in range(narrow):
            a_rows = att[p * share : (p + 1) * share, :]
            total = jnp.dot(a_rows[:, :width], wo_buf[shard, 0], preferred_element_type=jnp.float32)
            total += jnp.dot(a_rows[:, width:], wo_buf[shard, 1], preferred_element_type=jnp.float32)
            part[shard, p] = total.astype(jnp.bfloat16)
        for a in range(across_n):
            pair_copy(shard, a).start()

    def sum_pair(k):
        shard = block_of(k)
        for a in range(across_n):
            pair_copy(shard, a).wait_recv()
            total = part[shard, a * 2 + low].astype(jnp.float32) + pair_in[shard, a].astype(jnp.float32)
            pair_sum[shard, a] = total.astype(jnp.bfloat16)
        for d in range(1, across_n):
            far_copy(shard, d).start()

    def finish(k):
        shard = block_of(k)
        total = part[shard, high * 2 + low].astype(jnp.float32) + pair_in[shard, high].astype(jnp.float32)
        for d in range(1, across_n):
            far_arrival(shard, d).wait_recv()
            total += far_in[shard, d - 1].astype(jnp.float32)
        out_ref[:, pl.ds(pl.multiple_of(shard * cols, cols), cols)] = total.astype(out_ref.dtype)

    heads = 2 * per_half
    for b in range(1, blocks):
        for h in range(heads):
            attend(h, b)
    pass_on(1)
    pass_on(2)
    kv_copy.wait_recv()
    for h in range(heads):
        attend(h, 0)
    own[2].wait()
    multiply(0)

    @pl.loop(1, n)
    def _(k):
        @pl.when(k > 2)
        def _():
            pass_on(k)

        sum_pair(k - 1)

        @pl.when(k > 1)
        def _():
            finish(k - 2)

        shard = block_of(k)

        @pl.loop(0, wo_chunks)
        def _(c):
            o_across(shard, c, other).wait_recv()

        multiply(k)

    sum_pair(n - 1)
    finish(n - 2)
    finish(n - 1)

    kv_copy.wait_send()

    @pl.loop(0, n)
    def _(shard):
        for a in range(across_n):
            pair_copy(shard, a).wait_send()
        for d in range(1, across_n):
            far_copy(shard, d).wait_send()
        goes_right = jnp.logical_and(shard <= me, has_right)
        goes_left = jnp.logical_and(shard >= me, has_left)
        for count, to_right, to_left, to_other in (
            (chunks, q_right, q_left, q_across), (wo_chunks, o_right, o_left, o_across)
        ):
            @pl.loop(0, count)
            def _(c):
                @pl.when(goes_right)
                def _():
                    to_right(shard, c).wait_send()

                @pl.when(goes_left)
                def _():
                    to_left(shard, c).wait_send()

                @pl.when(shard != me)
                def _():
                    to_other(shard, c, y).wait_send()


def layer(hidden, wq, wo, seg_q, seg_k):
    n, narrow = lax.axis_size("wide"), lax.axis_size("narrow")
    tok, width = hidden.shape
    half = wq.shape[2] // 2
    chunks = max(1, wq.shape[1] // ROWS)
    wo_chunks = WO_CHUNKS
    cols = wo.shape[3]
    share = tok // narrow
    vmem = pl.BlockSpec(memory_space=pltpu.VMEM)
    hbm = pl.BlockSpec(memory_space=pl.ANY)
    dma = pltpu.SemaphoreType.DMA
    bf16 = jnp.bfloat16
    return pl.pallas_call(
        functools.partial(layer_kernel, n, narrow, chunks, wo_chunks),
        out_shape=jax.ShapeDtypeStruct((share, n * cols), bf16),
        in_specs=[vmem, hbm, hbm, vmem, vmem],
        out_specs=vmem,
        scratch_shapes=[
            pltpu.VMEM((2, 3, width, half), bf16),
            pltpu.VMEM((2, 3, tok, half), jnp.float32),
            pltpu.VMEM((n,) + wo.shape[1:], bf16),
            pltpu.VMEM((2, tok, half), bf16),
            pltpu.VMEM((2, 2, tok + SHIFT, half), bf16),
            pltpu.VMEM((tok, 2 * half), bf16),
            pltpu.VMEM((n, narrow, share, cols), bf16),
            pltpu.VMEM((n, narrow // 2, share, cols), bf16),
            pltpu.VMEM((n, narrow // 2, share, cols), bf16),
            pltpu.VMEM((n, max(1, narrow // 2 - 1), share, cols), bf16),
            dma((3,)),
        ]
        + [dma((n, chunks))] * 5
        + [dma((n, wo_chunks))] * 5
        + [dma((2,))]
        + [dma((n, narrow // 2))] * 2
        + [dma((n, max(1, narrow // 2 - 1)))] * 2,
        compiler_params=pltpu.CompilerParams(
            collective_id=0, has_side_effects=True, vmem_limit_bytes=58 * 1024 * 1024
        ),
    )(hidden, wq, wo, seg_q, seg_k)


def per_device(hidden, w_qkv, w_out, seg_ids, shift_heads):
    tok_rows = hidden.shape[0]
    local_f = w_qkv.shape[2]
    heads_here = local_f // HEAD_DIM
    blocks = tok_rows // SHIFT
    narrow = lax.axis_size("narrow")
    first_tok = lax.axis_index("wide") * tok_rows
    shifted = lax.dynamic_slice_in_dim(shift_heads, lax.axis_index("narrow") * heads_here, heads_here) > 0

    doubled = jnp.concatenate([seg_ids[-SHIFT:], seg_ids], 0)
    seg_here = lax.dynamic_slice_in_dim(doubled, first_tok, tok_rows + SHIFT)
    seg_q = seg_here[SHIFT:, None]
    windows = jnp.stack([seg_here[b * SHIFT : (b + 2) * SHIFT] for b in range(blocks)])
    odd = (jnp.arange(blocks) % 2 == 1)[None, :, None]
    reaches = (shifted[:, None, None] != odd) | (jnp.arange(2 * SHIFT) >= SHIFT)[None, None, :]
    seg_k = jnp.where(reaches, windows[None], -1)[:, :, None, :]

    wq = w_qkv.transpose(1, 0, 2)
    wo = w_out.reshape(narrow, 2, local_f // 2, -1)
    return layer(hidden, wq, wo, seg_q, seg_k)


def hub_kernel(
    row_chunks, direct,
    hidden_ref, wq_ref, wo_ref, seg_ref, shift_ref, out_ref,
    wbuf, hid, acc, q_buf, kv_buf, att, wo_buf, stage, seg_col,
    own_sem, he_s, he_r, hx_s, hx_r, hc_s, hc_r,
    wm_s, wm_r, we_s, we_r, wy_s, wy_r, kv_sem,
    om_s, om_r, oe_s, oe_r, oy_s, oy_r, od_s, od_r,
    ax_s, ax_r, ae_s, ae_r, ac_s, ac_r, res_s, res_r,
):
    n, narrow = lax.axis_size("wide"), lax.axis_size("narrow")
    me = lax.axis_index("wide")
    y = lax.axis_index("groups")
    spot = lax.axis_index("narrow")
    opp = 1 - y
    side = me // (n // 2)
    inner, outer = n // 2 - 1 + side, side * (n - 1)
    far_inner, far_outer = n - 1 - inner, n - 1 - outer
    is_inner, is_outer = me == inner, me == outer
    high, low = spot // 2, lax.rem(spot, 2)
    core_n, x_n = high * 2 + 1 - low, (1 - high) * 2 + low
    diag_n = (1 - high) * 2 + 1 - low
    depth = wq_ref.shape[1]
    tok = hidden_ref.shape[0]
    heads = wbuf.shape[0]
    chunks = 2 * row_chunks
    rows = depth // row_chunks
    wo_chunks = 4
    quarter = tok // narrow
    span = 2 * tok
    blocks = span // SHIFT
    own_pos = 1 - side
    own_row = pl.multiple_of(own_pos * tok, tok)
    far_row = pl.multiple_of(side * tok, tok)
    wo_half, wo_cols = wo_buf.shape[2], wo_buf.shape[3]
    wo_rows, wo_lanes = wo_half // 2, wo_cols // 2
    cols = wo_ref.shape[1]
    to_core, to_x, to_y = {"narrow": core_n}, {"narrow": x_n}, {"groups": opp}
    to_far, to_inner, to_outer = {"wide": far_inner}, {"wide": inner}, {"wide": outer}
    my_pos = jnp.where(is_inner, own_pos, side)
    my_first = my_pos * (blocks // 2)
    first_b, second_b = my_first + 1 - my_pos, my_first + my_pos

    def remote(src, dst, send, recv, device):
        return pltpu.make_async_remote_copy(
            src_ref=src, dst_ref=dst, send_sem=send, recv_sem=recv,
            device_id=device, device_id_type=MESH,
        )

    def w_at(shard, part, c):
        start = pl.multiple_of(shard * depth + lax.rem(c, row_chunks) * rows, rows)
        return wbuf.at[c // row_chunks * 2 + part, :, pl.ds(start, rows)]

    def wq_at(part, c):
        start = pl.multiple_of(lax.rem(c, row_chunks) * rows, rows)
        lane = pl.multiple_of((c // row_chunks * 2 + part) * HEAD_DIM, HEAD_DIM)
        return wq_ref.at[:, pl.ds(start, rows), pl.ds(lane, HEAD_DIM)]

    def o_at(shard, part, c):
        start = pl.multiple_of(lax.rem(c, 2) * wo_rows, wo_rows)
        return wo_buf.at[shard, part, pl.ds(start, wo_rows), pl.ds(pl.multiple_of(c // 2 * wo_lanes, wo_lanes), wo_lanes)]

    def wo_at(part, c):
        start = pl.multiple_of(part * wo_half + lax.rem(c, 2) * wo_rows, wo_rows)
        lane = pl.multiple_of(spot * wo_cols + c // 2 * wo_lanes, wo_lanes)
        return wo_ref.at[pl.ds(start, wo_rows), pl.ds(lane, wo_lanes)]

    def h_at(row_n, k):
        start = pl.multiple_of(far_row + row_n * quarter, quarter)
        return hid.at[pl.ds(start, quarter), pl.ds(pl.multiple_of(k * depth, depth), depth)]

    def h_end(k):
        src = hidden_ref.at[
            pl.ds(pl.multiple_of(spot * quarter, quarter), quarter), pl.ds(pl.multiple_of(k * depth, depth), depth)
        ]
        return remote(src, h_at(spot, k), he_s.at[k], he_r.at[k], to_inner)

    def h_x(k, row_n):
        return remote(h_at(row_n, k), h_at(row_n, k), hx_s.at[k], hx_r.at[k], to_x)

    def h_core(j, k, row_n):
        return remote(h_at(row_n, k), h_at(row_n, k), hc_s.at[j, k], hc_r.at[j, k], to_core)

    def w_end(j, c):
        part = y if j == 0 else opp
        return remote(wq_at(part, c), w_at(outer, part, c), we_s.at[j, c], we_r.at[j, c], to_inner)

    def w_mid_send(s, c):
        if s == 0:
            return remote(wq_at(y, c), w_at(inner, y, c), wm_s.at[s, c], wm_r.at[s, c], to_far)
        return remote(w_at(outer, y, c), w_at(outer, y, c), wm_s.at[s, c], wm_r.at[s, c], to_far)

    def far_shard(s):
        return jnp.where(s == 0, far_inner, far_outer)

    def w_mid_recv(s, c):
        ref = w_at(far_shard(s), y, c)
        return remote(ref, ref, wm_s.at[s, c], wm_r.at[s, c], to_far)

    def y_shard(s):
        return jnp.where(s == 2, outer, far_shard(s))

    def w_y(s, c, part):
        ref = w_at(y_shard(s), part, c)
        return remote(ref, ref, wy_s.at[s, c], wy_r.at[s, c], to_y)

    def o_end(j, c):
        part = y if j == 0 else opp
        return remote(wo_at(part, c), o_at(outer, part, c), oe_s.at[j, c], oe_r.at[j, c], to_inner)

    def o_mid_send(s, c):
        if s == 0:
            return remote(wo_at(y, c), o_at(inner, y, c), om_s.at[s, c], om_r.at[s, c], to_far)
        return remote(o_at(outer, y, c), o_at(outer, y, c), om_s.at[s, c], om_r.at[s, c], to_far)

    def o_mid_recv(s, c):
        ref = o_at(far_shard(s), y, c)
        return remote(ref, ref, om_s.at[s, c], om_r.at[s, c], to_far)

    def o_down(s, c):
        if s == 0:
            return remote(wo_at(y, c), o_at(inner, y, c), od_s.at[s, c], od_r.at[s, c], to_outer)
        ref = o_at(far_shard(s - 1), y, c)
        return remote(ref, ref, od_s.at[s, c], od_r.at[s, c], to_outer)

    def o_down_recv(s, c):
        ref = o_at(inner if s == 0 else far_shard(s - 1), y, c)
        return remote(ref, ref, od_s.at[s, c], od_r.at[s, c], to_outer)

    def o_y(s, c, part):
        ref = o_at(inner if s == 2 else far_shard(s), part, c)
        return remote(ref, ref, oy_s.at[s, c], oy_r.at[s, c], to_y)

    def att_at(row_n, g, b):
        return att.at[row_n, g, pl.ds(pl.multiple_of(b * SHIFT, SHIFT), SHIFT)]

    def att_x(g, b, row_n):
        ref = att_at(row_n, g, b)
        return remote(ref, ref, ax_s.at[g, b], ax_r.at[g, b], to_x)

    def att_core(j, g, b, row_n):
        ref = att_at(row_n, g, b)
        return remote(ref, ref, ac_s.at[j, g, b], ac_r.at[j, g, b], to_core)

    def att_end(g, b):
        ref = att_at(spot, g, b)
        return remote(ref, ref, ae_s.at[g, b], ae_r.at[g, b], to_outer)

    def share(g, b):
        att_x(g, b, spot).start()
        att_core(0, g, b, spot).start()

    def relay(g, b):
        att_x(g, b, x_n).wait_recv()
        att_core(1, g, b, x_n).start()

    def gathered(b):
        for g in range(2):
            att_core(0, g, b, core_n).wait_recv()
            att_core(1, g, b, diag_n).wait_recv()

    shards = (me, jnp.where(is_inner, far_inner, inner), jnp.where(is_inner, outer, far_inner), far_outer)
    slots = ((0, 0, wo_cols), (1, 0, wo_cols), (2, 0, wo_cols), (3, 0, wo_lanes), (3, wo_lanes, wo_lanes))

    def res_cols(slot, row_n):
        order, lane, size = slots[slot]
        return pl.ds(pl.multiple_of(shards[order] * cols + row_n * wo_cols + lane, size), size)

    def result(slot, to_n):
        order, lane, size = slots[slot]
        return remote(
            stage.at[order, pl.ds(pl.multiple_of(to_n * quarter, quarter), quarter), lane : lane + size],
            out_ref.at[:, res_cols(slot, spot)],
            res_s.at[slot, to_n], res_r.at[slot, spot], {"narrow": to_n},
        )

    def result_arrival(slot, from_n):
        ref = out_ref.at[:, res_cols(slot, from_n)]
        return remote(ref, ref, res_s.at[slot, 0], res_r.at[slot, from_n], to_core)

    def multiply(slot, b):
        order, lane, size = slots[slot]
        mine = pl.ds(pl.multiple_of(b * SHIFT, SHIFT), SHIFT)
        local = b - my_first
        a_cols = att.shape[3]
        total = None
        for p in range(narrow):
            for g in range(2):
                start = (p % (narrow // 2) * 2 + g) * a_cols
                term = jnp.dot(
                    att[p, g, mine],
                    wo_buf[shards[order], p // (narrow // 2), start : start + a_cols, lane : lane + size],
                    preferred_element_type=jnp.float32,
                )
                total = term if total is None else total + term
        done = total.astype(jnp.bfloat16)
        stage[order, pl.ds(pl.multiple_of(local * SHIFT, SHIFT), SHIFT), lane : lane + size] = done
        for k in range(SHIFT // quarter):
            to_n = local * (SHIFT // quarter) + k

            @pl.when(spot == to_n)
            def _():
                out_ref[:, res_cols(slot, spot)] = done[k * quarter : (k + 1) * quarter]

            @pl.when(spot != to_n)
            def _():
                result(slot, to_n).start()

    def multiply_both(slot):
        @pl.loop(0, 2)
        def _(k):
            multiply(slot, jnp.where(k == 0, first_b, second_b))

    def finish_sends(y_slots):
        for slot in range(len(slots)):
            for p in range(narrow):
                @pl.when(spot != p)
                def _():
                    result_arrival(slot, p).wait_recv()
        for slot in range(len(slots)):
            for p in range(narrow):
                @pl.when(spot != p)
                def _():
                    result(slot, p).wait_send()
        for g in range(2):
            for b in (first_b, second_b):
                att_x(g, b, spot).wait_send()
                att_core(0, g, b, spot).wait_send()
                att_core(1, g, b, x_n).wait_send()

        @pl.loop(0, wo_chunks)
        def _(c):
            for s in y_slots:
                o_y(s, c, y).wait_send()

    def kv_copy(g):
        return remote(
            kv_buf.at[pl.ds(2 * g, 2), :, pl.ds(span, SHIFT)], kv_buf.at[pl.ds(2 * g, 2), :, pl.ds(0, SHIFT)],
            kv_sem.at[0, g], kv_sem.at[1, g], to_far,
        )

    barrier = pltpu.get_barrier_semaphore()

    def greet(peers):
        for device in peers:
            pl.semaphore_signal(barrier, inc=1, device_id=device, device_id_type=MESH)
        pl.semaphore_wait(barrier, len(peers))

    beside = [{"narrow": core_n}, {"narrow": x_n}, {"narrow": diag_n}, to_y]

    def own_wo(h):
        return pltpu.make_async_copy(
            wo_ref.at[pl.ds(h * wo_half, wo_half), pl.ds(pl.multiple_of(spot * wo_cols, wo_cols), wo_cols)],
            wo_buf.at[me, h],
            own_sem.at[heads + 1 + h],
        )

    @pl.when(is_outer)
    def _():
        greet(beside + [to_inner])

        @pl.loop(0, n)
        def _(k):
            h_end(k).start()

        def each_end(act):
            @pl.loop(0, chunks)
            def _(c):
                act(w_end(0, c))

            @pl.loop(0, direct)
            def _(c):
                act(w_end(1, c))

            @pl.loop(row_chunks, chunks)
            def _(c):
                act(w_end(1, c))

            for j in range(2):
                @pl.loop(0, wo_chunks)
                def _(c):
                    act(o_end(j, c))

        each_end(lambda copy: copy.start())
        for h in range(2):
            own_wo(h).start()

        def down(s, first, last):
            @pl.loop(first, last)
            def _(c):
                o_down_recv(s, c).wait_recv()
                o_y(2 if s == 0 else s - 1, c, y).start()

        def take(g, b):
            att_end(g, b).wait_recv()
            share(g, b)

        def y_arrived(s, first, last):
            @pl.loop(first, last)
            def _(c):
                o_y(s, c, opp).wait_recv()

        down(0, 0, wo_chunks)
        for h in range(2):
            own_wo(h).wait()
        y_arrived(2, 0, wo_chunks)
        take(0, first_b)
        relay(0, first_b)
        take(0, second_b)
        down(1, 0, 2)
        take(1, first_b)
        relay(0, second_b)
        relay(1, first_b)
        gathered(first_b)
        multiply(0, first_b)
        multiply(1, first_b)
        down(1, 2, wo_chunks)
        take(1, second_b)
        relay(1, second_b)
        gathered(second_b)
        multiply(0, second_b)
        multiply(1, second_b)
        down(2, 0, 1)
        y_arrived(0, 0, wo_chunks)
        multiply(2, first_b)
        down(2, 1, 2)
        multiply(2, second_b)
        down(2, 2, wo_chunks)
        for k in range(2):
            y_arrived(1, 2 * k, 2 * k + 2)
            multiply_both(3 + k)

        @pl.loop(0, n)
        def _(k):
            h_end(k).wait_send()

        each_end(lambda copy: copy.wait_send())
        finish_sends((0, 1, 2))

    @pl.when(is_inner)
    def _():
        own = [
            pltpu.make_async_copy(
                wq_ref.at[:, :, pl.ds(h * HEAD_DIM, HEAD_DIM)],
                wbuf.at[h, :, pl.ds(pl.multiple_of(inner * depth, depth), depth)],
                own_sem.at[h],
            )
            for h in range(heads)
        ]
        own.append(pltpu.make_async_copy(hidden_ref, hid.at[pl.ds(own_row, tok)], own_sem.at[heads]))
        for copy in own:
            copy.start()
        for h in range(2):
            own_wo(h).start()
        greet(beside + [to_far, to_outer])

        @pl.loop(0, chunks)
        def _(c):
            w_mid_send(0, c).start()

        @pl.loop(0, wo_chunks)
        def _(c):
            o_down(0, c).start()

        acc[...] = jnp.zeros_like(acc)
        seg_rows = seg_ref.shape[0]
        lanes = seg_ref.shape[1]
        seg_first = side * (span // lanes)
        for k in range(span // lanes):
            line = seg_ref[pl.ds(seg_first + k, 1), :]
            seg_col[k * lanes : (k + 1) * lanes, :] = jnp.broadcast_to(line, (lanes, lanes)).T

        def add(row, size, shard, part, c):
            start = pl.multiple_of(shard * depth + lax.rem(c, row_chunks) * rows, rows)
            head = c // row_chunks * 2 + part
            here = pl.ds(row, size)
            piece = hid[here, pl.ds(start, rows)]
            both = jnp.concatenate([wbuf[head, i, pl.ds(start, rows)] for i in range(2)], axis=1)
            found = jnp.dot(piece, both, preferred_element_type=jnp.float32)
            acc[head, 0, here] += found[:, :HEAD_DIM]
            acc[head, 1, here] += found[:, HEAD_DIM:]
            acc[head, 2, here] += jnp.dot(piece, wbuf[head, 2, pl.ds(start, rows)], preferred_element_type=jnp.float32)

        def add_all(shard, part, c):
            add(0, span, shard, part, c)

        def add_at(t, shard, part, c):
            @pl.when(t < chunks)
            def _():
                add(own_row, tok, shard, part, c)

            @pl.when(t >= chunks)
            def _():
                add_all(shard, part, c)

        for copy in own:
            copy.wait()

        @pl.loop(0, 2 * chunks)
        def _(u):
            add(own_row, tok, inner, u // chunks, lax.rem(u, chunks))

        lag = row_chunks
        lead = chunks - 2
        catch_up = 4 * chunks - lag

        @pl.loop(0, 2 * chunks)
        def _(t):
            s, c = t // chunks, lax.rem(t, chunks)
            w_mid_recv(s, c).wait_recv()
            w_y(s, c, y).start()

            q = t - lead

            @pl.when(jnp.logical_and(q >= 0, q < chunks))
            def _():
                w_end(0, q).wait_recv()
                w_mid_send(1, q).start()

            @pl.when(jnp.logical_and(q >= direct, q < row_chunks))
            def _():
                w_y(2, q, y).start()

            @pl.when(jnp.logical_and(t >= 1, t < 1 + n))
            def _():
                h_end(t - 1).wait_recv()
                h_x(t - 1, spot).start()
                h_core(0, t - 1, spot).start()

            @pl.when(jnp.logical_and(t >= 4, t < 4 + n))
            def _():
                h_x(t - 4, x_n).wait_recv()
                h_core(1, t - 4, x_n).start()

            @pl.when(t == chunks)
            def _():
                @pl.loop(0, n)
                def _(k):
                    h_core(0, k, core_n).wait_recv()
                    h_core(1, k, diag_n).wait_recv()

            add_at(t, far_shard(s), y, c)

            @pl.when(t >= lag)
            def _():
                v = t - lag
                w_y(v // chunks, lax.rem(v, chunks), opp).wait_recv()
                add_at(t, far_shard(v // chunks), opp, lax.rem(v, chunks))

            @pl.when(t >= chunks)
            def _():
                add_all(outer, y, t - chunks)
                u0 = 4 * (t - chunks)

                @pl.loop(u0, jnp.minimum(u0 + 4, catch_up))
                def _(u):
                    first = u < 2 * chunks
                    part = jnp.where(first, u // chunks, jnp.where(u < 3 * chunks, y, opp))
                    add(far_row, tok, jnp.where(first, inner, far_inner), part, lax.rem(u, chunks))

            @pl.when(t >= chunks + row_chunks)
            def _():
                k = lax.rem(t - chunks - row_chunks + direct, row_chunks)

                @pl.when(k < direct)
                def _():
                    w_end(1, k).wait_recv()

                @pl.when(k >= direct)
                def _():
                    w_y(2, k, opp).wait_recv()

                add_all(outer, opp, k)

        causal = lax.broadcasted_iota(jnp.int32, (SHIFT, 2 * SHIFT), 1) <= (
            lax.broadcasted_iota(jnp.int32, (SHIFT, 2 * SHIFT), 0) + SHIFT
        )
        per_block = SHIFT // lanes

        def seg_line(b):
            at = [lax.rem(seg_first + b * per_block + k + seg_rows, seg_rows) for k in range(per_block)]
            return jnp.concatenate([seg_ref[pl.ds(i, 1), :] for i in at], axis=1)

        def attend(g, b):
            mine, seen = slice(b * SHIFT, (b + 1) * SHIFT), slice(b * SHIFT, (b + 2) * SHIFT)
            seg_q = jnp.concatenate([seg_col[mine, :]] * (2 * per_block), axis=1)
            near, prior = seg_line(b), seg_line(b - 1)
            for k in range(2):
                h = 2 * g + k
                reach = shift_ref[spot * heads + h]
                if b % 2 == 1:
                    reach = 1 - reach
                seg_k = jnp.concatenate([prior * reach + (reach - 1), near], axis=1)
                scores = lax.dot_general(
                    q_buf[h, mine], kv_buf[h, 0, seen], (((1,), (1,)), ((), ())),
                    preferred_element_type=jnp.float32,
                ) * (1.0 / math.sqrt(HEAD_DIM))
                allowed = causal & (seg_q == seg_k)
                scores = jnp.where(allowed, scores, masked_out)
                exponent = jnp.exp(scores - jnp.max(scores, axis=-1, keepdims=True))
                weights = exponent / jnp.sum(exponent, axis=-1, keepdims=True)
                att[spot, g, mine, k * HEAD_DIM : (k + 1) * HEAD_DIM] = jnp.dot(
                    weights.astype(jnp.bfloat16), kv_buf[h, 1, seen], preferred_element_type=jnp.float32
                ).astype(jnp.bfloat16)
            pos = b // (blocks // 2)

            @pl.when(pos == own_pos)
            def _():
                share(g, b)

            @pl.when(pos != own_pos)
            def _():
                att_end(g, b).start()

        def settle(g):
            for h in (2 * g, 2 * g + 1):
                for i in range(2):
                    kv_buf[h, i, SHIFT:] = acc[h, 1 + i].astype(jnp.bfloat16)
            kv_copy(g).start()
            for h in (2 * g, 2 * g + 1):
                q_buf[h] = acc[h, 0].astype(jnp.bfloat16)

        def near_wo(c):
            o_mid_recv(0, c).wait_recv()
            o_y(0, c, y).start()
            o_down(1, c).start()

        def far_wo(c):
            o_mid_recv(1, c).wait_recv()
            o_y(1, c, y).start()
            o_down(2, c).start()

        def pass_wo(c):
            o_end(0, c).wait_recv()
            o_mid_send(1, c).start()

        def last_y(c):
            w_y(1, c, opp).wait_recv()
            add_all(far_outer, opp, c)

        def last_end(c):
            w_end(1, c).wait_recv()
            add_all(outer, opp, c)

        settle(0)
        for c in range(2):
            o_mid_send(0, c).start()
        attend(0, 1)
        last_y(row_chunks)
        attend(0, 2)
        last_y(row_chunks + 1)
        attend(0, 3)

        @pl.loop(row_chunks, chunks - 2)
        def _(c):
            last_end(c)

        relay(0, first_b)
        last_y(row_chunks + 2)
        kv_copy(0).wait_recv()
        attend(0, 0)

        @pl.loop(chunks - 2, chunks)
        def _(c):
            last_end(c)

        last_y(row_chunks + 3)
        settle(1)
        for c in range(2, wo_chunks):
            o_mid_send(0, c).start()
        attend(1, 1)
        near_wo(0)
        near_wo(1)
        attend(1, 2)
        pass_wo(0)
        pass_wo(1)
        attend(1, 3)
        relay(0, second_b)
        pass_wo(2)
        for h in range(2):
            own_wo(h).wait()
        relay(1, first_b)
        kv_copy(1).wait_recv()
        attend(1, 0)
        pass_wo(3)
        gathered(first_b)
        multiply(0, first_b)
        near_wo(2)
        near_wo(3)
        relay(1, second_b)
        gathered(second_b)
        multiply(0, second_b)
        far_wo(0)

        @pl.loop(0, wo_chunks)
        def _(c):
            o_y(0, c, opp).wait_recv()

        multiply(1, first_b)
        far_wo(1)
        multiply(1, second_b)

        @pl.loop(0, wo_chunks)
        def _(c):
            o_end(1, c).wait_recv()

        multiply(2, first_b)
        far_wo(2)
        multiply(2, second_b)
        far_wo(3)
        for k in range(2):
            for c in range(2 * k, 2 * k + 2):
                o_y(1, c, opp).wait_recv()
            multiply_both(3 + k)

        @pl.loop(0, n)
        def _(k):
            h_x(k, spot).wait_send()
            h_core(0, k, spot).wait_send()
            h_core(1, k, x_n).wait_send()

        @pl.loop(0, chunks)
        def _(c):
            for s in range(2):
                w_mid_send(s, c).wait_send()
                w_y(s, c, y).wait_send()

        @pl.loop(direct, row_chunks)
        def _(c):
            w_y(2, c, y).wait_send()

        @pl.loop(0, wo_chunks)
        def _(c):
            for s in range(2):
                o_mid_send(s, c).wait_send()
            for s in range(3):
                o_down(s, c).wait_send()

        other_first = (1 - own_pos) * (blocks // 2)
        for g in range(2):
            kv_copy(g).wait_send()
            for k in range(blocks // 2):
                att_end(g, other_first + k).wait_send()
        finish_sends((0, 1))


def hub_layer(hidden, wq, wo, seg, shift_heads):
    n, narrow = lax.axis_size("wide"), lax.axis_size("narrow")
    tok, width = hidden.shape
    heads = wq.shape[2] // HEAD_DIM
    row_chunks = wq.shape[1] // HUB_ROWS
    chunks, wo_chunks = 2 * row_chunks, 4
    cols = wo.shape[1]
    wo_half, wo_cols = wo.shape[0] // 2, cols // narrow
    quarter, span = tok // narrow, 2 * tok
    blocks = span // SHIFT
    vmem = pl.BlockSpec(memory_space=pltpu.VMEM)
    smem = pl.BlockSpec(memory_space=pltpu.SMEM)
    hbm = pl.BlockSpec(memory_space=pl.ANY)
    dma = pltpu.SemaphoreType.DMA
    bf16 = jnp.bfloat16
    return pl.pallas_call(
        functools.partial(hub_kernel, row_chunks, DIRECT),
        out_shape=jax.ShapeDtypeStruct((quarter, n * cols), bf16),
        in_specs=[hbm, hbm, hbm, vmem, smem],
        out_specs=vmem,
        scratch_shapes=[
            pltpu.VMEM((heads, 3, width, HEAD_DIM), bf16),
            pltpu.VMEM((span, width), bf16),
            pltpu.VMEM((heads, 3, span, HEAD_DIM), jnp.float32),
            pltpu.VMEM((heads, span, HEAD_DIM), bf16),
            pltpu.VMEM((heads, 2, span + SHIFT, HEAD_DIM), bf16),
            pltpu.VMEM((narrow, 2, span, 2 * HEAD_DIM), bf16),
            pltpu.VMEM((n, 2, wo_half, wo_cols), bf16),
            pltpu.VMEM((n, tok, wo_cols), bf16),
            pltpu.VMEM((span, seg.shape[1]), jnp.int32),
            dma((heads + 3,)),
        ]
        + [dma((n,))] * 4
        + [dma((2, n))] * 2
        + [dma((2, chunks))] * 4
        + [dma((3, chunks))] * 2
        + [dma((2, 2))]
        + [dma((2, wo_chunks))] * 4
        + [dma((3, wo_chunks))] * 4
        + [dma((2, blocks))] * 4
        + [dma((2, 2, blocks))] * 2
        + [dma((5, narrow))] * 2,
        compiler_params=pltpu.CompilerParams(
            collective_id=0, has_side_effects=True, vmem_limit_bytes=58 * 1024 * 1024
        ),
    )(hidden, wq, wo, seg, shift_heads)


def hub_per_device(hidden, w_qkv, w_out, seg_ids, shift_heads):
    return hub_layer(hidden, w_qkv.transpose(1, 0, 2), w_out, seg_ids.reshape(-1, 128), shift_heads)


def solution(mesh):
    placed = (
        P(("groups", "wide"), None),
        P("wide", None, "narrow"),
        P(None, "wide"),
        P("groups"),
        P(),
    )
    shape = mesh.shape
    hub = shape["groups"] == 2 and shape["wide"] == 4 and shape["narrow"] == 4
    return jax.shard_map(
        hub_per_device if hub else per_device,
        mesh=mesh,
        in_specs=placed,
        out_specs=P(("groups", "wide", "narrow"), None),
        check_vma=False,
    )
```

```python
import functools
import math

import jax
import jax.numpy as jnp
from jax import lax
from jax.experimental import pallas as pl
from jax.experimental.pallas import tpu as pltpu
from jax.sharding import PartitionSpec as P

HEAD_DIM = 128
GROUP = 512
SHIFT = 256

masked_out = -1e30
MESH = pl.DeviceIdType.MESH
ROWS = 128
WO_CHUNKS = 4
HUB_ROWS = 256
DIRECT = 2


def layer_kernel(
    n, narrow, chunks, wo_chunks,
    hidden_ref, wq_ref, wo_ref, segq_ref, segk_ref, out_ref,
    wbuf, acc, wo_buf, q_buf, kv_buf, att, part, pair_in, pair_sum, far_in,
    own_sem,
    qs_r, qs_l, qr, qs_y, qr_y,
    os_r, os_l, o_r, os_y, or_y,
    kv_sem, pair_s, pair_r, far_s, far_r,
):
    me = lax.axis_index("wide")
    y = lax.axis_index("groups")
    spot = lax.axis_index("narrow")
    other = 1 - y
    across_n = narrow // 2
    high, low = spot // 2, lax.rem(spot, 2)
    depth = wq_ref.shape[1]
    half = wbuf.shape[3]
    tok = hidden_ref.shape[0]
    rows = depth // chunks
    steps = (n - 1) * chunks
    wo_rows = wo_buf.shape[2] // wo_chunks
    cols = wo_buf.shape[3]
    blocks = tok // SHIFT
    per_half = half // HEAD_DIM
    has_left, has_right = me > 0, me < n - 1
    right, left = {"wide": me + 1}, {"wide": me - 1}
    after, before = {"wide": lax.rem(me + 1, n)}, {"wide": lax.rem(me + n - 1, n)}
    opposite = {"groups": other}
    pair = {"narrow": high * 2 + 1 - low}
    far = [{"narrow": lax.rem(high + d, across_n) * 2 + low} for d in range(1, across_n)]
    far_from = [{"narrow": lax.rem(high + across_n - d, across_n) * 2 + low} for d in range(1, across_n)]

    barrier = pltpu.get_barrier_semaphore()
    greeted = [after, before, opposite, pair] + far
    for device in greeted:
        pl.semaphore_signal(barrier, inc=1, device_id=device, device_id_type=MESH)

    def w_at(shard, part_of, c):
        start = pl.multiple_of(shard * depth + c * rows, rows)
        return wbuf.at[part_of, :, pl.ds(start, rows)]

    def wq_own(c):
        return wq_ref.at[
            :, pl.ds(pl.multiple_of(c * rows, rows), rows), pl.ds(pl.multiple_of(y * half, half), half)
        ]

    def o_at(shard, part_of, c):
        return wo_buf.at[shard, part_of, pl.ds(pl.multiple_of(c * wo_rows, wo_rows), wo_rows)]

    def wo_own(c):
        return wo_ref.at[spot, y, pl.ds(pl.multiple_of(c * wo_rows, wo_rows), wo_rows)]

    def remote(src, dst, send, recv, device):
        return pltpu.make_async_remote_copy(
            src_ref=src, dst_ref=dst, send_sem=send, recv_sem=recv,
            device_id=device, device_id_type=MESH,
        )

    def q_right(shard, c, src=None):
        dst = w_at(shard, y, c)
        return remote(dst if src is None else src, dst, qs_r.at[shard, c], qr.at[shard, c], right)

    def q_left(shard, c, src=None):
        dst = w_at(shard, y, c)
        return remote(dst if src is None else src, dst, qs_l.at[shard, c], qr.at[shard, c], left)

    def q_across(shard, c, part_of):
        ref = w_at(shard, part_of, c)
        return remote(ref, ref, qs_y.at[shard, c], qr_y.at[shard, c], opposite)

    def o_right(shard, c, src=None):
        dst = o_at(shard, y, c)
        return remote(dst if src is None else src, dst, os_r.at[shard, c], o_r.at[shard, c], right)

    def o_left(shard, c, src=None):
        dst = o_at(shard, y, c)
        return remote(dst if src is None else src, dst, os_l.at[shard, c], o_r.at[shard, c], left)

    def o_across(shard, c, part_of):
        ref = o_at(shard, part_of, c)
        return remote(ref, ref, os_y.at[shard, c], or_y.at[shard, c], opposite)

    own = [
        pltpu.make_async_copy(
            wq_ref.at[:, :, pl.ds(h * half, half)],
            wbuf.at[h, :, pl.ds(pl.multiple_of(me * depth, depth), depth)],
            own_sem.at[h],
        )
        for h in range(2)
    ]
    own.append(pltpu.make_async_copy(wo_ref.at[spot], wo_buf.at[me], own_sem.at[2]))
    for copy in own:
        copy.start()
    pl.semaphore_wait(barrier, len(greeted))

    @pl.loop(0, chunks)
    def _(c):
        @pl.when(has_right)
        def _():
            q_right(me, c, wq_own(c)).start()

        @pl.when(has_left)
        def _():
            q_left(me, c, wq_own(c)).start()

    acc[...] = jnp.zeros_like(acc)
    own[0].wait()
    own[1].wait()

    def add(shard, part_of, c):
        start = pl.multiple_of(shard * depth + c * rows, rows)
        piece = hidden_ref[:, pl.ds(start, rows)]
        for i in range(3):
            acc[part_of, i] += jnp.dot(
                piece, wbuf[part_of, i, pl.ds(start, rows)], preferred_element_type=jnp.float32
            )

    @pl.loop(0, 2 * chunks)
    def _(i):
        add(me, i // chunks, lax.rem(i, chunks))

    def add_across(t):
        s, c = t // chunks, lax.rem(t, chunks)
        for there, shard in ((me - 1 - s >= 0, me - 1 - s), (me + 1 + s <= n - 1, me + 1 + s)):
            @pl.when(there)
            def _():
                q_across(shard, c, other).wait_recv()
                add(shard, other, c)

    def send_own_wo():
        @pl.loop(0, wo_chunks)
        def _(c):
            @pl.when(has_right)
            def _():
                o_right(me, c, wo_own(c)).start()

            @pl.when(has_left)
            def _():
                o_left(me, c, wo_own(c)).start()

    @pl.loop(0, steps)
    def _(t):
        s, c = t // chunks, lax.rem(t, chunks)

        @pl.when(t == steps - chunks)
        def _():
            send_own_wo()

        @pl.when(me - 1 - s >= 0)
        def _():
            q_right(me - 1 - s, c).wait_recv()

            @pl.when(has_right)
            def _():
                q_right(me - 1 - s, c).start()

            q_across(me - 1 - s, c, y).start()

        @pl.when(me + 1 + s <= n - 1)
        def _():
            q_left(me + 1 + s, c).wait_recv()

            @pl.when(has_left)
            def _():
                q_left(me + 1 + s, c).start()

            q_across(me + 1 + s, c, y).start()

        for there, shard in ((me - 1 - s >= 0, me - 1 - s), (me + 1 + s <= n - 1, me + 1 + s)):
            @pl.when(there)
            def _():
                add(shard, y, c)

        @pl.when(t > 0)
        def _():
            add_across(t - 1)

    add_across(steps - 1)
    for h in range(2):
        q_buf[h] = acc[h, 0].astype(jnp.bfloat16)
        for i in range(2):
            kv_buf[h, i, SHIFT:] = acc[h, 1 + i].astype(jnp.bfloat16)

    kv_copy = remote(
        kv_buf.at[:, :, pl.ds(tok, SHIFT)], kv_buf.at[:, :, pl.ds(0, SHIFT)],
        kv_sem.at[0], kv_sem.at[1], after,
    )
    kv_copy.start()

    causal = lax.broadcasted_iota(jnp.int32, (SHIFT, 2 * SHIFT), 1) <= (
        lax.broadcasted_iota(jnp.int32, (SHIFT, 2 * SHIFT), 0) + SHIFT
    )

    def attend(h, b):
        lanes = slice((h % per_half) * HEAD_DIM, (h % per_half + 1) * HEAD_DIM)
        mine, seen = slice(b * SHIFT, (b + 1) * SHIFT), slice(b * SHIFT, (b + 2) * SHIFT)
        keys, values = kv_buf.at[h // per_half, 0], kv_buf.at[h // per_half, 1]
        scores = lax.dot_general(
            q_buf[h // per_half, mine, lanes], keys[seen, lanes], (((1,), (1,)), ((), ())),
            preferred_element_type=jnp.float32,
        ) * (1.0 / math.sqrt(HEAD_DIM))
        allowed = causal & (segq_ref[mine, :] == segk_ref[h, b])
        scores = jnp.where(allowed, scores, masked_out)
        exponent = jnp.exp(scores - jnp.max(scores, axis=-1, keepdims=True))
        weights = exponent / jnp.sum(exponent, axis=-1, keepdims=True)
        att[mine, h * HEAD_DIM : (h + 1) * HEAD_DIM] = jnp.dot(
            weights.astype(jnp.bfloat16), values[seen, lanes], preferred_element_type=jnp.float32
        ).astype(jnp.bfloat16)

    least = jnp.minimum(me, n - 1 - me)

    def block_of(k):
        turn = (k + 1) // 2
        near = jnp.where(lax.rem(k, 2) == 1, me - turn, me + turn)
        rest = jnp.where(me > least, me - (k - least), me + (k - least))
        return jnp.where(k <= 2 * least, near, rest)

    def pass_on(k):
        shard = block_of(k)

        @pl.loop(0, wo_chunks)
        def _(c):
            o_right(shard, c).wait_recv()

            @pl.when(jnp.logical_and(shard < me, has_right))
            def _():
                o_right(shard, c).start()

            @pl.when(jnp.logical_and(shard > me, has_left))
            def _():
                o_left(shard, c).start()

            o_across(shard, c, y).start()

    def pair_copy(shard, a):
        return remote(
            part.at[shard, a * 2 + 1 - low], pair_in.at[shard, a],
            pair_s.at[shard, a], pair_r.at[shard, a], pair,
        )

    def far_copy(shard, d):
        a = lax.rem(high + d, across_n)
        return remote(
            pair_sum.at[shard, a], far_in.at[shard, d - 1],
            far_s.at[shard, d - 1], far_r.at[shard, d - 1], far[d - 1],
        )

    def far_arrival(shard, d):
        return remote(
            pair_sum.at[shard, high], far_in.at[shard, d - 1],
            far_s.at[shard, d - 1], far_r.at[shard, d - 1], far_from[d - 1],
        )

    def multiply(k):
        shard = block_of(k)
        width = att.shape[1] // 2
        share = tok // narrow
        for p in range(narrow):
            a_rows = att[p * share : (p + 1) * share, :]
            total = jnp.dot(a_rows[:, :width], wo_buf[shard, 0], preferred_element_type=jnp.float32)
            total += jnp.dot(a_rows[:, width:], wo_buf[shard, 1], preferred_element_type=jnp.float32)
            part[shard, p] = total.astype(jnp.bfloat16)
        for a in range(across_n):
            pair_copy(shard, a).start()

    def sum_pair(k):
        shard = block_of(k)
        for a in range(across_n):
            pair_copy(shard, a).wait_recv()
            total = part[shard, a * 2 + low].astype(jnp.float32) + pair_in[shard, a].astype(jnp.float32)
            pair_sum[shard, a] = total.astype(jnp.bfloat16)
        for d in range(1, across_n):
            far_copy(shard, d).start()

    def finish(k):
        shard = block_of(k)
        total = part[shard, high * 2 + low].astype(jnp.float32) + pair_in[shard, high].astype(jnp.float32)
        for d in range(1, across_n):
            far_arrival(shard, d).wait_recv()
            total += far_in[shard, d - 1].astype(jnp.float32)
        out_ref[:, pl.ds(pl.multiple_of(shard * cols, cols), cols)] = total.astype(out_ref.dtype)

    heads = 2 * per_half
    for b in range(1, blocks):
        for h in range(heads):
            attend(h, b)
    pass_on(1)
    pass_on(2)
    kv_copy.wait_recv()
    for h in range(heads):
        attend(h, 0)
    own[2].wait()
    multiply(0)

    @pl.loop(1, n)
    def _(k):
        @pl.when(k > 2)
        def _():
            pass_on(k)

        sum_pair(k - 1)

        @pl.when(k > 1)
        def _():
            finish(k - 2)

        shard = block_of(k)

        @pl.loop(0, wo_chunks)
        def _(c):
            o_across(shard, c, other).wait_recv()

        multiply(k)

    sum_pair(n - 1)
    finish(n - 2)
    finish(n - 1)

    kv_copy.wait_send()

    @pl.loop(0, n)
    def _(shard):
        for a in range(across_n):
            pair_copy(shard, a).wait_send()
        for d in range(1, across_n):
            far_copy(shard, d).wait_send()
        goes_right = jnp.logical_and(shard <= me, has_right)
        goes_left = jnp.logical_and(shard >= me, has_left)
        for count, to_right, to_left, to_other in (
            (chunks, q_right, q_left, q_across), (wo_chunks, o_right, o_left, o_across)
        ):
            @pl.loop(0, count)
            def _(c):
                @pl.when(goes_right)
                def _():
                    to_right(shard, c).wait_send()

                @pl.when(goes_left)
                def _():
                    to_left(shard, c).wait_send()

                @pl.when(shard != me)
                def _():
                    to_other(shard, c, y).wait_send()


def layer(hidden, wq, wo, seg_q, seg_k):
    n, narrow = lax.axis_size("wide"), lax.axis_size("narrow")
    tok, width = hidden.shape
    half = wq.shape[2] // 2
    chunks = max(1, wq.shape[1] // ROWS)
    wo_chunks = WO_CHUNKS
    cols = wo.shape[3]
    share = tok // narrow
    vmem = pl.BlockSpec(memory_space=pltpu.VMEM)
    hbm = pl.BlockSpec(memory_space=pl.ANY)
    dma = pltpu.SemaphoreType.DMA
    bf16 = jnp.bfloat16
    return pl.pallas_call(
        functools.partial(layer_kernel, n, narrow, chunks, wo_chunks),
        out_shape=jax.ShapeDtypeStruct((share, n * cols), bf16),
        in_specs=[vmem, hbm, hbm, vmem, vmem],
        out_specs=vmem,
        scratch_shapes=[
            pltpu.VMEM((2, 3, width, half), bf16),
            pltpu.VMEM((2, 3, tok, half), jnp.float32),
            pltpu.VMEM((n,) + wo.shape[1:], bf16),
            pltpu.VMEM((2, tok, half), bf16),
            pltpu.VMEM((2, 2, tok + SHIFT, half), bf16),
            pltpu.VMEM((tok, 2 * half), bf16),
            pltpu.VMEM((n, narrow, share, cols), bf16),
            pltpu.VMEM((n, narrow // 2, share, cols), bf16),
            pltpu.VMEM((n, narrow // 2, share, cols), bf16),
            pltpu.VMEM((n, max(1, narrow // 2 - 1), share, cols), bf16),
            dma((3,)),
        ]
        + [dma((n, chunks))] * 5
        + [dma((n, wo_chunks))] * 5
        + [dma((2,))]
        + [dma((n, narrow // 2))] * 2
        + [dma((n, max(1, narrow // 2 - 1)))] * 2,
        compiler_params=pltpu.CompilerParams(
            collective_id=0, has_side_effects=True, vmem_limit_bytes=58 * 1024 * 1024
        ),
    )(hidden, wq, wo, seg_q, seg_k)


def per_device(hidden, w_qkv, w_out, seg_ids, shift_heads):
    tok_rows = hidden.shape[0]
    local_f = w_qkv.shape[2]
    heads_here = local_f // HEAD_DIM
    blocks = tok_rows // SHIFT
    narrow = lax.axis_size("narrow")
    first_tok = lax.axis_index("wide") * tok_rows
    shifted = lax.dynamic_slice_in_dim(shift_heads, lax.axis_index("narrow") * heads_here, heads_here) > 0

    doubled = jnp.concatenate([seg_ids[-SHIFT:], seg_ids], 0)
    seg_here = lax.dynamic_slice_in_dim(doubled, first_tok, tok_rows + SHIFT)
    seg_q = seg_here[SHIFT:, None]
    windows = jnp.stack([seg_here[b * SHIFT : (b + 2) * SHIFT] for b in range(blocks)])
    odd = (jnp.arange(blocks) % 2 == 1)[None, :, None]
    reaches = (shifted[:, None, None] != odd) | (jnp.arange(2 * SHIFT) >= SHIFT)[None, None, :]
    seg_k = jnp.where(reaches, windows[None], -1)[:, :, None, :]

    wq = w_qkv.transpose(1, 0, 2)
    wo = w_out.reshape(narrow, 2, local_f // 2, -1)
    return layer(hidden, wq, wo, seg_q, seg_k)


def hub_kernel(
    row_chunks, direct,
    hidden_ref, wq_ref, wo_ref, seg_ref, shift_ref, out_ref,
    wbuf, hid, acc, q_buf, kv_buf, att, wo_buf, stage, seg_col,
    own_sem, he_s, he_r, hx_s, hx_r, hc_s, hc_r,
    wm_s, wm_r, we_s, we_r, wy_s, wy_r, kv_sem,
    om_s, om_r, oe_s, oe_r, oy_s, oy_r,
    ax_s, ax_r, ac_s, ac_r, res_s, res_r,
):
    n, narrow = lax.axis_size("wide"), lax.axis_size("narrow")
    me = lax.axis_index("wide")
    y = lax.axis_index("groups")
    spot = lax.axis_index("narrow")
    opp = 1 - y
    side = me // (n // 2)
    inner, outer = n // 2 - 1 + side, side * (n - 1)
    far_inner, far_outer = n - 1 - inner, n - 1 - outer
    is_inner, is_outer = me == inner, me == outer
    high, low = spot // 2, lax.rem(spot, 2)
    core_n, x_n = high * 2 + 1 - low, (1 - high) * 2 + low
    diag_n = (1 - high) * 2 + 1 - low
    depth = wq_ref.shape[1]
    tok = hidden_ref.shape[0]
    heads = wbuf.shape[0]
    chunks = 2 * row_chunks
    rows = depth // row_chunks
    wo_chunks = 4
    quarter = tok // narrow
    span = 2 * tok
    blocks = span // SHIFT
    own_pos = 1 - side
    own_row = pl.multiple_of(own_pos * tok, tok)
    far_row = pl.multiple_of(side * tok, tok)
    wo_half, wo_cols = wo_buf.shape[2], wo_buf.shape[3]
    wo_rows, wo_lanes = wo_half // 2, wo_cols // 2
    cols = wo_ref.shape[1]
    to_core, to_x, to_y = {"narrow": core_n}, {"narrow": x_n}, {"groups": opp}
    to_far, to_inner = {"wide": far_inner}, {"wide": inner}

    def remote(src, dst, send, recv, device):
        return pltpu.make_async_remote_copy(
            src_ref=src, dst_ref=dst, send_sem=send, recv_sem=recv,
            device_id=device, device_id_type=MESH,
        )

    def w_at(shard, part, c):
        start = pl.multiple_of(shard * depth + lax.rem(c, row_chunks) * rows, rows)
        return wbuf.at[c // row_chunks * 2 + part, :, pl.ds(start, rows)]

    def wq_at(part, c):
        start = pl.multiple_of(lax.rem(c, row_chunks) * rows, rows)
        lane = pl.multiple_of((c // row_chunks * 2 + part) * HEAD_DIM, HEAD_DIM)
        return wq_ref.at[:, pl.ds(start, rows), pl.ds(lane, HEAD_DIM)]

    def o_at(shard, part, c):
        start = pl.multiple_of(lax.rem(c, 2) * wo_rows, wo_rows)
        return wo_buf.at[shard, part, pl.ds(start, wo_rows), pl.ds(pl.multiple_of(c // 2 * wo_lanes, wo_lanes), wo_lanes)]

    def wo_at(part, c):
        start = pl.multiple_of(part * wo_half + lax.rem(c, 2) * wo_rows, wo_rows)
        lane = pl.multiple_of(spot * wo_cols + c // 2 * wo_lanes, wo_lanes)
        return wo_ref.at[pl.ds(start, wo_rows), pl.ds(lane, wo_lanes)]

    def h_at(row_n, k):
        start = pl.multiple_of(far_row + row_n * quarter, quarter)
        return hid.at[pl.ds(start, quarter), pl.ds(pl.multiple_of(k * depth, depth), depth)]

    def h_end(k):
        src = hidden_ref.at[
            pl.ds(pl.multiple_of(spot * quarter, quarter), quarter), pl.ds(pl.multiple_of(k * depth, depth), depth)
        ]
        return remote(src, h_at(spot, k), he_s.at[k], he_r.at[k], to_inner)

    def h_x(k, row_n):
        return remote(h_at(row_n, k), h_at(row_n, k), hx_s.at[k], hx_r.at[k], to_x)

    def h_core(j, k, row_n):
        return remote(h_at(row_n, k), h_at(row_n, k), hc_s.at[j, k], hc_r.at[j, k], to_core)

    def w_end(j, c):
        part = y if j == 0 else opp
        return remote(wq_at(part, c), w_at(outer, part, c), we_s.at[j, c], we_r.at[j, c], to_inner)

    def w_mid_send(s, c):
        if s == 0:
            return remote(wq_at(y, c), w_at(inner, y, c), wm_s.at[s, c], wm_r.at[s, c], to_far)
        return remote(w_at(outer, y, c), w_at(outer, y, c), wm_s.at[s, c], wm_r.at[s, c], to_far)

    def far_shard(s):
        return jnp.where(s == 0, far_inner, far_outer)

    def w_mid_recv(s, c):
        ref = w_at(far_shard(s), y, c)
        return remote(ref, ref, wm_s.at[s, c], wm_r.at[s, c], to_far)

    def y_shard(s):
        return jnp.where(s == 2, outer, far_shard(s))

    def w_y(s, c, part):
        ref = w_at(y_shard(s), part, c)
        return remote(ref, ref, wy_s.at[s, c], wy_r.at[s, c], to_y)

    def o_end(j, c):
        part = y if j == 0 else opp
        return remote(wo_at(part, c), o_at(outer, part, c), oe_s.at[j, c], oe_r.at[j, c], to_inner)

    def o_mid_send(s, c):
        if s == 0:
            return remote(wo_at(y, c), o_at(inner, y, c), om_s.at[s, c], om_r.at[s, c], to_far)
        return remote(o_at(outer, y, c), o_at(outer, y, c), om_s.at[s, c], om_r.at[s, c], to_far)

    def o_mid_recv(s, c):
        ref = o_at(far_shard(s), y, c)
        return remote(ref, ref, om_s.at[s, c], om_r.at[s, c], to_far)

    def o_y(s, c, part):
        ref = o_at(far_shard(s), part, c)
        return remote(ref, ref, oy_s.at[s, c], oy_r.at[s, c], to_y)

    def att_at(row_n, g, b):
        return att.at[row_n, g, pl.ds(pl.multiple_of(b * SHIFT, SHIFT), SHIFT)]

    def att_x(g, b, row_n):
        ref = att_at(row_n, g, b)
        return remote(ref, ref, ax_s.at[g, b], ax_r.at[g, b], to_x)

    def att_core(j, g, b, row_n):
        ref = att_at(row_n, g, b)
        return remote(ref, ref, ac_s.at[j, g, b], ac_r.at[j, g, b], to_core)

    shards = (inner, far_inner, outer, far_outer)
    slots = ((0, 0, wo_cols), (1, 0, wo_cols)) + tuple((s, k * wo_lanes, wo_lanes) for s in (2, 3) for k in range(2))

    def res_cols(slot, row_n):
        order, lane, size = slots[slot]
        return pl.ds(pl.multiple_of(shards[order] * cols + row_n * wo_cols + lane, size), size)

    def result(slot, pos, to_n):
        order, lane, size = slots[slot]
        return remote(
            stage.at[order, pl.ds(pl.multiple_of(pos * tok + to_n * quarter, quarter), quarter), lane : lane + size],
            out_ref.at[:, res_cols(slot, spot)],
            res_s.at[slot, pos, to_n], res_r.at[slot, spot],
            {"wide": side * (n // 2) + pos, "narrow": to_n},
        )

    def result_arrival(slot, from_n):
        ref = out_ref.at[:, res_cols(slot, from_n)]
        return remote(ref, ref, res_s.at[slot, 0, 0], res_r.at[slot, from_n], to_core)

    def kv_copy(g):
        return remote(
            kv_buf.at[pl.ds(2 * g, 2), :, pl.ds(span, SHIFT)], kv_buf.at[pl.ds(2 * g, 2), :, pl.ds(0, SHIFT)],
            kv_sem.at[0, g], kv_sem.at[1, g], to_far,
        )

    barrier = pltpu.get_barrier_semaphore()

    @pl.when(is_outer)
    def _():
        for p in range(narrow):
            pl.semaphore_signal(barrier, inc=1, device_id={"wide": inner, "narrow": p}, device_id_type=MESH)
        pl.semaphore_wait(barrier, narrow)

        @pl.loop(0, n)
        def _(k):
            h_end(k).start()

        def each_end(act):
            @pl.loop(0, chunks)
            def _(c):
                act(w_end(0, c))

            @pl.loop(0, direct)
            def _(c):
                act(w_end(1, c))

            @pl.loop(row_chunks, chunks)
            def _(c):
                act(w_end(1, c))

            for lane_half in range(2):
                for j in range(2):
                    for c in range(2 * lane_half, 2 * lane_half + 2):
                        act(o_end(j, c))

        each_end(lambda copy: copy.start())

        @pl.loop(0, n)
        def _(k):
            h_end(k).wait_send()

        each_end(lambda copy: copy.wait_send())
        for slot in range(len(slots)):
            for p in range(narrow):
                result_arrival(slot, p).wait_recv()

    @pl.when(is_inner)
    def _():
        own = [
            pltpu.make_async_copy(
                wq_ref.at[:, :, pl.ds(h * HEAD_DIM, HEAD_DIM)],
                wbuf.at[h, :, pl.ds(pl.multiple_of(inner * depth, depth), depth)],
                own_sem.at[h],
            )
            for h in range(heads)
        ]
        own.append(pltpu.make_async_copy(hidden_ref, hid.at[pl.ds(own_row, tok)], own_sem.at[heads]))
        own += [
            pltpu.make_async_copy(
                wo_ref.at[pl.ds(h * wo_half, wo_half), pl.ds(pl.multiple_of(spot * wo_cols, wo_cols), wo_cols)],
                wo_buf.at[inner, h],
                own_sem.at[heads + 1 + h],
            )
            for h in range(2)
        ]
        for copy in own:
            copy.start()
        peers = [{"narrow": core_n}, {"narrow": x_n}, {"narrow": diag_n}, to_y, to_far]
        peers += [{"wide": outer, "narrow": p} for p in range(narrow)]
        for device in peers:
            pl.semaphore_signal(barrier, inc=1, device_id=device, device_id_type=MESH)
        pl.semaphore_wait(barrier, len(peers))

        @pl.loop(0, chunks)
        def _(c):
            w_mid_send(0, c).start()

        acc[...] = jnp.zeros_like(acc)
        seg_rows = seg_ref.shape[0]
        lanes = seg_ref.shape[1]
        seg_first = side * (span // lanes)
        for k in range(span // lanes):
            line = seg_ref[pl.ds(seg_first + k, 1), :]
            seg_col[k * lanes : (k + 1) * lanes, :] = jnp.broadcast_to(line, (lanes, lanes)).T

        def add(row, size, shard, part, c):
            start = pl.multiple_of(shard * depth + lax.rem(c, row_chunks) * rows, rows)
            head = c // row_chunks * 2 + part
            here = pl.ds(row, size)
            piece = hid[here, pl.ds(start, rows)]
            both = jnp.concatenate([wbuf[head, i, pl.ds(start, rows)] for i in range(2)], axis=1)
            found = jnp.dot(piece, both, preferred_element_type=jnp.float32)
            acc[head, 0, here] += found[:, :HEAD_DIM]
            acc[head, 1, here] += found[:, HEAD_DIM:]
            acc[head, 2, here] += jnp.dot(piece, wbuf[head, 2, pl.ds(start, rows)], preferred_element_type=jnp.float32)

        def add_all(shard, part, c):
            add(0, span, shard, part, c)

        def add_at(t, shard, part, c):
            @pl.when(t < chunks)
            def _():
                add(own_row, tok, shard, part, c)

            @pl.when(t >= chunks)
            def _():
                add_all(shard, part, c)

        for copy in own[: heads + 1]:
            copy.wait()

        @pl.loop(0, 2 * chunks)
        def _(u):
            add(own_row, tok, inner, u // chunks, lax.rem(u, chunks))

        lag = row_chunks
        lead = chunks - 2
        catch_up = 4 * chunks - lag

        @pl.loop(0, 2 * chunks)
        def _(t):
            s, c = t // chunks, lax.rem(t, chunks)
            q = t - lead

            @pl.when(jnp.logical_and(q >= 0, q < chunks))
            def _():
                w_end(0, q).wait_recv()
                w_mid_send(1, q).start()

            @pl.when(jnp.logical_and(q >= direct, q < row_chunks))
            def _():
                w_y(2, q, y).start()

            w_mid_recv(s, c).wait_recv()
            w_y(s, c, y).start()

            @pl.when(jnp.logical_and(t >= 1, t < 1 + n))
            def _():
                h_end(t - 1).wait_recv()
                h_x(t - 1, spot).start()
                h_core(0, t - 1, spot).start()

            @pl.when(jnp.logical_and(t >= 4, t < 4 + n))
            def _():
                h_x(t - 4, x_n).wait_recv()
                h_core(1, t - 4, x_n).start()

            @pl.when(t == chunks)
            def _():
                @pl.loop(0, n)
                def _(k):
                    h_core(0, k, core_n).wait_recv()
                    h_core(1, k, diag_n).wait_recv()

            add_at(t, far_shard(s), y, c)

            @pl.when(t >= lag)
            def _():
                v = t - lag
                w_y(v // chunks, lax.rem(v, chunks), opp).wait_recv()
                add_at(t, far_shard(v // chunks), opp, lax.rem(v, chunks))

            @pl.when(t >= chunks)
            def _():
                add_all(outer, y, t - chunks)
                u0 = 4 * (t - chunks)

                @pl.loop(u0, jnp.minimum(u0 + 4, catch_up))
                def _(u):
                    turn = u // row_chunks
                    near = lax.rem(turn, 4) < 2
                    part = jnp.where(near, lax.rem(turn, 2), jnp.where(lax.rem(turn, 2) == 0, y, opp))
                    c = lax.rem(u, row_chunks) + turn // 4 * row_chunks
                    add(far_row, tok, jnp.where(near, inner, far_inner), part, c)

            @pl.when(t >= chunks + row_chunks)
            def _():
                k = lax.rem(t - chunks - row_chunks + direct, row_chunks)

                @pl.when(k < direct)
                def _():
                    w_end(1, k).wait_recv()

                @pl.when(k >= direct)
                def _():
                    w_y(2, k, opp).wait_recv()

                add_all(outer, opp, k)

        causal = lax.broadcasted_iota(jnp.int32, (SHIFT, 2 * SHIFT), 1) <= (
            lax.broadcasted_iota(jnp.int32, (SHIFT, 2 * SHIFT), 0) + SHIFT
        )
        per_block = SHIFT // lanes

        def seg_line(b):
            at = [lax.rem(seg_first + b * per_block + k + seg_rows, seg_rows) for k in range(per_block)]
            return jnp.concatenate([seg_ref[pl.ds(i, 1), :] for i in at], axis=1)

        def attend(g, b):
            mine, seen = slice(b * SHIFT, (b + 1) * SHIFT), slice(b * SHIFT, (b + 2) * SHIFT)
            seg_q = jnp.concatenate([seg_col[mine, :]] * (2 * per_block), axis=1)
            near, prior = seg_line(b), seg_line(b - 1)
            for k in range(2):
                h = 2 * g + k
                reach = shift_ref[spot * heads + h]
                if b % 2 == 1:
                    reach = 1 - reach
                seg_k = jnp.concatenate([prior * reach + (reach - 1), near], axis=1)
                scores = lax.dot_general(
                    q_buf[h, mine], kv_buf[h, 0, seen], (((1,), (1,)), ((), ())),
                    preferred_element_type=jnp.float32,
                ) * (1.0 / math.sqrt(HEAD_DIM))
                allowed = causal & (seg_q == seg_k)
                scores = jnp.where(allowed, scores, masked_out)
                exponent = jnp.exp(scores - jnp.max(scores, axis=-1, keepdims=True))
                weights = exponent / jnp.sum(exponent, axis=-1, keepdims=True)
                att[spot, g, mine, k * HEAD_DIM : (k + 1) * HEAD_DIM] = jnp.dot(
                    weights.astype(jnp.bfloat16), kv_buf[h, 1, seen], preferred_element_type=jnp.float32
                ).astype(jnp.bfloat16)
            att_x(g, b, spot).start()
            att_core(0, g, b, spot).start()

        def relay(g, b):
            att_x(g, b, x_n).wait_recv()
            att_core(1, g, b, x_n).start()

        def gathered(b):
            for g in range(2):
                att_core(0, g, b, core_n).wait_recv()
                att_core(1, g, b, diag_n).wait_recv()

        def settle(g):
            for h in (2 * g, 2 * g + 1):
                for i in range(2):
                    kv_buf[h, i, SHIFT:] = acc[h, 1 + i].astype(jnp.bfloat16)
            kv_copy(g).start()
            for h in (2 * g, 2 * g + 1):
                q_buf[h] = acc[h, 0].astype(jnp.bfloat16)

        def multiply(slot, b):
            order, lane, size = slots[slot]
            mine = pl.ds(pl.multiple_of(b * SHIFT, SHIFT), SHIFT)
            a_cols = att.shape[3]
            total = None
            for p in range(narrow):
                for g in range(2):
                    start = (p % (narrow // 2) * 2 + g) * a_cols
                    term = jnp.dot(
                        att[p, g, mine],
                        wo_buf[shards[order], p // (narrow // 2), start : start + a_cols, lane : lane + size],
                        preferred_element_type=jnp.float32,
                    )
                    total = term if total is None else total + term
            done = total.astype(jnp.bfloat16)
            stage[order, mine, lane : lane + size] = done
            pos = b // (blocks // 2)
            for k in range(SHIFT // quarter):
                to_n = lax.rem(b, blocks // 2) * (SHIFT // quarter) + k
                here = jnp.logical_and(pos == own_pos, spot == to_n)

                @pl.when(here)
                def _():
                    out_ref[:, res_cols(slot, spot)] = done[k * quarter : (k + 1) * quarter]

                @pl.when(jnp.logical_not(here))
                def _():
                    result(slot, pos, to_n).start()

        def multiply_these(slot, first, count):
            @pl.loop(0, count)
            def _(k):
                multiply(slot, lax.rem(first + k, blocks))

        def near_wo(c):
            o_mid_recv(0, c).wait_recv()
            o_y(0, c, y).start()

        def far_wo(c):
            o_mid_recv(1, c).wait_recv()
            o_y(1, c, y).start()

        def pass_wo(c):
            o_end(0, c).wait_recv()
            o_mid_send(1, c).start()

        def last_y(c):
            w_y(1, c, opp).wait_recv()
            add_all(far_outer, opp, c)

        def last_end(c):
            w_end(1, c).wait_recv()
            add_all(outer, opp, c)

        settle(0)
        for c in range(3):
            o_mid_send(0, c).start()
        attend(0, 1)
        last_y(row_chunks)
        attend(0, 2)
        last_y(row_chunks + 1)
        attend(0, 3)

        @pl.loop(row_chunks, chunks - 2)
        def _(c):
            last_end(c)

        relay(0, 1)
        kv_copy(0).wait_recv()
        attend(0, 0)
        relay(0, 2)
        last_y(row_chunks + 2)
        last_end(chunks - 2)
        relay(0, 3)
        last_end(chunks - 1)
        last_y(row_chunks + 3)
        settle(1)
        o_mid_send(0, 3).start()
        attend(1, 1)
        relay(0, 0)
        near_wo(0)
        near_wo(1)
        attend(1, 2)
        near_wo(2)
        pass_wo(0)
        attend(1, 3)
        pass_wo(1)
        own[heads + 1].wait()
        own[heads + 2].wait()
        relay(1, 1)
        gathered(1)
        multiply(0, 1)
        kv_copy(1).wait_recv()
        attend(1, 0)
        relay(1, 2)
        gathered(2)
        multiply(0, 2)
        near_wo(3)
        for j in range(2):
            o_end(1, j).wait_recv()
        multiply_these(2, 1, 2)
        relay(1, 3)
        gathered(3)
        multiply(0, 3)
        multiply(2, 3)
        pass_wo(2)

        @pl.loop(0, wo_chunks)
        def _(c):
            o_y(0, c, opp).wait_recv()

        multiply_these(1, 1, 3)
        pass_wo(3)
        far_wo(0)
        relay(1, 0)
        gathered(0)
        multiply(0, 0)
        far_wo(1)
        multiply(1, 0)
        multiply(2, 0)
        far_wo(2)
        far_wo(3)
        first = side * (blocks // 2)
        for j in range(2):
            o_y(1, j, opp).wait_recv()
        multiply_these(4, first, blocks)
        for j in range(2):
            o_end(1, 2 + j).wait_recv()
        multiply_these(3, first, blocks)
        for j in range(2):
            o_y(1, 2 + j, opp).wait_recv()
        multiply_these(5, first, blocks)

        for slot in range(len(slots)):
            for p in range(narrow):
                @pl.when(spot != p)
                def _():
                    result_arrival(slot, p).wait_recv()

        @pl.loop(0, n)
        def _(k):
            h_x(k, spot).wait_send()
            h_core(0, k, spot).wait_send()
            h_core(1, k, x_n).wait_send()

        @pl.loop(0, chunks)
        def _(c):
            for s in range(2):
                w_mid_send(s, c).wait_send()
                w_y(s, c, y).wait_send()

        @pl.loop(direct, row_chunks)
        def _(c):
            w_y(2, c, y).wait_send()

        @pl.loop(0, wo_chunks)
        def _(c):
            for s in range(2):
                o_mid_send(s, c).wait_send()
                o_y(s, c, y).wait_send()

        for g in range(2):
            kv_copy(g).wait_send()

            @pl.loop(0, blocks)
            def _(b):
                att_x(g, b, spot).wait_send()
                att_core(0, g, b, spot).wait_send()
                att_core(1, g, b, x_n).wait_send()

        for slot in range(len(slots)):
            for pos in range(2):
                for to_n in range(narrow):
                    @pl.when(jnp.logical_not(jnp.logical_and(pos == own_pos, spot == to_n)))
                    def _():
                        result(slot, pos, to_n).wait_send()


def hub_layer(hidden, wq, wo, seg, shift_heads):
    n, narrow = lax.axis_size("wide"), lax.axis_size("narrow")
    tok, width = hidden.shape
    heads = wq.shape[2] // HEAD_DIM
    row_chunks = wq.shape[1] // HUB_ROWS
    chunks, wo_chunks = 2 * row_chunks, 4
    cols = wo.shape[1]
    wo_half, wo_cols = wo.shape[0] // 2, cols // narrow
    quarter, span = tok // narrow, 2 * tok
    blocks = span // SHIFT
    vmem = pl.BlockSpec(memory_space=pltpu.VMEM)
    smem = pl.BlockSpec(memory_space=pltpu.SMEM)
    hbm = pl.BlockSpec(memory_space=pl.ANY)
    dma = pltpu.SemaphoreType.DMA
    bf16 = jnp.bfloat16
    return pl.pallas_call(
        functools.partial(hub_kernel, row_chunks, DIRECT),
        out_shape=pltpu.VMEM((quarter, n * cols), bf16),
        in_specs=[hbm, hbm, hbm, vmem, smem],
        out_specs=vmem,
        scratch_shapes=[
            pltpu.VMEM((heads, 3, width, HEAD_DIM), bf16),
            pltpu.VMEM((span, width), bf16),
            pltpu.VMEM((heads, 3, span, HEAD_DIM), jnp.float32),
            pltpu.VMEM((heads, span, HEAD_DIM), bf16),
            pltpu.VMEM((heads, 2, span + SHIFT, HEAD_DIM), bf16),
            pltpu.VMEM((narrow, 2, span, 2 * HEAD_DIM), bf16),
            pltpu.VMEM((n, 2, wo_half, wo_cols), bf16),
            pltpu.VMEM((n, span, wo_cols), bf16),
            pltpu.VMEM((span, seg.shape[1]), jnp.int32),
            dma((heads + 3,)),
        ]
        + [dma((n,))] * 4
        + [dma((2, n))] * 2
        + [dma((2, chunks))] * 4
        + [dma((3, chunks))] * 2
        + [dma((2, 2))]
        + [dma((2, wo_chunks))] * 6
        + [dma((2, blocks))] * 2
        + [dma((2, 2, blocks))] * 2
        + [dma((6, 2, narrow)), dma((6, narrow))],
        compiler_params=pltpu.CompilerParams(
            collective_id=0, has_side_effects=True, vmem_limit_bytes=58 * 1024 * 1024
        ),
    )(hidden, wq, wo, seg, shift_heads)


def hub_per_device(hidden, w_qkv, w_out, seg_ids, shift_heads):
    return hub_layer(hidden, w_qkv.transpose(1, 0, 2), w_out, seg_ids.reshape(-1, 128), shift_heads)


def solution(mesh):
    placed = (
        P(("groups", "wide"), None),
        P("wide", None, "narrow"),
        P(None, "wide"),
        P("groups"),
        P(),
    )
    shape = mesh.shape
    hub = shape["groups"] == 2 and shape["wide"] == 4 and shape["narrow"] == 4
    return jax.shard_map(
        hub_per_device if hub else per_device,
        mesh=mesh,
        in_specs=placed,
        out_specs=P(("groups", "wide", "narrow"), None),
        check_vma=False,
    )
```

```python
import functools
import math

import jax
import jax.numpy as jnp
from jax import lax
from jax.experimental import pallas as pl
from jax.experimental.pallas import tpu as pltpu
from jax.sharding import PartitionSpec as P

HEAD_DIM = 128
GROUP = 512
SHIFT = 256

masked_out = -1e30
MESH = pl.DeviceIdType.MESH
ROWS = 128
WO_CHUNKS = 4
HUB_ROWS = 256
DIRECT = 2


def layer_kernel(
    n, narrow, chunks, wo_chunks,
    hidden_ref, wq_ref, wo_ref, segq_ref, segk_ref, out_ref,
    wbuf, acc, wo_buf, q_buf, kv_buf, att, part, pair_in, pair_sum, far_in,
    own_sem,
    qs_r, qs_l, qr, qs_y, qr_y,
    os_r, os_l, o_r, os_y, or_y,
    kv_sem, pair_s, pair_r, far_s, far_r,
):
    me = lax.axis_index("wide")
    y = lax.axis_index("groups")
    spot = lax.axis_index("narrow")
    other = 1 - y
    across_n = narrow // 2
    high, low = spot // 2, lax.rem(spot, 2)
    depth = wq_ref.shape[1]
    half = wbuf.shape[3]
    tok = hidden_ref.shape[0]
    rows = depth // chunks
    steps = (n - 1) * chunks
    wo_rows = wo_buf.shape[2] // wo_chunks
    cols = wo_buf.shape[3]
    blocks = tok // SHIFT
    per_half = half // HEAD_DIM
    has_left, has_right = me > 0, me < n - 1
    right, left = {"wide": me + 1}, {"wide": me - 1}
    after, before = {"wide": lax.rem(me + 1, n)}, {"wide": lax.rem(me + n - 1, n)}
    opposite = {"groups": other}
    pair = {"narrow": high * 2 + 1 - low}
    far = [{"narrow": lax.rem(high + d, across_n) * 2 + low} for d in range(1, across_n)]
    far_from = [{"narrow": lax.rem(high + across_n - d, across_n) * 2 + low} for d in range(1, across_n)]

    barrier = pltpu.get_barrier_semaphore()
    greeted = [after, before, opposite, pair] + far
    for device in greeted:
        pl.semaphore_signal(barrier, inc=1, device_id=device, device_id_type=MESH)

    def w_at(shard, part_of, c):
        start = pl.multiple_of(shard * depth + c * rows, rows)
        return wbuf.at[part_of, :, pl.ds(start, rows)]

    def wq_own(c):
        return wq_ref.at[
            :, pl.ds(pl.multiple_of(c * rows, rows), rows), pl.ds(pl.multiple_of(y * half, half), half)
        ]

    def o_at(shard, part_of, c):
        return wo_buf.at[shard, part_of, pl.ds(pl.multiple_of(c * wo_rows, wo_rows), wo_rows)]

    def wo_own(c):
        return wo_ref.at[spot, y, pl.ds(pl.multiple_of(c * wo_rows, wo_rows), wo_rows)]

    def remote(src, dst, send, recv, device):
        return pltpu.make_async_remote_copy(
            src_ref=src, dst_ref=dst, send_sem=send, recv_sem=recv,
            device_id=device, device_id_type=MESH,
        )

    def q_right(shard, c, src=None):
        dst = w_at(shard, y, c)
        return remote(dst if src is None else src, dst, qs_r.at[shard, c], qr.at[shard, c], right)

    def q_left(shard, c, src=None):
        dst = w_at(shard, y, c)
        return remote(dst if src is None else src, dst, qs_l.at[shard, c], qr.at[shard, c], left)

    def q_across(shard, c, part_of):
        ref = w_at(shard, part_of, c)
        return remote(ref, ref, qs_y.at[shard, c], qr_y.at[shard, c], opposite)

    def o_right(shard, c, src=None):
        dst = o_at(shard, y, c)
        return remote(dst if src is None else src, dst, os_r.at[shard, c], o_r.at[shard, c], right)

    def o_left(shard, c, src=None):
        dst = o_at(shard, y, c)
        return remote(dst if src is None else src, dst, os_l.at[shard, c], o_r.at[shard, c], left)

    def o_across(shard, c, part_of):
        ref = o_at(shard, part_of, c)
        return remote(ref, ref, os_y.at[shard, c], or_y.at[shard, c], opposite)

    own = [
        pltpu.make_async_copy(
            wq_ref.at[:, :, pl.ds(h * half, half)],
            wbuf.at[h, :, pl.ds(pl.multiple_of(me * depth, depth), depth)],
            own_sem.at[h],
        )
        for h in range(2)
    ]
    own.append(pltpu.make_async_copy(wo_ref.at[spot], wo_buf.at[me], own_sem.at[2]))
    for copy in own:
        copy.start()
    pl.semaphore_wait(barrier, len(greeted))

    @pl.loop(0, chunks)
    def _(c):
        @pl.when(has_right)
        def _():
            q_right(me, c, wq_own(c)).start()

        @pl.when(has_left)
        def _():
            q_left(me, c, wq_own(c)).start()

    acc[...] = jnp.zeros_like(acc)
    own[0].wait()
    own[1].wait()

    def add(shard, part_of, c):
        start = pl.multiple_of(shard * depth + c * rows, rows)
        piece = hidden_ref[:, pl.ds(start, rows)]
        for i in range(3):
            acc[part_of, i] += jnp.dot(
                piece, wbuf[part_of, i, pl.ds(start, rows)], preferred_element_type=jnp.float32
            )

    @pl.loop(0, 2 * chunks)
    def _(i):
        add(me, i // chunks, lax.rem(i, chunks))

    def add_across(t):
        s, c = t // chunks, lax.rem(t, chunks)
        for there, shard in ((me - 1 - s >= 0, me - 1 - s), (me + 1 + s <= n - 1, me + 1 + s)):
            @pl.when(there)
            def _():
                q_across(shard, c, other).wait_recv()
                add(shard, other, c)

    def send_own_wo():
        @pl.loop(0, wo_chunks)
        def _(c):
            @pl.when(has_right)
            def _():
                o_right(me, c, wo_own(c)).start()

            @pl.when(has_left)
            def _():
                o_left(me, c, wo_own(c)).start()

    @pl.loop(0, steps)
    def _(t):
        s, c = t // chunks, lax.rem(t, chunks)

        @pl.when(t == steps - chunks)
        def _():
            send_own_wo()

        @pl.when(me - 1 - s >= 0)
        def _():
            q_right(me - 1 - s, c).wait_recv()

            @pl.when(has_right)
            def _():
                q_right(me - 1 - s, c).start()

            q_across(me - 1 - s, c, y).start()

        @pl.when(me + 1 + s <= n - 1)
        def _():
            q_left(me + 1 + s, c).wait_recv()

            @pl.when(has_left)
            def _():
                q_left(me + 1 + s, c).start()

            q_across(me + 1 + s, c, y).start()

        for there, shard in ((me - 1 - s >= 0, me - 1 - s), (me + 1 + s <= n - 1, me + 1 + s)):
            @pl.when(there)
            def _():
                add(shard, y, c)

        @pl.when(t > 0)
        def _():
            add_across(t - 1)

    add_across(steps - 1)
    for h in range(2):
        q_buf[h] = acc[h, 0].astype(jnp.bfloat16)
        for i in range(2):
            kv_buf[h, i, SHIFT:] = acc[h, 1 + i].astype(jnp.bfloat16)

    kv_copy = remote(
        kv_buf.at[:, :, pl.ds(tok, SHIFT)], kv_buf.at[:, :, pl.ds(0, SHIFT)],
        kv_sem.at[0], kv_sem.at[1], after,
    )
    kv_copy.start()

    causal = lax.broadcasted_iota(jnp.int32, (SHIFT, 2 * SHIFT), 1) <= (
        lax.broadcasted_iota(jnp.int32, (SHIFT, 2 * SHIFT), 0) + SHIFT
    )

    def attend(h, b):
        lanes = slice((h % per_half) * HEAD_DIM, (h % per_half + 1) * HEAD_DIM)
        mine, seen = slice(b * SHIFT, (b + 1) * SHIFT), slice(b * SHIFT, (b + 2) * SHIFT)
        keys, values = kv_buf.at[h // per_half, 0], kv_buf.at[h // per_half, 1]
        scores = lax.dot_general(
            q_buf[h // per_half, mine, lanes], keys[seen, lanes], (((1,), (1,)), ((), ())),
            preferred_element_type=jnp.float32,
        ) * (1.0 / math.sqrt(HEAD_DIM))
        allowed = causal & (segq_ref[mine, :] == segk_ref[h, b])
        scores = jnp.where(allowed, scores, masked_out)
        exponent = jnp.exp(scores - jnp.max(scores, axis=-1, keepdims=True))
        weights = exponent / jnp.sum(exponent, axis=-1, keepdims=True)
        att[mine, h * HEAD_DIM : (h + 1) * HEAD_DIM] = jnp.dot(
            weights.astype(jnp.bfloat16), values[seen, lanes], preferred_element_type=jnp.float32
        ).astype(jnp.bfloat16)

    least = jnp.minimum(me, n - 1 - me)

    def block_of(k):
        turn = (k + 1) // 2
        near = jnp.where(lax.rem(k, 2) == 1, me - turn, me + turn)
        rest = jnp.where(me > least, me - (k - least), me + (k - least))
        return jnp.where(k <= 2 * least, near, rest)

    def pass_on(k):
        shard = block_of(k)

        @pl.loop(0, wo_chunks)
        def _(c):
            o_right(shard, c).wait_recv()

            @pl.when(jnp.logical_and(shard < me, has_right))
            def _():
                o_right(shard, c).start()

            @pl.when(jnp.logical_and(shard > me, has_left))
            def _():
                o_left(shard, c).start()

            o_across(shard, c, y).start()

    def pair_copy(shard, a):
        return remote(
            part.at[shard, a * 2 + 1 - low], pair_in.at[shard, a],
            pair_s.at[shard, a], pair_r.at[shard, a], pair,
        )

    def far_copy(shard, d):
        a = lax.rem(high + d, across_n)
        return remote(
            pair_sum.at[shard, a], far_in.at[shard, d - 1],
            far_s.at[shard, d - 1], far_r.at[shard, d - 1], far[d - 1],
        )

    def far_arrival(shard, d):
        return remote(
            pair_sum.at[shard, high], far_in.at[shard, d - 1],
            far_s.at[shard, d - 1], far_r.at[shard, d - 1], far_from[d - 1],
        )

    def multiply(k):
        shard = block_of(k)
        width = att.shape[1] // 2
        share = tok // narrow
        for p in range(narrow):
            a_rows = att[p * share : (p + 1) * share, :]
            total = jnp.dot(a_rows[:, :width], wo_buf[shard, 0], preferred_element_type=jnp.float32)
            total += jnp.dot(a_rows[:, width:], wo_buf[shard, 1], preferred_element_type=jnp.float32)
            part[shard, p] = total.astype(jnp.bfloat16)
        for a in range(across_n):
            pair_copy(shard, a).start()

    def sum_pair(k):
        shard = block_of(k)
        for a in range(across_n):
            pair_copy(shard, a).wait_recv()
            total = part[shard, a * 2 + low].astype(jnp.float32) + pair_in[shard, a].astype(jnp.float32)
            pair_sum[shard, a] = total.astype(jnp.bfloat16)
        for d in range(1, across_n):
            far_copy(shard, d).start()

    def finish(k):
        shard = block_of(k)
        total = part[shard, high * 2 + low].astype(jnp.float32) + pair_in[shard, high].astype(jnp.float32)
        for d in range(1, across_n):
            far_arrival(shard, d).wait_recv()
            total += far_in[shard, d - 1].astype(jnp.float32)
        out_ref[:, pl.ds(pl.multiple_of(shard * cols, cols), cols)] = total.astype(out_ref.dtype)

    heads = 2 * per_half
    for b in range(1, blocks):
        for h in range(heads):
            attend(h, b)
    pass_on(1)
    pass_on(2)
    kv_copy.wait_recv()
    for h in range(heads):
        attend(h, 0)
    own[2].wait()
    multiply(0)

    @pl.loop(1, n)
    def _(k):
        @pl.when(k > 2)
        def _():
            pass_on(k)

        sum_pair(k - 1)

        @pl.when(k > 1)
        def _():
            finish(k - 2)

        shard = block_of(k)

        @pl.loop(0, wo_chunks)
        def _(c):
            o_across(shard, c, other).wait_recv()

        multiply(k)

    sum_pair(n - 1)
    finish(n - 2)
    finish(n - 1)

    kv_copy.wait_send()

    @pl.loop(0, n)
    def _(shard):
        for a in range(across_n):
            pair_copy(shard, a).wait_send()
        for d in range(1, across_n):
            far_copy(shard, d).wait_send()
        goes_right = jnp.logical_and(shard <= me, has_right)
        goes_left = jnp.logical_and(shard >= me, has_left)
        for count, to_right, to_left, to_other in (
            (chunks, q_right, q_left, q_across), (wo_chunks, o_right, o_left, o_across)
        ):
            @pl.loop(0, count)
            def _(c):
                @pl.when(goes_right)
                def _():
                    to_right(shard, c).wait_send()

                @pl.when(goes_left)
                def _():
                    to_left(shard, c).wait_send()

                @pl.when(shard != me)
                def _():
                    to_other(shard, c, y).wait_send()


def layer(hidden, wq, wo, seg_q, seg_k):
    n, narrow = lax.axis_size("wide"), lax.axis_size("narrow")
    tok, width = hidden.shape
    half = wq.shape[2] // 2
    chunks = max(1, wq.shape[1] // ROWS)
    wo_chunks = WO_CHUNKS
    cols = wo.shape[3]
    share = tok // narrow
    vmem = pl.BlockSpec(memory_space=pltpu.VMEM)
    hbm = pl.BlockSpec(memory_space=pl.ANY)
    dma = pltpu.SemaphoreType.DMA
    bf16 = jnp.bfloat16
    return pl.pallas_call(
        functools.partial(layer_kernel, n, narrow, chunks, wo_chunks),
        out_shape=jax.ShapeDtypeStruct((share, n * cols), bf16),
        in_specs=[vmem, hbm, hbm, vmem, vmem],
        out_specs=vmem,
        scratch_shapes=[
            pltpu.VMEM((2, 3, width, half), bf16),
            pltpu.VMEM((2, 3, tok, half), jnp.float32),
            pltpu.VMEM((n,) + wo.shape[1:], bf16),
            pltpu.VMEM((2, tok, half), bf16),
            pltpu.VMEM((2, 2, tok + SHIFT, half), bf16),
            pltpu.VMEM((tok, 2 * half), bf16),
            pltpu.VMEM((n, narrow, share, cols), bf16),
            pltpu.VMEM((n, narrow // 2, share, cols), bf16),
            pltpu.VMEM((n, narrow // 2, share, cols), bf16),
            pltpu.VMEM((n, max(1, narrow // 2 - 1), share, cols), bf16),
            dma((3,)),
        ]
        + [dma((n, chunks))] * 5
        + [dma((n, wo_chunks))] * 5
        + [dma((2,))]
        + [dma((n, narrow // 2))] * 2
        + [dma((n, max(1, narrow // 2 - 1)))] * 2,
        compiler_params=pltpu.CompilerParams(
            collective_id=0, has_side_effects=True, vmem_limit_bytes=58 * 1024 * 1024
        ),
    )(hidden, wq, wo, seg_q, seg_k)


def per_device(hidden, w_qkv, w_out, seg_ids, shift_heads):
    tok_rows = hidden.shape[0]
    local_f = w_qkv.shape[2]
    heads_here = local_f // HEAD_DIM
    blocks = tok_rows // SHIFT
    narrow = lax.axis_size("narrow")
    first_tok = lax.axis_index("wide") * tok_rows
    shifted = lax.dynamic_slice_in_dim(shift_heads, lax.axis_index("narrow") * heads_here, heads_here) > 0

    doubled = jnp.concatenate([seg_ids[-SHIFT:], seg_ids], 0)
    seg_here = lax.dynamic_slice_in_dim(doubled, first_tok, tok_rows + SHIFT)
    seg_q = seg_here[SHIFT:, None]
    windows = jnp.stack([seg_here[b * SHIFT : (b + 2) * SHIFT] for b in range(blocks)])
    odd = (jnp.arange(blocks) % 2 == 1)[None, :, None]
    reaches = (shifted[:, None, None] != odd) | (jnp.arange(2 * SHIFT) >= SHIFT)[None, None, :]
    seg_k = jnp.where(reaches, windows[None], -1)[:, :, None, :]

    wq = w_qkv.transpose(1, 0, 2)
    wo = w_out.reshape(narrow, 2, local_f // 2, -1)
    return layer(hidden, wq, wo, seg_q, seg_k)


def hub_kernel(
    row_chunks, direct,
    hidden_ref, wq_ref, wo_ref, seg_ref, shift_ref, out_ref,
    wbuf, hid, acc, q_buf, kv_buf, att, wo_buf, stage, seg_col,
    own_sem, sends, joint, he_r, hx_r, wm_r, we_r, wy_r, w0_r, kv_r, om_r, oe_r, od_r, ax_r, ae_r,
):
    n, narrow = lax.axis_size("wide"), lax.axis_size("narrow")
    me = lax.axis_index("wide")
    y = lax.axis_index("groups")
    spot = lax.axis_index("narrow")
    opp = 1 - y
    side = me // (n // 2)
    inner, outer = n // 2 - 1 + side, side * (n - 1)
    far_inner, far_outer = n - 1 - inner, n - 1 - outer
    is_inner, is_outer = me == inner, me == outer
    high, low = spot // 2, lax.rem(spot, 2)
    core_n, x_n = high * 2 + 1 - low, (1 - high) * 2 + low
    diag_n = (1 - high) * 2 + 1 - low
    depth = wq_ref.shape[1]
    tok = hidden_ref.shape[0]
    heads = wbuf.shape[0]
    chunks = 2 * row_chunks
    rows = depth // row_chunks
    wo_chunks = 8
    sub = wo_chunks // 4
    quarter = tok // narrow
    span = 2 * tok
    blocks = span // SHIFT
    own_pos = 1 - side
    own_row = pl.multiple_of(own_pos * tok, tok)
    far_row = pl.multiple_of(side * tok, tok)
    wo_half, wo_cols = wo_buf.shape[2], wo_buf.shape[3]
    wo_rows, wo_lanes = wo_half // (2 * sub), wo_cols // 2
    cols = wo_ref.shape[1]
    to_core, to_x, to_y = {"narrow": core_n}, {"narrow": x_n}, {"groups": opp}
    to_far, to_inner, to_outer = {"wide": far_inner}, {"wide": inner}, {"wide": outer}
    my_pos = jnp.where(is_inner, own_pos, side)

    def remote(src, dst, send, recv, device):
        return pltpu.make_async_remote_copy(
            src_ref=src, dst_ref=dst, send_sem=send, recv_sem=recv,
            device_id=device, device_id_type=MESH,
        )

    def arrived(place, ref):
        remote(ref, ref, sends.at[0], joint.at[place], to_core).wait_recv()

    def sent(place, ref):
        remote(ref, ref, sends.at[place], joint.at[0], to_core).wait_send()

    def w_at(shard, part, c):
        start = pl.multiple_of(shard * depth + lax.rem(c, row_chunks) * rows, rows)
        return wbuf.at[c // row_chunks * 2 + part, :, pl.ds(start, rows)]

    def wq_at(part, c):
        start = pl.multiple_of(lax.rem(c, row_chunks) * rows, rows)
        lane = pl.multiple_of((c // row_chunks * 2 + part) * HEAD_DIM, HEAD_DIM)
        return wq_ref.at[:, pl.ds(start, rows), pl.ds(lane, HEAD_DIM)]

    def o_at(shard, part, c):
        start = pl.multiple_of(lax.rem(c, 2 * sub) * wo_rows, wo_rows)
        lane = pl.multiple_of(c // (2 * sub) * wo_lanes, wo_lanes)
        return wo_buf.at[shard, part, pl.ds(start, wo_rows), pl.ds(lane, wo_lanes)]

    def wo_at(part, c):
        start = pl.multiple_of(part * wo_half + lax.rem(c, 2 * sub) * wo_rows, wo_rows)
        lane = pl.multiple_of(spot * wo_cols + c // (2 * sub) * wo_lanes, wo_lanes)
        return wo_ref.at[pl.ds(start, wo_rows), pl.ds(lane, wo_lanes)]

    def h_at(row_n, k):
        start = pl.multiple_of(far_row + row_n * quarter, quarter)
        return hid.at[pl.ds(start, quarter), pl.ds(pl.multiple_of(k * depth, depth), depth)]

    def h_end(k):
        src = hidden_ref.at[
            pl.ds(pl.multiple_of(spot * quarter, quarter), quarter), pl.ds(pl.multiple_of(k * depth, depth), depth)
        ]
        return remote(src, h_at(spot, k), sends.at[0], he_r.at[k], to_inner)

    def h_x(k, row_n):
        return remote(h_at(row_n, k), h_at(row_n, k), sends.at[0], hx_r.at[k], to_x)

    def h_core(k, row_n):
        return remote(h_at(row_n, k), h_at(row_n, k), sends.at[0], joint.at[0], to_core)

    def w_end(j, c):
        part = y if j == 0 else opp
        return remote(wq_at(part, c), w_at(outer, part, c), sends.at[1], we_r.at[j, c], to_inner)

    def w_mid_send(s, c):
        if s == 0:
            return remote(wq_at(y, c), w_at(inner, y, c), sends.at[1], wm_r.at[s, c], to_far)
        return remote(w_at(outer, y, c), w_at(outer, y, c), sends.at[1], wm_r.at[s, c], to_far)

    def far_shard(s):
        return jnp.where(s == 0, far_inner, far_outer)

    def w_mid_recv(s, c):
        ref = w_at(far_shard(s), y, c)
        return remote(ref, ref, sends.at[1], wm_r.at[s, c], to_far)

    def w_y(s, c, part):
        ref = w_at(far_shard(s), part, c)
        return remote(ref, ref, sends.at[1], wy_r.at[s, c], to_y)

    def w_y_outer(c, part):
        ref = w_at(outer, part, c)
        return remote(ref, ref, sends.at[2], w0_r.at[c], to_y)

    def o_end(j, c):
        part = y if j == 0 else opp
        return remote(wo_at(part, c), o_at(outer, part, c), sends.at[4], oe_r.at[c] if j == 0 else joint.at[4 + c // (2 * sub)], to_inner)

    def o_mid_send(s, c):
        if s == 0:
            return remote(wo_at(y, c), o_at(inner, y, c), sends.at[4], om_r.at[s, c], to_far)
        return remote(o_at(outer, y, c), o_at(outer, y, c), sends.at[4], om_r.at[s, c], to_far)

    def o_mid_recv(s, c):
        ref = o_at(far_shard(s), y, c)
        return remote(ref, ref, sends.at[4], om_r.at[s, c], to_far)

    def o_down(c):
        return remote(wo_at(y, c), o_at(inner, y, c), sends.at[5], od_r.at[c], to_outer)

    def o_y(s, c, part):
        ref = o_at(inner if s == 2 else far_shard(s), part, c)
        place = (1, 2 + c // (2 * sub), 6)[s]
        return remote(ref, ref, sends.at[5 if s == 2 else 4], joint.at[place], to_y)

    def att_at(row_n, g, b):
        return att.at[row_n, g, pl.ds(pl.multiple_of(b * SHIFT, SHIFT), SHIFT)]

    def att_x(g, b, row_n):
        ref = att_at(row_n, g, b)
        return remote(ref, ref, sends.at[6], ax_r.at[g, b], to_x)

    def att_core(g, b, row_n):
        ref = att_at(row_n, g, b)
        return remote(ref, ref, sends.at[6], joint.at[8 + b], to_core)

    def att_end(g, b):
        ref = att_at(spot, g, b)
        return remote(ref, ref, sends.at[7], ae_r.at[g, b], to_outer)

    def share(g, b):
        att_x(g, b, spot).start()
        att_core(g, b, spot).start()

    def relay(g, b):
        att_x(g, b, x_n).wait_recv()
        att_core(g, b, x_n).start()

    def gathered(b):
        arrived(8 + b, att.at[pl.ds(0, narrow // 2), :, pl.ds(pl.multiple_of(b * SHIFT, SHIFT), SHIFT)])

    shards = (inner, far_inner, outer, far_outer)
    slots = ((0, 0, wo_cols), (1, 0, wo_cols)) + tuple((s, k * wo_lanes, wo_lanes) for s in (2, 3) for k in range(2))
    slots += ((2, 0, wo_cols),)

    def res_cols(slot, row_n):
        order, lane, size = slots[slot]
        return pl.ds(pl.multiple_of(shards[order] * cols + row_n * wo_cols + lane, size), size)

    def result(slot, pos, to_n):
        order, lane, size = slots[slot]
        return remote(
            stage.at[order, pl.ds(pl.multiple_of(pos * tok + to_n * quarter, quarter), quarter), lane : lane + size],
            out_ref.at[:, res_cols(slot, spot)],
            sends.at[8], joint.at[7],
            {"wide": side * (n // 2) + pos, "narrow": to_n},
        )

    def multiply(slot, b):
        order, lane, size = slots[slot]
        mine = pl.ds(pl.multiple_of(b * SHIFT, SHIFT), SHIFT)
        a_cols = att.shape[3]
        total = None
        for p in range(narrow):
            for g in range(2):
                start = (p % (narrow // 2) * 2 + g) * a_cols
                term = jnp.dot(
                    att[p, g, mine],
                    wo_buf[shards[order], p // (narrow // 2), start : start + a_cols, lane : lane + size],
                    preferred_element_type=jnp.float32,
                )
                total = term if total is None else total + term
        done = total.astype(jnp.bfloat16)
        stage[order, mine, lane : lane + size] = done
        pos = b // (blocks // 2)
        for k in range(SHIFT // quarter):
            to_n = lax.rem(b, blocks // 2) * (SHIFT // quarter) + k
            here = jnp.logical_and(pos == my_pos, spot == to_n)

            @pl.when(here)
            def _():
                out_ref[:, res_cols(slot, spot)] = done[k * quarter : (k + 1) * quarter]

            @pl.when(jnp.logical_not(here))
            def _():
                result(slot, pos, to_n).start()

    def kv_copy(g):
        return remote(
            kv_buf.at[pl.ds(2 * g, 2), :, pl.ds(span, SHIFT)], kv_buf.at[pl.ds(2 * g, 2), :, pl.ds(0, SHIFT)],
            sends.at[3], kv_r.at[g], to_far,
        )

    barrier = pltpu.get_barrier_semaphore()
    beside = [{"narrow": core_n}, {"narrow": x_n}, {"narrow": diag_n}, to_y]

    def greet(peers):
        for device in peers:
            pl.semaphore_signal(barrier, inc=1, device_id=device, device_id_type=MESH)
        pl.semaphore_wait(barrier, len(peers))

    def own_wo(h):
        return pltpu.make_async_copy(
            wo_ref.at[pl.ds(h * wo_half, wo_half), pl.ds(pl.multiple_of(spot * wo_cols, wo_cols), wo_cols)],
            wo_buf.at[me, h],
            own_sem.at[2 + h],
        )


    @pl.when(is_outer)
    def _():
        greet(beside + [{"wide": inner, "narrow": p} for p in range(narrow)])

        @pl.loop(0, n)
        def _(k):
            h_end(k).start()

        def each_end(act):
            @pl.loop(0, chunks)
            def _(c):
                act(w_end(0, c))

            @pl.loop(0, direct)
            def _(c):
                act(w_end(1, c))

            @pl.loop(row_chunks, chunks)
            def _(c):
                act(w_end(1, c))

            for lane_half in range(2):
                for j in range(2):
                    @pl.loop(lane_half * 2 * sub, (lane_half + 1) * 2 * sub)
                    def _(c):
                        act(o_end(j, c))

        each_end(lambda copy: copy.start())
        for h in range(2):
            own_wo(h).start()

        @pl.loop(0, wo_chunks)
        def _(c):
            o_down(c).wait_recv()
            o_y(2, c, y).start()

        arrived(6, wo_buf.at[inner, opp])
        for h in range(2):
            own_wo(h).wait()

        def take(g, b):
            att_end(g, b).wait_recv()
            share(g, b)

        first_b, second_b = side + 1, 3 * side
        take(0, first_b)
        relay(0, first_b)
        take(0, second_b)
        relay(0, second_b)
        take(1, first_b)

        @pl.when(side == 1)
        def _():
            take(1, second_b)

        relay(1, first_b)

        @pl.when(side == 0)
        def _():
            take(1, second_b)

        gathered(first_b)
        multiply(0, first_b)
        multiply(6, first_b)
        relay(1, second_b)
        gathered(second_b)
        multiply(0, second_b)
        multiply(6, second_b)

        sent(0, hid.at[pl.ds(0, quarter)])
        sent(1, wbuf.at[0, :, pl.ds(0, (chunks + direct + row_chunks) * rows)])
        sent(4, wo_buf.at[0])
        sent(5, wo_buf.at[0, 0])
        sent(6, att.at[pl.ds(0, 3), 0])
        sent(8, stage.at[0, pl.ds(0, 2 * (narrow - 1) * quarter)])
        arrived(7, out_ref.at[:, pl.ds(0, (4 * narrow - 2) * wo_cols)])

    @pl.when(is_inner)
    def _():
        own = [
            pltpu.make_async_copy(
                wq_ref.at[:, :, pl.ds(h * HEAD_DIM, HEAD_DIM)],
                wbuf.at[h, :, pl.ds(pl.multiple_of(inner * depth, depth), depth)],
                own_sem.at[0],
            )
            for h in range(heads)
        ]
        own.append(pltpu.make_async_copy(hidden_ref, hid.at[pl.ds(own_row, tok)], own_sem.at[1]))
        for copy in own:
            copy.start()
        for h in range(2):
            own_wo(h).start()
        greet(beside + [to_far] + [{"wide": outer, "narrow": p} for p in range(narrow)])

        @pl.loop(0, chunks)
        def _(c):
            w_mid_send(0, c).start()

        @pl.loop(0, wo_chunks)
        def _(c):
            o_down(c).start()

        acc[...] = jnp.zeros_like(acc)
        seg_rows = seg_ref.shape[0]
        lanes = seg_ref.shape[1]
        seg_first = side * (span // lanes)
        for k in range(span // lanes):
            line = seg_ref[pl.ds(seg_first + k, 1), :]
            seg_col[k * lanes : (k + 1) * lanes, :] = jnp.broadcast_to(line, (lanes, lanes)).T

        def add(row, size, shard, part, c):
            start = pl.multiple_of(shard * depth + lax.rem(c, row_chunks) * rows, rows)
            head = c // row_chunks * 2 + part
            here = pl.ds(row, size)
            piece = hid[here, pl.ds(start, rows)]
            both = jnp.concatenate([wbuf[head, i, pl.ds(start, rows)] for i in range(2)], axis=1)
            found = jnp.dot(piece, both, preferred_element_type=jnp.float32)
            acc[head, 0, here] += found[:, :HEAD_DIM]
            acc[head, 1, here] += found[:, HEAD_DIM:]
            acc[head, 2, here] += jnp.dot(piece, wbuf[head, 2, pl.ds(start, rows)], preferred_element_type=jnp.float32)

        def add_all(shard, part, c):
            add(0, span, shard, part, c)

        def add_at(t, shard, part, c):
            @pl.when(t < chunks)
            def _():
                add(own_row, tok, shard, part, c)

            @pl.when(t >= chunks)
            def _():
                add_all(shard, part, c)

        pltpu.make_async_copy(
            wbuf.at[:, :, pl.ds(0, depth)],
            wbuf.at[:, :, pl.ds(pl.multiple_of(inner * depth, depth), depth)],
            own_sem.at[0],
        ).wait()
        own[heads].wait()

        @pl.loop(0, 2 * chunks)
        def _(u):
            add(own_row, tok, inner, u // chunks, lax.rem(u, chunks))

        lag = row_chunks
        lead = chunks - 2
        catch_up = 4 * chunks - lag

        @pl.loop(0, 2 * chunks)
        def _(t):
            s, c = t // chunks, lax.rem(t, chunks)
            q = t - lead

            @pl.when(jnp.logical_and(q >= 0, q < chunks))
            def _():
                w_end(0, q).wait_recv()
                w_mid_send(1, q).start()

            @pl.when(jnp.logical_and(q >= direct, q < row_chunks))
            def _():
                w_y_outer(q, y).start()

            w_mid_recv(s, c).wait_recv()
            w_y(s, c, y).start()

            @pl.when(jnp.logical_and(t >= 1, t < 1 + n))
            def _():
                h_end(t - 1).wait_recv()
                h_x(t - 1, spot).start()
                h_core(t - 1, spot).start()

            @pl.when(jnp.logical_and(t >= 4, t < 4 + n))
            def _():
                h_x(t - 4, x_n).wait_recv()
                h_core(t - 4, x_n).start()

            @pl.when(t == chunks)
            def _():
                arrived(0, hid.at[pl.ds(far_row, narrow // 2 * quarter)])

            add_at(t, far_shard(s), y, c)

            @pl.when(t >= lag)
            def _():
                v = t - lag
                w_y(v // chunks, lax.rem(v, chunks), opp).wait_recv()
                add_at(t, far_shard(v // chunks), opp, lax.rem(v, chunks))

            @pl.when(t >= chunks)
            def _():
                add_all(outer, y, t - chunks)
                u0 = 4 * (t - chunks)

                @pl.loop(u0, jnp.minimum(u0 + 4, catch_up))
                def _(u):
                    turn = u // row_chunks
                    near = lax.rem(turn, 4) < 2
                    part = jnp.where(near, lax.rem(turn, 2), jnp.where(lax.rem(turn, 2) == 0, y, opp))
                    c = lax.rem(u, row_chunks) + turn // 4 * row_chunks
                    add(far_row, tok, jnp.where(near, inner, far_inner), part, c)

            @pl.when(t >= chunks + row_chunks)
            def _():
                k = lax.rem(t - chunks - row_chunks + direct, row_chunks)

                @pl.when(k < direct)
                def _():
                    w_end(1, k).wait_recv()

                @pl.when(k >= direct)
                def _():
                    w_y_outer(k, opp).wait_recv()

                add_all(outer, opp, k)

        causal = lax.broadcasted_iota(jnp.int32, (SHIFT, 2 * SHIFT), 1) <= (
            lax.broadcasted_iota(jnp.int32, (SHIFT, 2 * SHIFT), 0) + SHIFT
        )
        per_block = SHIFT // lanes

        def seg_line(b):
            at = [lax.rem(seg_first + b * per_block + k + seg_rows, seg_rows) for k in range(per_block)]
            return jnp.concatenate([seg_ref[pl.ds(i, 1), :] for i in at], axis=1)

        def attend(g, b):
            mine, seen = slice(b * SHIFT, (b + 1) * SHIFT), slice(b * SHIFT, (b + 2) * SHIFT)
            seg_q = jnp.concatenate([seg_col[mine, :]] * (2 * per_block), axis=1)
            near, prior = seg_line(b), seg_line(b - 1)
            for k in range(2):
                h = 2 * g + k
                reach = shift_ref[spot * heads + h]
                if b % 2 == 1:
                    reach = 1 - reach
                seg_k = jnp.concatenate([prior * reach + (reach - 1), near], axis=1)
                scores = lax.dot_general(
                    q_buf[h, mine], kv_buf[h, 0, seen], (((1,), (1,)), ((), ())),
                    preferred_element_type=jnp.float32,
                ) * (1.0 / math.sqrt(HEAD_DIM))
                allowed = causal & (seg_q == seg_k)
                scores = jnp.where(allowed, scores, masked_out)
                exponent = jnp.exp(scores - jnp.max(scores, axis=-1, keepdims=True))
                weights = exponent / jnp.sum(exponent, axis=-1, keepdims=True)
                att[spot, g, mine, k * HEAD_DIM : (k + 1) * HEAD_DIM] = jnp.dot(
                    weights.astype(jnp.bfloat16), kv_buf[h, 1, seen], preferred_element_type=jnp.float32
                ).astype(jnp.bfloat16)
            share(g, b)

            @pl.when(b // (blocks // 2) == side)
            def _():
                att_end(g, b).start()

        def settle(g):
            for h in (2 * g, 2 * g + 1):
                for i in range(2):
                    kv_buf[h, i, SHIFT:] = acc[h, 1 + i].astype(jnp.bfloat16)
            kv_copy(g).start()
            for h in (2 * g, 2 * g + 1):
                q_buf[h] = acc[h, 0].astype(jnp.bfloat16)

        def multiply_these(slot, first, count):
            @pl.loop(0, count)
            def _(k):
                multiply(slot, lax.rem(first + k, blocks))

        def multiply_own(slot, b):
            @pl.when(b // (blocks // 2) == own_pos)
            def _():
                multiply(slot, b)

        def relay_wo(arrival, *onward):
            def act(i):
                @pl.loop(i * sub, (i + 1) * sub)
                def _(c):
                    arrival(c).wait_recv()
                    for copy in onward:
                        copy(c).start()

            return act

        near_wo = relay_wo(lambda c: o_mid_recv(0, c), lambda c: o_y(0, c, y))
        far_wo = relay_wo(lambda c: o_mid_recv(1, c), lambda c: o_y(1, c, y))
        pass_wo = relay_wo(lambda c: o_end(0, c), lambda c: o_mid_send(1, c))

        def own_mid(first, last):
            @pl.loop(first * sub, last * sub)
            def _(c):
                o_mid_send(0, c).start()

        def half_of(shard, lane_half):
            return wo_buf.at[shard, opp, :, lane_half * wo_lanes : (lane_half + 1) * wo_lanes]

        def last_y(c):
            w_y(1, c, opp).wait_recv()
            add_all(far_outer, opp, c)

        def last_end(c):
            w_end(1, c).wait_recv()
            add_all(outer, opp, c)

        settle(0)
        own_mid(0, 3)
        attend(0, 1)
        last_y(row_chunks)
        attend(0, 2)
        last_y(row_chunks + 1)
        attend(0, 3)

        @pl.loop(row_chunks, chunks - 2)
        def _(c):
            last_end(c)

        relay(0, 1)
        kv_copy(0).wait_recv()
        attend(0, 0)
        relay(0, 2)
        last_y(row_chunks + 2)
        last_end(chunks - 2)
        relay(0, 3)
        last_end(chunks - 1)
        last_y(row_chunks + 3)
        settle(1)
        own_mid(3, 4)
        attend(1, 1)
        near_wo(0)
        near_wo(1)
        relay(0, 0)
        attend(1, 2)
        near_wo(2)
        pass_wo(0)
        attend(1, 3)
        pass_wo(1)
        for h in range(2):
            own_wo(h).wait()
        relay(1, 1)
        gathered(1)
        multiply_own(0, 1)
        kv_copy(1).wait_recv()
        attend(1, 0)
        near_wo(3)
        relay(1, 2)
        gathered(2)
        multiply_own(0, 2)
        arrived(4, half_of(outer, 0))
        multiply(2, own_pos + 1)
        far_wo(0)
        relay(1, 3)
        pass_wo(2)
        gathered(3)
        multiply_own(0, 3)
        multiply_own(2, 3)
        relay(1, 0)
        far_wo(1)
        pass_wo(3)
        arrived(1, wo_buf.at[far_inner, opp])
        multiply(1, side + 1)
        multiply(1, 3)
        gathered(0)
        multiply(1, 0)
        far_wo(2)
        multiply(1, own_pos + 1)
        multiply_own(0, 0)
        multiply_own(2, 0)
        far_wo(3)
        first = side * (blocks // 2)
        arrived(2, half_of(far_outer, 0))
        multiply_these(4, first, blocks)
        arrived(5, half_of(outer, 1))
        multiply_these(3, own_pos * (blocks // 2), blocks // 2)
        arrived(3, half_of(far_outer, 1))
        multiply_these(5, first, blocks)

        sent(0, hid.at[pl.ds(0, 3 * quarter)])
        sent(1, wbuf.at[pl.ds(0, 2)])
        sent(2, wbuf.at[0, :, pl.ds(0, (row_chunks - direct) * rows)])
        sent(3, kv_buf.at[:, :, pl.ds(0, SHIFT)])
        sent(4, wo_buf.at[pl.ds(0, 2)])
        sent(5, wo_buf.at[0, 0])
        sent(6, att.at[pl.ds(0, 3)])
        sent(7, att.at[0, 0])
        pieces = 4 * (narrow - 1) + 2 * narrow
        sent(8, hid.at[pl.ds(0, pieces * quarter * wo_cols // hid.shape[1])])
        arrived(7, out_ref.at[:, pl.ds(0, 4 * (narrow - 1) * wo_cols)])


def hub_layer(hidden, wq, wo, seg, shift_heads):
    n, narrow = lax.axis_size("wide"), lax.axis_size("narrow")
    tok, width = hidden.shape
    heads = wq.shape[2] // HEAD_DIM
    row_chunks = wq.shape[1] // HUB_ROWS
    chunks, wo_chunks = 2 * row_chunks, 8
    cols = wo.shape[1]
    wo_half, wo_cols = wo.shape[0] // 2, cols // narrow
    quarter, span = tok // narrow, 2 * tok
    blocks = span // SHIFT
    vmem = pl.BlockSpec(memory_space=pltpu.VMEM)
    smem = pl.BlockSpec(memory_space=pltpu.SMEM)
    hbm = pl.BlockSpec(memory_space=pl.ANY)
    dma = pltpu.SemaphoreType.DMA
    bf16 = jnp.bfloat16
    return pl.pallas_call(
        functools.partial(hub_kernel, row_chunks, DIRECT),
        out_shape=pltpu.VMEM((quarter, n * cols), bf16),
        in_specs=[hbm, hbm, hbm, vmem, smem],
        out_specs=vmem,
        scratch_shapes=[
            pltpu.VMEM((heads, 3, width, HEAD_DIM), bf16),
            pltpu.VMEM((span, width), bf16),
            pltpu.VMEM((heads, 3, span, HEAD_DIM), jnp.float32),
            pltpu.VMEM((heads, span, HEAD_DIM), bf16),
            pltpu.VMEM((heads, 2, span + SHIFT, HEAD_DIM), bf16),
            pltpu.VMEM((narrow, 2, span, 2 * HEAD_DIM), bf16),
            pltpu.VMEM((n, 2, wo_half, wo_cols), bf16),
            pltpu.VMEM((n, span, wo_cols), bf16),
            pltpu.VMEM((span, seg.shape[1]), jnp.int32),
            dma((4,)),
            dma((9,)),
            dma((8 + blocks,)),
        ]
        + [dma((n,))] * 2
        + [dma((2, chunks))] * 3
        + [dma((row_chunks,)), dma((2,)), dma((2, wo_chunks)), dma((wo_chunks,)), dma((wo_chunks,))]
        + [dma((2, blocks))] * 2,
        compiler_params=pltpu.CompilerParams(
            collective_id=0, has_side_effects=True, vmem_limit_bytes=58 * 1024 * 1024
        ),
    )(hidden, wq, wo, seg, shift_heads)


def hub_per_device(hidden, w_qkv, w_out, seg_ids, shift_heads):
    return hub_layer(hidden, w_qkv.transpose(1, 0, 2), w_out, seg_ids.reshape(-1, 128), shift_heads)


def solution(mesh):
    placed = (
        P(("groups", "wide"), None),
        P("wide", None, "narrow"),
        P(None, "wide"),
        P("groups"),
        P(),
    )
    shape = mesh.shape
    hub = shape["groups"] == 2 and shape["wide"] == 4 and shape["narrow"] == 4
    return jax.shard_map(
        hub_per_device if hub else per_device,
        mesh=mesh,
        in_specs=placed,
        out_specs=P(("groups", "wide", "narrow"), None),
        check_vma=False,
    )
```

```python
import functools
import math

import jax
import jax.numpy as jnp
from jax import lax
from jax.experimental import pallas as pl
from jax.experimental.pallas import tpu as pltpu
from jax.sharding import PartitionSpec as P

HEAD_DIM = 128
GROUP = 512
SHIFT = 256

masked_out = -1e30
MESH = pl.DeviceIdType.MESH
ROWS = 128
WO_CHUNKS = 4
HUB_ROWS = 256
DIRECT = 2


def layer_kernel(
    n, narrow, chunks, wo_chunks,
    hidden_ref, wq_ref, wo_ref, segq_ref, segk_ref, out_ref,
    wbuf, acc, wo_buf, q_buf, kv_buf, att, part, pair_in, pair_sum, far_in,
    own_sem,
    qs_r, qs_l, qr, qs_y, qr_y,
    os_r, os_l, o_r, os_y, or_y,
    kv_sem, pair_s, pair_r, far_s, far_r,
):
    me = lax.axis_index("wide")
    y = lax.axis_index("groups")
    spot = lax.axis_index("narrow")
    other = 1 - y
    across_n = narrow // 2
    high, low = spot // 2, lax.rem(spot, 2)
    depth = wq_ref.shape[1]
    half = wbuf.shape[3]
    tok = hidden_ref.shape[0]
    rows = depth // chunks
    steps = (n - 1) * chunks
    wo_rows = wo_buf.shape[2] // wo_chunks
    cols = wo_buf.shape[3]
    blocks = tok // SHIFT
    per_half = half // HEAD_DIM
    has_left, has_right = me > 0, me < n - 1
    right, left = {"wide": me + 1}, {"wide": me - 1}
    after, before = {"wide": lax.rem(me + 1, n)}, {"wide": lax.rem(me + n - 1, n)}
    opposite = {"groups": other}
    pair = {"narrow": high * 2 + 1 - low}
    far = [{"narrow": lax.rem(high + d, across_n) * 2 + low} for d in range(1, across_n)]
    far_from = [{"narrow": lax.rem(high + across_n - d, across_n) * 2 + low} for d in range(1, across_n)]

    barrier = pltpu.get_barrier_semaphore()
    greeted = [after, before, opposite, pair] + far
    for device in greeted:
        pl.semaphore_signal(barrier, inc=1, device_id=device, device_id_type=MESH)

    def w_at(shard, part_of, c):
        start = pl.multiple_of(shard * depth + c * rows, rows)
        return wbuf.at[part_of, :, pl.ds(start, rows)]

    def wq_own(c):
        return wq_ref.at[
            :, pl.ds(pl.multiple_of(c * rows, rows), rows), pl.ds(pl.multiple_of(y * half, half), half)
        ]

    def o_at(shard, part_of, c):
        return wo_buf.at[shard, part_of, pl.ds(pl.multiple_of(c * wo_rows, wo_rows), wo_rows)]

    def wo_own(c):
        return wo_ref.at[spot, y, pl.ds(pl.multiple_of(c * wo_rows, wo_rows), wo_rows)]

    def remote(src, dst, send, recv, device):
        return pltpu.make_async_remote_copy(
            src_ref=src, dst_ref=dst, send_sem=send, recv_sem=recv,
            device_id=device, device_id_type=MESH,
        )

    def q_right(shard, c, src=None):
        dst = w_at(shard, y, c)
        return remote(dst if src is None else src, dst, qs_r.at[shard, c], qr.at[shard, c], right)

    def q_left(shard, c, src=None):
        dst = w_at(shard, y, c)
        return remote(dst if src is None else src, dst, qs_l.at[shard, c], qr.at[shard, c], left)

    def q_across(shard, c, part_of):
        ref = w_at(shard, part_of, c)
        return remote(ref, ref, qs_y.at[shard, c], qr_y.at[shard, c], opposite)

    def o_right(shard, c, src=None):
        dst = o_at(shard, y, c)
        return remote(dst if src is None else src, dst, os_r.at[shard, c], o_r.at[shard, c], right)

    def o_left(shard, c, src=None):
        dst = o_at(shard, y, c)
        return remote(dst if src is None else src, dst, os_l.at[shard, c], o_r.at[shard, c], left)

    def o_across(shard, c, part_of):
        ref = o_at(shard, part_of, c)
        return remote(ref, ref, os_y.at[shard, c], or_y.at[shard, c], opposite)

    own = [
        pltpu.make_async_copy(
            wq_ref.at[:, :, pl.ds(h * half, half)],
            wbuf.at[h, :, pl.ds(pl.multiple_of(me * depth, depth), depth)],
            own_sem.at[h],
        )
        for h in range(2)
    ]
    own.append(pltpu.make_async_copy(wo_ref.at[spot], wo_buf.at[me], own_sem.at[2]))
    for copy in own:
        copy.start()
    pl.semaphore_wait(barrier, len(greeted))

    @pl.loop(0, chunks)
    def _(c):
        @pl.when(has_right)
        def _():
            q_right(me, c, wq_own(c)).start()

        @pl.when(has_left)
        def _():
            q_left(me, c, wq_own(c)).start()

    acc[...] = jnp.zeros_like(acc)
    own[0].wait()
    own[1].wait()

    def add(shard, part_of, c):
        start = pl.multiple_of(shard * depth + c * rows, rows)
        piece = hidden_ref[:, pl.ds(start, rows)]
        for i in range(3):
            acc[part_of, i] += jnp.dot(
                piece, wbuf[part_of, i, pl.ds(start, rows)], preferred_element_type=jnp.float32
            )

    @pl.loop(0, 2 * chunks)
    def _(i):
        add(me, i // chunks, lax.rem(i, chunks))

    def add_across(t):
        s, c = t // chunks, lax.rem(t, chunks)
        for there, shard in ((me - 1 - s >= 0, me - 1 - s), (me + 1 + s <= n - 1, me + 1 + s)):
            @pl.when(there)
            def _():
                q_across(shard, c, other).wait_recv()
                add(shard, other, c)

    def send_own_wo():
        @pl.loop(0, wo_chunks)
        def _(c):
            @pl.when(has_right)
            def _():
                o_right(me, c, wo_own(c)).start()

            @pl.when(has_left)
            def _():
                o_left(me, c, wo_own(c)).start()

    @pl.loop(0, steps)
    def _(t):
        s, c = t // chunks, lax.rem(t, chunks)

        @pl.when(t == steps - chunks)
        def _():
            send_own_wo()

        @pl.when(me - 1 - s >= 0)
        def _():
            q_right(me - 1 - s, c).wait_recv()

            @pl.when(has_right)
            def _():
                q_right(me - 1 - s, c).start()

            q_across(me - 1 - s, c, y).start()

        @pl.when(me + 1 + s <= n - 1)
        def _():
            q_left(me + 1 + s, c).wait_recv()

            @pl.when(has_left)
            def _():
                q_left(me + 1 + s, c).start()

            q_across(me + 1 + s, c, y).start()

        for there, shard in ((me - 1 - s >= 0, me - 1 - s), (me + 1 + s <= n - 1, me + 1 + s)):
            @pl.when(there)
            def _():
                add(shard, y, c)

        @pl.when(t > 0)
        def _():
            add_across(t - 1)

    add_across(steps - 1)
    for h in range(2):
        q_buf[h] = acc[h, 0].astype(jnp.bfloat16)
        for i in range(2):
            kv_buf[h, i, SHIFT:] = acc[h, 1 + i].astype(jnp.bfloat16)

    kv_copy = remote(
        kv_buf.at[:, :, pl.ds(tok, SHIFT)], kv_buf.at[:, :, pl.ds(0, SHIFT)],
        kv_sem.at[0], kv_sem.at[1], after,
    )
    kv_copy.start()

    causal = lax.broadcasted_iota(jnp.int32, (SHIFT, 2 * SHIFT), 1) <= (
        lax.broadcasted_iota(jnp.int32, (SHIFT, 2 * SHIFT), 0) + SHIFT
    )

    def attend(h, b):
        lanes = slice((h % per_half) * HEAD_DIM, (h % per_half + 1) * HEAD_DIM)
        mine, seen = slice(b * SHIFT, (b + 1) * SHIFT), slice(b * SHIFT, (b + 2) * SHIFT)
        keys, values = kv_buf.at[h // per_half, 0], kv_buf.at[h // per_half, 1]
        scores = lax.dot_general(
            q_buf[h // per_half, mine, lanes], keys[seen, lanes], (((1,), (1,)), ((), ())),
            preferred_element_type=jnp.float32,
        ) * (1.0 / math.sqrt(HEAD_DIM))
        allowed = causal & (segq_ref[mine, :] == segk_ref[h, b])
        scores = jnp.where(allowed, scores, masked_out)
        exponent = jnp.exp(scores - jnp.max(scores, axis=-1, keepdims=True))
        weights = exponent / jnp.sum(exponent, axis=-1, keepdims=True)
        att[mine, h * HEAD_DIM : (h + 1) * HEAD_DIM] = jnp.dot(
            weights.astype(jnp.bfloat16), values[seen, lanes], preferred_element_type=jnp.float32
        ).astype(jnp.bfloat16)

    least = jnp.minimum(me, n - 1 - me)

    def block_of(k):
        turn = (k + 1) // 2
        near = jnp.where(lax.rem(k, 2) == 1, me - turn, me + turn)
        rest = jnp.where(me > least, me - (k - least), me + (k - least))
        return jnp.where(k <= 2 * least, near, rest)

    def pass_on(k):
        shard = block_of(k)

        @pl.loop(0, wo_chunks)
        def _(c):
            o_right(shard, c).wait_recv()

            @pl.when(jnp.logical_and(shard < me, has_right))
            def _():
                o_right(shard, c).start()

            @pl.when(jnp.logical_and(shard > me, has_left))
            def _():
                o_left(shard, c).start()

            o_across(shard, c, y).start()

    def pair_copy(shard, a):
        return remote(
            part.at[shard, a * 2 + 1 - low], pair_in.at[shard, a],
            pair_s.at[shard, a], pair_r.at[shard, a], pair,
        )

    def far_copy(shard, d):
        a = lax.rem(high + d, across_n)
        return remote(
            pair_sum.at[shard, a], far_in.at[shard, d - 1],
            far_s.at[shard, d - 1], far_r.at[shard, d - 1], far[d - 1],
        )

    def far_arrival(shard, d):
        return remote(
            pair_sum.at[shard, high], far_in.at[shard, d - 1],
            far_s.at[shard, d - 1], far_r.at[shard, d - 1], far_from[d - 1],
        )

    def multiply(k):
        shard = block_of(k)
        width = att.shape[1] // 2
        share = tok // narrow
        for p in range(narrow):
            a_rows = att[p * share : (p + 1) * share, :]
            total = jnp.dot(a_rows[:, :width], wo_buf[shard, 0], preferred_element_type=jnp.float32)
            total += jnp.dot(a_rows[:, width:], wo_buf[shard, 1], preferred_element_type=jnp.float32)
            part[shard, p] = total.astype(jnp.bfloat16)
        for a in range(across_n):
            pair_copy(shard, a).start()

    def sum_pair(k):
        shard = block_of(k)
        for a in range(across_n):
            pair_copy(shard, a).wait_recv()
            total = part[shard, a * 2 + low].astype(jnp.float32) + pair_in[shard, a].astype(jnp.float32)
            pair_sum[shard, a] = total.astype(jnp.bfloat16)
        for d in range(1, across_n):
            far_copy(shard, d).start()

    def finish(k):
        shard = block_of(k)
        total = part[shard, high * 2 + low].astype(jnp.float32) + pair_in[shard, high].astype(jnp.float32)
        for d in range(1, across_n):
            far_arrival(shard, d).wait_recv()
            total += far_in[shard, d - 1].astype(jnp.float32)
        out_ref[:, pl.ds(pl.multiple_of(shard * cols, cols), cols)] = total.astype(out_ref.dtype)

    heads = 2 * per_half
    for b in range(1, blocks):
        for h in range(heads):
            attend(h, b)
    pass_on(1)
    pass_on(2)
    kv_copy.wait_recv()
    for h in range(heads):
        attend(h, 0)
    own[2].wait()
    multiply(0)

    @pl.loop(1, n)
    def _(k):
        @pl.when(k > 2)
        def _():
            pass_on(k)

        sum_pair(k - 1)

        @pl.when(k > 1)
        def _():
            finish(k - 2)

        shard = block_of(k)

        @pl.loop(0, wo_chunks)
        def _(c):
            o_across(shard, c, other).wait_recv()

        multiply(k)

    sum_pair(n - 1)
    finish(n - 2)
    finish(n - 1)

    kv_copy.wait_send()

    @pl.loop(0, n)
    def _(shard):
        for a in range(across_n):
            pair_copy(shard, a).wait_send()
        for d in range(1, across_n):
            far_copy(shard, d).wait_send()
        goes_right = jnp.logical_and(shard <= me, has_right)
        goes_left = jnp.logical_and(shard >= me, has_left)
        for count, to_right, to_left, to_other in (
            (chunks, q_right, q_left, q_across), (wo_chunks, o_right, o_left, o_across)
        ):
            @pl.loop(0, count)
            def _(c):
                @pl.when(goes_right)
                def _():
                    to_right(shard, c).wait_send()

                @pl.when(goes_left)
                def _():
                    to_left(shard, c).wait_send()

                @pl.when(shard != me)
                def _():
                    to_other(shard, c, y).wait_send()


def layer(hidden, wq, wo, seg_q, seg_k):
    n, narrow = lax.axis_size("wide"), lax.axis_size("narrow")
    tok, width = hidden.shape
    half = wq.shape[2] // 2
    chunks = max(1, wq.shape[1] // ROWS)
    wo_chunks = WO_CHUNKS
    cols = wo.shape[3]
    share = tok // narrow
    vmem = pl.BlockSpec(memory_space=pltpu.VMEM)
    hbm = pl.BlockSpec(memory_space=pl.ANY)
    dma = pltpu.SemaphoreType.DMA
    bf16 = jnp.bfloat16
    return pl.pallas_call(
        functools.partial(layer_kernel, n, narrow, chunks, wo_chunks),
        out_shape=jax.ShapeDtypeStruct((share, n * cols), bf16),
        in_specs=[vmem, hbm, hbm, vmem, vmem],
        out_specs=vmem,
        scratch_shapes=[
            pltpu.VMEM((2, 3, width, half), bf16),
            pltpu.VMEM((2, 3, tok, half), jnp.float32),
            pltpu.VMEM((n,) + wo.shape[1:], bf16),
            pltpu.VMEM((2, tok, half), bf16),
            pltpu.VMEM((2, 2, tok + SHIFT, half), bf16),
            pltpu.VMEM((tok, 2 * half), bf16),
            pltpu.VMEM((n, narrow, share, cols), bf16),
            pltpu.VMEM((n, narrow // 2, share, cols), bf16),
            pltpu.VMEM((n, narrow // 2, share, cols), bf16),
            pltpu.VMEM((n, max(1, narrow // 2 - 1), share, cols), bf16),
            dma((3,)),
        ]
        + [dma((n, chunks))] * 5
        + [dma((n, wo_chunks))] * 5
        + [dma((2,))]
        + [dma((n, narrow // 2))] * 2
        + [dma((n, max(1, narrow // 2 - 1)))] * 2,
        compiler_params=pltpu.CompilerParams(
            collective_id=0, has_side_effects=True, vmem_limit_bytes=58 * 1024 * 1024
        ),
    )(hidden, wq, wo, seg_q, seg_k)


def per_device(hidden, w_qkv, w_out, seg_ids, shift_heads):
    tok_rows = hidden.shape[0]
    local_f = w_qkv.shape[2]
    heads_here = local_f // HEAD_DIM
    blocks = tok_rows // SHIFT
    narrow = lax.axis_size("narrow")
    first_tok = lax.axis_index("wide") * tok_rows
    shifted = lax.dynamic_slice_in_dim(shift_heads, lax.axis_index("narrow") * heads_here, heads_here) > 0

    doubled = jnp.concatenate([seg_ids[-SHIFT:], seg_ids], 0)
    seg_here = lax.dynamic_slice_in_dim(doubled, first_tok, tok_rows + SHIFT)
    seg_q = seg_here[SHIFT:, None]
    windows = jnp.stack([seg_here[b * SHIFT : (b + 2) * SHIFT] for b in range(blocks)])
    odd = (jnp.arange(blocks) % 2 == 1)[None, :, None]
    reaches = (shifted[:, None, None] != odd) | (jnp.arange(2 * SHIFT) >= SHIFT)[None, None, :]
    seg_k = jnp.where(reaches, windows[None], -1)[:, :, None, :]

    wq = w_qkv.transpose(1, 0, 2)
    wo = w_out.reshape(narrow, 2, local_f // 2, -1)
    return layer(hidden, wq, wo, seg_q, seg_k)


def hub_kernel(
    row_chunks, direct,
    hidden_ref, wq_ref, wo_ref, seg_ref, shift_ref, out_ref,
    wbuf, hid, acc, q_buf, kv_buf, att, wo_buf, stage, early, seg_col,
    own_sem, sends, joint, he_r, hx_r, wm_r, we_r, wy_r, w0_r, kv_r, om_r, oe_r, od_r, ax_r, ae_r,
):
    n, narrow = lax.axis_size("wide"), lax.axis_size("narrow")
    me = lax.axis_index("wide")
    y = lax.axis_index("groups")
    spot = lax.axis_index("narrow")
    opp = 1 - y
    side = me // (n // 2)
    inner, outer = n // 2 - 1 + side, side * (n - 1)
    far_inner, far_outer = n - 1 - inner, n - 1 - outer
    is_inner, is_outer = me == inner, me == outer
    high, low = spot // 2, lax.rem(spot, 2)
    core_n, x_n = high * 2 + 1 - low, (1 - high) * 2 + low
    diag_n = (1 - high) * 2 + 1 - low
    depth = wq_ref.shape[1]
    tok = hidden_ref.shape[0]
    heads = wbuf.shape[0]
    chunks = 2 * row_chunks
    rows = depth // row_chunks
    wo_chunks = 8
    sub = wo_chunks // 4
    quarter = tok // narrow
    span = 2 * tok
    blocks = span // SHIFT
    own_pos = 1 - side
    own_row = pl.multiple_of(own_pos * tok, tok)
    far_row = pl.multiple_of(side * tok, tok)
    wo_half, wo_cols = wo_buf.shape[2], wo_buf.shape[3]
    wo_rows, wo_lanes = wo_half // (2 * sub), wo_cols // 2
    cols = wo_ref.shape[1]
    to_core, to_x, to_y = {"narrow": core_n}, {"narrow": x_n}, {"groups": opp}
    to_far, to_inner, to_outer = {"wide": far_inner}, {"wide": inner}, {"wide": outer}
    my_pos = jnp.where(is_inner, own_pos, side)

    def remote(src, dst, send, recv, device):
        return pltpu.make_async_remote_copy(
            src_ref=src, dst_ref=dst, send_sem=send, recv_sem=recv,
            device_id=device, device_id_type=MESH,
        )

    def arrived(place, ref):
        remote(ref, ref, sends.at[0], joint.at[place], to_core).wait_recv()

    def sent(place, ref):
        remote(ref, ref, sends.at[place], joint.at[0], to_core).wait_send()

    def w_at(shard, part, c):
        start = pl.multiple_of(shard * depth + lax.rem(c, row_chunks) * rows, rows)
        return wbuf.at[c // row_chunks * 2 + part, :, pl.ds(start, rows)]

    def wq_at(part, c):
        start = pl.multiple_of(lax.rem(c, row_chunks) * rows, rows)
        lane = pl.multiple_of((c // row_chunks * 2 + part) * HEAD_DIM, HEAD_DIM)
        return wq_ref.at[:, pl.ds(start, rows), pl.ds(lane, HEAD_DIM)]

    def o_at(shard, part, c):
        start = pl.multiple_of(lax.rem(c, 2 * sub) * wo_rows, wo_rows)
        lane = pl.multiple_of(c // (2 * sub) * wo_lanes, wo_lanes)
        return wo_buf.at[shard, part, pl.ds(start, wo_rows), pl.ds(lane, wo_lanes)]

    def wo_at(part, c):
        start = pl.multiple_of(part * wo_half + lax.rem(c, 2 * sub) * wo_rows, wo_rows)
        lane = pl.multiple_of(spot * wo_cols + c // (2 * sub) * wo_lanes, wo_lanes)
        return wo_ref.at[pl.ds(start, wo_rows), pl.ds(lane, wo_lanes)]

    def h_at(row_n, k):
        start = pl.multiple_of(far_row + row_n * quarter, quarter)
        return hid.at[pl.ds(start, quarter), pl.ds(pl.multiple_of(k * depth, depth), depth)]

    def h_end(k):
        src = hidden_ref.at[
            pl.ds(pl.multiple_of(spot * quarter, quarter), quarter), pl.ds(pl.multiple_of(k * depth, depth), depth)
        ]
        return remote(src, h_at(spot, k), sends.at[0], he_r.at[k], to_inner)

    def h_x(k, row_n):
        return remote(h_at(row_n, k), h_at(row_n, k), sends.at[0], hx_r.at[k], to_x)

    def h_core(k, row_n):
        return remote(h_at(row_n, k), h_at(row_n, k), sends.at[0], joint.at[0], to_core)

    def w_end(j, c):
        part = y if j == 0 else opp
        return remote(wq_at(part, c), w_at(outer, part, c), sends.at[1], we_r.at[j, c], to_inner)

    def w_mid_send(s, c):
        if s == 0:
            return remote(wq_at(y, c), w_at(inner, y, c), sends.at[1], wm_r.at[s, c], to_far)
        return remote(w_at(outer, y, c), w_at(outer, y, c), sends.at[1], wm_r.at[s, c], to_far)

    def far_shard(s):
        return jnp.where(s == 0, far_inner, far_outer)

    def w_mid_recv(s, c):
        ref = w_at(far_shard(s), y, c)
        return remote(ref, ref, sends.at[1], wm_r.at[s, c], to_far)

    def w_y(s, c, part):
        ref = w_at(far_shard(s), part, c)
        return remote(ref, ref, sends.at[1], wy_r.at[s, c], to_y)

    def w_y_outer(c, part):
        ref = w_at(outer, part, c)
        return remote(ref, ref, sends.at[2], w0_r.at[c], to_y)

    def o_end(j, c):
        part = y if j == 0 else opp
        return remote(wo_at(part, c), o_at(outer, part, c), sends.at[4], oe_r.at[c] if j == 0 else joint.at[4], to_inner)

    def o_mid_send(s, c):
        if s == 0:
            return remote(wo_at(y, c), o_at(inner, y, c), sends.at[4], om_r.at[s, c], to_far)
        return remote(o_at(outer, y, c), o_at(outer, y, c), sends.at[4], om_r.at[s, c], to_far)

    def o_mid_recv(s, c):
        ref = o_at(far_shard(s), y, c)
        return remote(ref, ref, sends.at[4], om_r.at[s, c], to_far)

    def o_down(c):
        return remote(wo_at(y, c), o_at(inner, y, c), sends.at[5], od_r.at[c], to_outer)

    def o_y(s, c, part):
        ref = o_at(inner if s == 2 else far_shard(s), part, c)
        place = (1, 2 + c // (2 * sub), 6)[s]
        return remote(ref, ref, sends.at[5 if s == 2 else 4], joint.at[place], to_y)

    def att_at(row_n, g, b):
        return att.at[row_n, g, pl.ds(pl.multiple_of(b * SHIFT, SHIFT), SHIFT)]

    def att_x(g, b, row_n):
        ref = att_at(row_n, g, b)
        return remote(ref, ref, sends.at[6], ax_r.at[g, b], to_x)

    def att_core(g, b, row_n):
        ref = att_at(row_n, g, b)
        return remote(ref, ref, sends.at[6], joint.at[8 + b], to_core)

    def att_end(g, b):
        ref = att_at(spot, g, b)
        return remote(ref, ref, sends.at[7], ae_r.at[g, b], to_outer)

    def share(g, b):
        att_x(g, b, spot).start()
        att_core(g, b, spot).start()

    def relay(g, b):
        att_x(g, b, x_n).wait_recv()
        att_core(g, b, x_n).start()

    def gathered(b):
        arrived(8 + b, att.at[pl.ds(0, narrow // 2), :, pl.ds(pl.multiple_of(b * SHIFT, SHIFT), SHIFT)])

    shards = (inner, far_inner, outer, far_outer)
    slots = ((0, 0, wo_cols), (1, 0, wo_cols)) + tuple((s, k * wo_lanes, wo_lanes) for s in (2, 3) for k in range(2))
    slots += ((2, 0, wo_cols),)

    def res_cols(slot, row_n):
        order, lane, size = slots[slot]
        return pl.ds(pl.multiple_of(shards[order] * cols + row_n * wo_cols + lane, size), size)

    def result(slot, pos, to_n):
        order, lane, size = slots[slot]
        return remote(
            stage.at[order, pl.ds(pl.multiple_of(pos * tok + to_n * quarter, quarter), quarter), lane : lane + size],
            out_ref.at[:, res_cols(slot, spot)],
            sends.at[8], joint.at[7],
            {"wide": side * (n // 2) + pos, "narrow": to_n},
        )

    def product(slot, b, firsts):
        order, lane, size = slots[slot]
        mine = pl.ds(pl.multiple_of(b * SHIFT, SHIFT), SHIFT)
        a_cols = att.shape[3]
        total = None
        for row_half in firsts:
            for p in range(narrow // 2):
                for g in range(2):
                    start = (p * 2 + g) * a_cols
                    term = jnp.dot(
                        att[row_half * (narrow // 2) + p, g, mine],
                        wo_buf[shards[order], row_half, start : start + a_cols, lane : lane + size],
                        preferred_element_type=jnp.float32,
                    )
                    total = term if total is None else total + term
        return total

    def emit(slot, b, total):
        order, lane, size = slots[slot]
        mine = pl.ds(pl.multiple_of(b * SHIFT, SHIFT), SHIFT)
        done = total.astype(jnp.bfloat16)
        stage[order, mine, lane : lane + size] = done
        pos = b // (blocks // 2)
        for k in range(SHIFT // quarter):
            to_n = lax.rem(b, blocks // 2) * (SHIFT // quarter) + k
            here = jnp.logical_and(pos == my_pos, spot == to_n)

            @pl.when(here)
            def _():
                out_ref[:, res_cols(slot, spot)] = done[k * quarter : (k + 1) * quarter]

            @pl.when(jnp.logical_not(here))
            def _():
                result(slot, pos, to_n).start()

    def multiply(slot, b):
        emit(slot, b, product(slot, b, (0, 1)))

    def kv_copy(g):
        return remote(
            kv_buf.at[pl.ds(2 * g, 2), :, pl.ds(span, SHIFT)], kv_buf.at[pl.ds(2 * g, 2), :, pl.ds(0, SHIFT)],
            sends.at[3], kv_r.at[g], to_far,
        )

    barrier = pltpu.get_barrier_semaphore()
    beside = [{"narrow": core_n}, {"narrow": x_n}, {"narrow": diag_n}, to_y]

    def greet(peers):
        for device in peers:
            pl.semaphore_signal(barrier, inc=1, device_id=device, device_id_type=MESH)
        pl.semaphore_wait(barrier, len(peers))

    def own_wo(h):
        return pltpu.make_async_copy(
            wo_ref.at[pl.ds(h * wo_half, wo_half), pl.ds(pl.multiple_of(spot * wo_cols, wo_cols), wo_cols)],
            wo_buf.at[me, h],
            own_sem.at[2 + h],
        )


    @pl.when(is_outer)
    def _():
        greet(beside + [{"wide": inner, "narrow": p} for p in range(narrow)])

        @pl.loop(0, n)
        def _(k):
            h_end(k).start()

        def each_end(act):
            @pl.loop(0, chunks)
            def _(c):
                act(w_end(0, c))

            @pl.loop(0, direct)
            def _(c):
                act(w_end(1, c))

            @pl.loop(row_chunks, chunks)
            def _(c):
                act(w_end(1, c))

            for j in range(2):
                @pl.loop(0, wo_chunks)
                def _(c):
                    act(o_end(j, c))

        each_end(lambda copy: copy.start())
        for h in range(2):
            own_wo(h).start()

        @pl.loop(0, wo_chunks)
        def _(c):
            o_down(c).wait_recv()
            o_y(2, c, y).start()

        arrived(6, wo_buf.at[inner, opp])
        for h in range(2):
            own_wo(h).wait()

        def take(g, b):
            att_end(g, b).wait_recv()
            share(g, b)

        first_b, second_b = side + 1, 3 * side
        take(0, first_b)
        relay(0, first_b)
        take(0, second_b)
        relay(0, second_b)
        take(1, first_b)

        @pl.when(side == 1)
        def _():
            take(1, second_b)

        relay(1, first_b)

        @pl.when(side == 0)
        def _():
            take(1, second_b)

        gathered(first_b)
        multiply(0, first_b)
        multiply(6, first_b)
        relay(1, second_b)
        gathered(second_b)
        multiply(0, second_b)
        multiply(6, second_b)

        sent(0, hid.at[pl.ds(0, quarter)])
        sent(1, wbuf.at[0, :, pl.ds(0, (chunks + direct + row_chunks) * rows)])
        sent(4, wo_buf.at[0])
        sent(5, wo_buf.at[0, 0])
        sent(6, att.at[pl.ds(0, 3), 0])
        sent(8, stage.at[0, pl.ds(0, 2 * (narrow - 1) * quarter)])
        arrived(7, out_ref.at[:, pl.ds(0, (4 * narrow - 2) * wo_cols)])

    @pl.when(is_inner)
    def _():
        own = [
            pltpu.make_async_copy(
                wq_ref.at[:, :, pl.ds(h * HEAD_DIM, HEAD_DIM)],
                wbuf.at[h, :, pl.ds(pl.multiple_of(inner * depth, depth), depth)],
                own_sem.at[0],
            )
            for h in range(heads)
        ]
        own.append(pltpu.make_async_copy(hidden_ref, hid.at[pl.ds(own_row, tok)], own_sem.at[1]))
        for copy in own:
            copy.start()
        for h in range(2):
            own_wo(h).start()
        greet(beside + [to_far] + [{"wide": outer, "narrow": p} for p in range(narrow)])

        @pl.loop(0, chunks)
        def _(c):
            w_mid_send(0, c).start()

        @pl.loop(0, wo_chunks)
        def _(c):
            o_down(c).start()

        acc[...] = jnp.zeros_like(acc)
        seg_rows = seg_ref.shape[0]
        lanes = seg_ref.shape[1]
        seg_first = side * (span // lanes)
        for k in range(span // lanes):
            line = seg_ref[pl.ds(seg_first + k, 1), :]
            seg_col[k * lanes : (k + 1) * lanes, :] = jnp.broadcast_to(line, (lanes, lanes)).T

        def add(row, size, shard, part, c):
            start = pl.multiple_of(shard * depth + lax.rem(c, row_chunks) * rows, rows)
            head = c // row_chunks * 2 + part
            here = pl.ds(row, size)
            piece = hid[here, pl.ds(start, rows)]
            both = jnp.concatenate([wbuf[head, i, pl.ds(start, rows)] for i in range(2)], axis=1)
            found = jnp.dot(piece, both, preferred_element_type=jnp.float32)
            acc[head, 0, here] += found[:, :HEAD_DIM]
            acc[head, 1, here] += found[:, HEAD_DIM:]
            acc[head, 2, here] += jnp.dot(piece, wbuf[head, 2, pl.ds(start, rows)], preferred_element_type=jnp.float32)

        def add_all(shard, part, c):
            add(0, span, shard, part, c)

        def add_at(t, shard, part, c):
            @pl.when(t < chunks)
            def _():
                add(own_row, tok, shard, part, c)

            @pl.when(t >= chunks)
            def _():
                add_all(shard, part, c)

        pltpu.make_async_copy(
            wbuf.at[:, :, pl.ds(0, depth)],
            wbuf.at[:, :, pl.ds(pl.multiple_of(inner * depth, depth), depth)],
            own_sem.at[0],
        ).wait()
        own[heads].wait()

        @pl.loop(0, 2 * chunks)
        def _(u):
            add(own_row, tok, inner, u // chunks, lax.rem(u, chunks))

        def own_mid(first, last):
            @pl.loop(first, last)
            def _(c):
                o_mid_send(0, c).start()

        lag = row_chunks
        lead = chunks - 2
        catch_up = 4 * chunks - lag

        @pl.loop(0, 2 * chunks)
        def _(t):
            s, c = t // chunks, lax.rem(t, chunks)
            q = t - lead

            @pl.when(jnp.logical_and(q >= 0, q < chunks))
            def _():
                w_end(0, q).wait_recv()
                w_mid_send(1, q).start()

            @pl.when(jnp.logical_and(q >= direct, q < row_chunks))
            def _():
                w_y_outer(q, y).start()

            w_mid_recv(s, c).wait_recv()
            w_y(s, c, y).start()

            @pl.when(jnp.logical_and(t >= 1, t < 1 + n))
            def _():
                h_end(t - 1).wait_recv()
                h_x(t - 1, spot).start()
                h_core(t - 1, spot).start()

            @pl.when(jnp.logical_and(t >= 4, t < 4 + n))
            def _():
                h_x(t - 4, x_n).wait_recv()
                h_core(t - 4, x_n).start()

            @pl.when(t == chunks)
            def _():
                arrived(0, hid.at[pl.ds(far_row, narrow // 2 * quarter)])

            @pl.when(t == lead + chunks)
            def _():
                own_mid(0, 2)

            add_at(t, far_shard(s), y, c)

            @pl.when(t >= lag)
            def _():
                v = t - lag
                w_y(v // chunks, lax.rem(v, chunks), opp).wait_recv()
                add_at(t, far_shard(v // chunks), opp, lax.rem(v, chunks))

            @pl.when(t >= chunks)
            def _():
                add_all(outer, y, t - chunks)
                u0 = 4 * (t - chunks)

                @pl.loop(u0, jnp.minimum(u0 + 4, catch_up))
                def _(u):
                    turn = u // row_chunks
                    near = lax.rem(turn, 4) < 2
                    part = jnp.where(near, lax.rem(turn, 2), jnp.where(lax.rem(turn, 2) == 0, y, opp))
                    c = lax.rem(u, row_chunks) + turn // 4 * row_chunks
                    add(far_row, tok, jnp.where(near, inner, far_inner), part, c)

            @pl.when(t >= chunks + row_chunks)
            def _():
                k = lax.rem(t - chunks - row_chunks + direct, row_chunks)

                @pl.when(k < direct)
                def _():
                    w_end(1, k).wait_recv()

                @pl.when(k >= direct)
                def _():
                    w_y_outer(k, opp).wait_recv()

                add_all(outer, opp, k)

        causal = lax.broadcasted_iota(jnp.int32, (SHIFT, 2 * SHIFT), 1) <= (
            lax.broadcasted_iota(jnp.int32, (SHIFT, 2 * SHIFT), 0) + SHIFT
        )
        per_block = SHIFT // lanes

        def seg_line(b):
            at = [lax.rem(seg_first + b * per_block + k + seg_rows, seg_rows) for k in range(per_block)]
            return jnp.concatenate([seg_ref[pl.ds(i, 1), :] for i in at], axis=1)

        def attend(g, b):
            mine, seen = slice(b * SHIFT, (b + 1) * SHIFT), slice(b * SHIFT, (b + 2) * SHIFT)
            seg_q = jnp.concatenate([seg_col[mine, :]] * (2 * per_block), axis=1)
            near, prior = seg_line(b), seg_line(b - 1)
            for k in range(2):
                h = 2 * g + k
                reach = shift_ref[spot * heads + h]
                if b % 2 == 1:
                    reach = 1 - reach
                seg_k = jnp.concatenate([prior * reach + (reach - 1), near], axis=1)
                scores = lax.dot_general(
                    q_buf[h, mine], kv_buf[h, 0, seen], (((1,), (1,)), ((), ())),
                    preferred_element_type=jnp.float32,
                ) * (1.0 / math.sqrt(HEAD_DIM))
                allowed = causal & (seg_q == seg_k)
                scores = jnp.where(allowed, scores, masked_out)
                exponent = jnp.exp(scores - jnp.max(scores, axis=-1, keepdims=True))
                weights = exponent / jnp.sum(exponent, axis=-1, keepdims=True)
                att[spot, g, mine, k * HEAD_DIM : (k + 1) * HEAD_DIM] = jnp.dot(
                    weights.astype(jnp.bfloat16), kv_buf[h, 1, seen], preferred_element_type=jnp.float32
                ).astype(jnp.bfloat16)
            share(g, b)

            @pl.when(b // (blocks // 2) == side)
            def _():
                att_end(g, b).start()

        def settle(g):
            for h in (2 * g, 2 * g + 1):
                for i in range(2):
                    kv_buf[h, i, SHIFT:] = acc[h, 1 + i].astype(jnp.bfloat16)
            kv_copy(g).start()
            for h in (2 * g, 2 * g + 1):
                q_buf[h] = acc[h, 0].astype(jnp.bfloat16)

        def multiply_these(slot, first, count):
            @pl.loop(0, count)
            def _(k):
                multiply(slot, lax.rem(first + k, blocks))

        def multiply_own(slot, b):
            @pl.when(b // (blocks // 2) == own_pos)
            def _():
                multiply(slot, b)

        def relay_wo(arrival, *onward):
            def act(i, count):
                @pl.loop(i, i + count)
                def _(c):
                    arrival(c).wait_recv()
                    for copy in onward:
                        copy(c).start()

            return act

        near_wo = relay_wo(lambda c: o_mid_recv(0, c), lambda c: o_y(0, c, y))
        far_wo = relay_wo(lambda c: o_mid_recv(1, c), lambda c: o_y(1, c, y))
        pass_wo = relay_wo(lambda c: o_end(0, c), lambda c: o_mid_send(1, c))

        def half_of(shard, lane_half):
            return wo_buf.at[shard, opp, :, lane_half * wo_lanes : (lane_half + 1) * wo_lanes]

        def last_y(c):
            w_y(1, c, opp).wait_recv()
            add_all(far_outer, opp, c)

        def last_end(c):
            w_end(1, c).wait_recv()
            add_all(outer, opp, c)

        settle(0)
        own_mid(2, 7)
        attend(0, 1)
        last_y(row_chunks)
        near_wo(0, 2)
        attend(0, 2)
        last_y(row_chunks + 1)
        attend(0, 3)

        @pl.loop(row_chunks, chunks - 2)
        def _(c):
            last_end(c)

        relay(0, 1)
        kv_copy(0).wait_recv()
        attend(0, 0)
        relay(0, 2)
        last_y(row_chunks + 2)
        last_end(chunks - 2)
        near_wo(2, 2)
        relay(0, 3)
        last_end(chunks - 1)
        last_y(row_chunks + 3)
        settle(1)
        own_mid(7, 8)
        attend(1, 1)
        near_wo(4, 2)
        attend(1, 2)
        relay(0, 0)
        pass_wo(0, 2)
        attend(1, 3)
        near_wo(6, 1)
        for h in range(2):
            own_wo(h).wait()
        pass_wo(2, 2)
        relay(1, 1)
        gathered(1)
        multiply_own(0, 1)
        pass_wo(4, 2)
        kv_copy(1).wait_recv()
        attend(1, 0)
        near_wo(7, 1)
        pass_wo(6, 2)
        relay(1, 2)
        gathered(2)
        multiply_own(0, 2)
        far_wo(0, 2)
        relay(1, 3)
        gathered(3)
        multiply_own(0, 3)
        arrived(1, wo_buf.at[far_inner, opp])
        multiply(1, side + 1)
        far_wo(2, 1)
        relay(1, 0)
        multiply(1, 3)
        far_wo(3, 2)
        gathered(0)
        multiply(1, 0)
        far_wo(5, 1)
        multiply(1, own_pos + 1)
        multiply_own(0, 0)
        first = side * (blocks // 2)
        far_wo(6, 2)
        arrived(2, half_of(far_outer, 0))
        multiply_these(4, first, blocks)
        arrived(4, wo_buf.at[outer, opp])
        multiply_these(6, own_pos * (blocks // 2), blocks // 2)

        @pl.loop(0, blocks)
        def _(b):
            early[b] = product(5, b, (y,))

        arrived(3, half_of(far_outer, 1))

        @pl.loop(0, blocks)
        def _(turn):
            b = lax.rem(first + turn, blocks)
            emit(5, b, early[b] + product(5, b, (opp,)))

        sent(0, hid.at[pl.ds(0, 3 * quarter)])
        sent(1, wbuf.at[pl.ds(0, 2)])
        sent(2, wbuf.at[0, :, pl.ds(0, (row_chunks - direct) * rows)])
        sent(3, kv_buf.at[:, :, pl.ds(0, SHIFT)])
        sent(4, wo_buf.at[pl.ds(0, 2)])
        sent(5, wo_buf.at[0, 0])
        sent(6, att.at[pl.ds(0, 3)])
        sent(7, att.at[0, 0])
        pieces = 4 * (narrow - 1) + 2 * narrow
        sent(8, hid.at[pl.ds(0, pieces * quarter * wo_cols // hid.shape[1])])
        arrived(7, out_ref.at[:, pl.ds(0, 4 * (narrow - 1) * wo_cols)])


def hub_layer(hidden, wq, wo, seg, shift_heads):
    n, narrow = lax.axis_size("wide"), lax.axis_size("narrow")
    tok, width = hidden.shape
    heads = wq.shape[2] // HEAD_DIM
    row_chunks = wq.shape[1] // HUB_ROWS
    chunks, wo_chunks = 2 * row_chunks, 8
    cols = wo.shape[1]
    wo_half, wo_cols = wo.shape[0] // 2, cols // narrow
    quarter, span = tok // narrow, 2 * tok
    blocks = span // SHIFT
    vmem = pl.BlockSpec(memory_space=pltpu.VMEM)
    smem = pl.BlockSpec(memory_space=pltpu.SMEM)
    hbm = pl.BlockSpec(memory_space=pl.ANY)
    dma = pltpu.SemaphoreType.DMA
    bf16 = jnp.bfloat16
    return pl.pallas_call(
        functools.partial(hub_kernel, row_chunks, DIRECT),
        out_shape=pltpu.VMEM((quarter, n * cols), bf16),
        in_specs=[hbm, hbm, hbm, vmem, smem],
        out_specs=vmem,
        scratch_shapes=[
            pltpu.VMEM((heads, 3, width, HEAD_DIM), bf16),
            pltpu.VMEM((span, width), bf16),
            pltpu.VMEM((heads, 3, span, HEAD_DIM), jnp.float32),
            pltpu.VMEM((heads, span, HEAD_DIM), bf16),
            pltpu.VMEM((heads, 2, span + SHIFT, HEAD_DIM), bf16),
            pltpu.VMEM((narrow, 2, span, 2 * HEAD_DIM), bf16),
            pltpu.VMEM((n, 2, wo_half, wo_cols), bf16),
            pltpu.VMEM((n, span, wo_cols), bf16),
            pltpu.VMEM((blocks, SHIFT, wo_cols // 2), jnp.float32),
            pltpu.VMEM((span, seg.shape[1]), jnp.int32),
            dma((4,)),
            dma((9,)),
            dma((8 + blocks,)),
        ]
        + [dma((n,))] * 2
        + [dma((2, chunks))] * 3
        + [dma((row_chunks,)), dma((2,)), dma((2, wo_chunks)), dma((wo_chunks,)), dma((wo_chunks,))]
        + [dma((2, blocks))] * 2,
        compiler_params=pltpu.CompilerParams(
            collective_id=0, has_side_effects=True, vmem_limit_bytes=58 * 1024 * 1024
        ),
    )(hidden, wq, wo, seg, shift_heads)


def hub_per_device(hidden, w_qkv, w_out, seg_ids, shift_heads):
    return hub_layer(hidden, w_qkv.transpose(1, 0, 2), w_out, seg_ids.reshape(-1, 128), shift_heads)


def solution(mesh):
    placed = (
        P(("groups", "wide"), None),
        P("wide", None, "narrow"),
        P(None, "wide"),
        P("groups"),
        P(),
    )
    shape = mesh.shape
    hub = shape["groups"] == 2 and shape["wide"] == 4 and shape["narrow"] == 4
    return jax.shard_map(
        hub_per_device if hub else per_device,
        mesh=mesh,
        in_specs=placed,
        out_specs=P(("groups", "wide", "narrow"), None),
        check_vma=False,
    )
```

```python
import functools
import math

import jax
import jax.numpy as jnp
from jax import lax
from jax.experimental import pallas as pl
from jax.experimental.pallas import tpu as pltpu
from jax.sharding import PartitionSpec as P

HEAD_DIM = 128
GROUP = 512
SHIFT = 256

masked_out = -1e30
MESH = pl.DeviceIdType.MESH
ROWS = 128
WO_CHUNKS = 4
HUB_ROWS = 256
DIRECT = 2


def layer_kernel(
    n, narrow, chunks, wo_chunks,
    hidden_ref, wq_ref, wo_ref, segq_ref, segk_ref, out_ref,
    wbuf, acc, wo_buf, q_buf, kv_buf, att, part, pair_in, pair_sum, far_in,
    own_sem,
    qs_r, qs_l, qr, qs_y, qr_y,
    os_r, os_l, o_r, os_y, or_y,
    kv_sem, pair_s, pair_r, far_s, far_r,
):
    me = lax.axis_index("wide")
    y = lax.axis_index("groups")
    spot = lax.axis_index("narrow")
    other = 1 - y
    across_n = narrow // 2
    high, low = spot // 2, lax.rem(spot, 2)
    depth = wq_ref.shape[1]
    half = wbuf.shape[3]
    tok = hidden_ref.shape[0]
    rows = depth // chunks
    steps = (n - 1) * chunks
    wo_rows = wo_buf.shape[2] // wo_chunks
    cols = wo_buf.shape[3]
    blocks = tok // SHIFT
    per_half = half // HEAD_DIM
    has_left, has_right = me > 0, me < n - 1
    right, left = {"wide": me + 1}, {"wide": me - 1}
    after, before = {"wide": lax.rem(me + 1, n)}, {"wide": lax.rem(me + n - 1, n)}
    opposite = {"groups": other}
    pair = {"narrow": high * 2 + 1 - low}
    far = [{"narrow": lax.rem(high + d, across_n) * 2 + low} for d in range(1, across_n)]
    far_from = [{"narrow": lax.rem(high + across_n - d, across_n) * 2 + low} for d in range(1, across_n)]

    barrier = pltpu.get_barrier_semaphore()
    greeted = [after, before, opposite, pair] + far
    for device in greeted:
        pl.semaphore_signal(barrier, inc=1, device_id=device, device_id_type=MESH)

    def w_at(shard, part_of, c):
        start = pl.multiple_of(shard * depth + c * rows, rows)
        return wbuf.at[part_of, :, pl.ds(start, rows)]

    def wq_own(c):
        return wq_ref.at[
            :, pl.ds(pl.multiple_of(c * rows, rows), rows), pl.ds(pl.multiple_of(y * half, half), half)
        ]

    def o_at(shard, part_of, c):
        return wo_buf.at[shard, part_of, pl.ds(pl.multiple_of(c * wo_rows, wo_rows), wo_rows)]

    def wo_own(c):
        return wo_ref.at[spot, y, pl.ds(pl.multiple_of(c * wo_rows, wo_rows), wo_rows)]

    def remote(src, dst, send, recv, device):
        return pltpu.make_async_remote_copy(
            src_ref=src, dst_ref=dst, send_sem=send, recv_sem=recv,
            device_id=device, device_id_type=MESH,
        )

    def q_right(shard, c, src=None):
        dst = w_at(shard, y, c)
        return remote(dst if src is None else src, dst, qs_r.at[shard, c], qr.at[shard, c], right)

    def q_left(shard, c, src=None):
        dst = w_at(shard, y, c)
        return remote(dst if src is None else src, dst, qs_l.at[shard, c], qr.at[shard, c], left)

    def q_across(shard, c, part_of):
        ref = w_at(shard, part_of, c)
        return remote(ref, ref, qs_y.at[shard, c], qr_y.at[shard, c], opposite)

    def o_right(shard, c, src=None):
        dst = o_at(shard, y, c)
        return remote(dst if src is None else src, dst, os_r.at[shard, c], o_r.at[shard, c], right)

    def o_left(shard, c, src=None):
        dst = o_at(shard, y, c)
        return remote(dst if src is None else src, dst, os_l.at[shard, c], o_r.at[shard, c], left)

    def o_across(shard, c, part_of):
        ref = o_at(shard, part_of, c)
        return remote(ref, ref, os_y.at[shard, c], or_y.at[shard, c], opposite)

    own = [
        pltpu.make_async_copy(
            wq_ref.at[:, :, pl.ds(h * half, half)],
            wbuf.at[h, :, pl.ds(pl.multiple_of(me * depth, depth), depth)],
            own_sem.at[h],
        )
        for h in range(2)
    ]
    own.append(pltpu.make_async_copy(wo_ref.at[spot], wo_buf.at[me], own_sem.at[2]))
    for copy in own:
        copy.start()
    pl.semaphore_wait(barrier, len(greeted))

    @pl.loop(0, chunks)
    def _(c):
        @pl.when(has_right)
        def _():
            q_right(me, c, wq_own(c)).start()

        @pl.when(has_left)
        def _():
            q_left(me, c, wq_own(c)).start()

    acc[...] = jnp.zeros_like(acc)
    own[0].wait()
    own[1].wait()

    def add(shard, part_of, c):
        start = pl.multiple_of(shard * depth + c * rows, rows)
        piece = hidden_ref[:, pl.ds(start, rows)]
        for i in range(3):
            acc[part_of, i] += jnp.dot(
                piece, wbuf[part_of, i, pl.ds(start, rows)], preferred_element_type=jnp.float32
            )

    @pl.loop(0, 2 * chunks)
    def _(i):
        add(me, i // chunks, lax.rem(i, chunks))

    def add_across(t):
        s, c = t // chunks, lax.rem(t, chunks)
        for there, shard in ((me - 1 - s >= 0, me - 1 - s), (me + 1 + s <= n - 1, me + 1 + s)):
            @pl.when(there)
            def _():
                q_across(shard, c, other).wait_recv()
                add(shard, other, c)

    def send_own_wo():
        @pl.loop(0, wo_chunks)
        def _(c):
            @pl.when(has_right)
            def _():
                o_right(me, c, wo_own(c)).start()

            @pl.when(has_left)
            def _():
                o_left(me, c, wo_own(c)).start()

    @pl.loop(0, steps)
    def _(t):
        s, c = t // chunks, lax.rem(t, chunks)

        @pl.when(t == steps - chunks)
        def _():
            send_own_wo()

        @pl.when(me - 1 - s >= 0)
        def _():
            q_right(me - 1 - s, c).wait_recv()

            @pl.when(has_right)
            def _():
                q_right(me - 1 - s, c).start()

            q_across(me - 1 - s, c, y).start()

        @pl.when(me + 1 + s <= n - 1)
        def _():
            q_left(me + 1 + s, c).wait_recv()

            @pl.when(has_left)
            def _():
                q_left(me + 1 + s, c).start()

            q_across(me + 1 + s, c, y).start()

        for there, shard in ((me - 1 - s >= 0, me - 1 - s), (me + 1 + s <= n - 1, me + 1 + s)):
            @pl.when(there)
            def _():
                add(shard, y, c)

        @pl.when(t > 0)
        def _():
            add_across(t - 1)

    add_across(steps - 1)
    for h in range(2):
        q_buf[h] = acc[h, 0].astype(jnp.bfloat16)
        for i in range(2):
            kv_buf[h, i, SHIFT:] = acc[h, 1 + i].astype(jnp.bfloat16)

    kv_copy = remote(
        kv_buf.at[:, :, pl.ds(tok, SHIFT)], kv_buf.at[:, :, pl.ds(0, SHIFT)],
        kv_sem.at[0], kv_sem.at[1], after,
    )
    kv_copy.start()

    causal = lax.broadcasted_iota(jnp.int32, (SHIFT, 2 * SHIFT), 1) <= (
        lax.broadcasted_iota(jnp.int32, (SHIFT, 2 * SHIFT), 0) + SHIFT
    )

    def attend(h, b):
        lanes = slice((h % per_half) * HEAD_DIM, (h % per_half + 1) * HEAD_DIM)
        mine, seen = slice(b * SHIFT, (b + 1) * SHIFT), slice(b * SHIFT, (b + 2) * SHIFT)
        keys, values = kv_buf.at[h // per_half, 0], kv_buf.at[h // per_half, 1]
        scores = lax.dot_general(
            q_buf[h // per_half, mine, lanes], keys[seen, lanes], (((1,), (1,)), ((), ())),
            preferred_element_type=jnp.float32,
        ) * (1.0 / math.sqrt(HEAD_DIM))
        allowed = causal & (segq_ref[mine, :] == segk_ref[h, b])
        scores = jnp.where(allowed, scores, masked_out)
        exponent = jnp.exp(scores - jnp.max(scores, axis=-1, keepdims=True))
        weights = exponent / jnp.sum(exponent, axis=-1, keepdims=True)
        att[mine, h * HEAD_DIM : (h + 1) * HEAD_DIM] = jnp.dot(
            weights.astype(jnp.bfloat16), values[seen, lanes], preferred_element_type=jnp.float32
        ).astype(jnp.bfloat16)

    least = jnp.minimum(me, n - 1 - me)

    def block_of(k):
        turn = (k + 1) // 2
        near = jnp.where(lax.rem(k, 2) == 1, me - turn, me + turn)
        rest = jnp.where(me > least, me - (k - least), me + (k - least))
        return jnp.where(k <= 2 * least, near, rest)

    def pass_on(k):
        shard = block_of(k)

        @pl.loop(0, wo_chunks)
        def _(c):
            o_right(shard, c).wait_recv()

            @pl.when(jnp.logical_and(shard < me, has_right))
            def _():
                o_right(shard, c).start()

            @pl.when(jnp.logical_and(shard > me, has_left))
            def _():
                o_left(shard, c).start()

            o_across(shard, c, y).start()

    def pair_copy(shard, a):
        return remote(
            part.at[shard, a * 2 + 1 - low], pair_in.at[shard, a],
            pair_s.at[shard, a], pair_r.at[shard, a], pair,
        )

    def far_copy(shard, d):
        a = lax.rem(high + d, across_n)
        return remote(
            pair_sum.at[shard, a], far_in.at[shard, d - 1],
            far_s.at[shard, d - 1], far_r.at[shard, d - 1], far[d - 1],
        )

    def far_arrival(shard, d):
        return remote(
            pair_sum.at[shard, high], far_in.at[shard, d - 1],
            far_s.at[shard, d - 1], far_r.at[shard, d - 1], far_from[d - 1],
        )

    def multiply(k):
        shard = block_of(k)
        width = att.shape[1] // 2
        share = tok // narrow
        for p in range(narrow):
            a_rows = att[p * share : (p + 1) * share, :]
            total = jnp.dot(a_rows[:, :width], wo_buf[shard, 0], preferred_element_type=jnp.float32)
            total += jnp.dot(a_rows[:, width:], wo_buf[shard, 1], preferred_element_type=jnp.float32)
            part[shard, p] = total.astype(jnp.bfloat16)
        for a in range(across_n):
            pair_copy(shard, a).start()

    def sum_pair(k):
        shard = block_of(k)
        for a in range(across_n):
            pair_copy(shard, a).wait_recv()
            total = part[shard, a * 2 + low].astype(jnp.float32) + pair_in[shard, a].astype(jnp.float32)
            pair_sum[shard, a] = total.astype(jnp.bfloat16)
        for d in range(1, across_n):
            far_copy(shard, d).start()

    def finish(k):
        shard = block_of(k)
        total = part[shard, high * 2 + low].astype(jnp.float32) + pair_in[shard, high].astype(jnp.float32)
        for d in range(1, across_n):
            far_arrival(shard, d).wait_recv()
            total += far_in[shard, d - 1].astype(jnp.float32)
        out_ref[:, pl.ds(pl.multiple_of(shard * cols, cols), cols)] = total.astype(out_ref.dtype)

    heads = 2 * per_half
    for b in range(1, blocks):
        for h in range(heads):
            attend(h, b)
    pass_on(1)
    pass_on(2)
    kv_copy.wait_recv()
    for h in range(heads):
        attend(h, 0)
    own[2].wait()
    multiply(0)

    @pl.loop(1, n)
    def _(k):
        @pl.when(k > 2)
        def _():
            pass_on(k)

        sum_pair(k - 1)

        @pl.when(k > 1)
        def _():
            finish(k - 2)

        shard = block_of(k)

        @pl.loop(0, wo_chunks)
        def _(c):
            o_across(shard, c, other).wait_recv()

        multiply(k)

    sum_pair(n - 1)
    finish(n - 2)
    finish(n - 1)

    kv_copy.wait_send()

    @pl.loop(0, n)
    def _(shard):
        for a in range(across_n):
            pair_copy(shard, a).wait_send()
        for d in range(1, across_n):
            far_copy(shard, d).wait_send()
        goes_right = jnp.logical_and(shard <= me, has_right)
        goes_left = jnp.logical_and(shard >= me, has_left)
        for count, to_right, to_left, to_other in (
            (chunks, q_right, q_left, q_across), (wo_chunks, o_right, o_left, o_across)
        ):
            @pl.loop(0, count)
            def _(c):
                @pl.when(goes_right)
                def _():
                    to_right(shard, c).wait_send()

                @pl.when(goes_left)
                def _():
                    to_left(shard, c).wait_send()

                @pl.when(shard != me)
                def _():
                    to_other(shard, c, y).wait_send()


def layer(hidden, wq, wo, seg_q, seg_k):
    n, narrow = lax.axis_size("wide"), lax.axis_size("narrow")
    tok, width = hidden.shape
    half = wq.shape[2] // 2
    chunks = max(1, wq.shape[1] // ROWS)
    wo_chunks = WO_CHUNKS
    cols = wo.shape[3]
    share = tok // narrow
    vmem = pl.BlockSpec(memory_space=pltpu.VMEM)
    hbm = pl.BlockSpec(memory_space=pl.ANY)
    dma = pltpu.SemaphoreType.DMA
    bf16 = jnp.bfloat16
    return pl.pallas_call(
        functools.partial(layer_kernel, n, narrow, chunks, wo_chunks),
        out_shape=jax.ShapeDtypeStruct((share, n * cols), bf16),
        in_specs=[vmem, hbm, hbm, vmem, vmem],
        out_specs=vmem,
        scratch_shapes=[
            pltpu.VMEM((2, 3, width, half), bf16),
            pltpu.VMEM((2, 3, tok, half), jnp.float32),
            pltpu.VMEM((n,) + wo.shape[1:], bf16),
            pltpu.VMEM((2, tok, half), bf16),
            pltpu.VMEM((2, 2, tok + SHIFT, half), bf16),
            pltpu.VMEM((tok, 2 * half), bf16),
            pltpu.VMEM((n, narrow, share, cols), bf16),
            pltpu.VMEM((n, narrow // 2, share, cols), bf16),
            pltpu.VMEM((n, narrow // 2, share, cols), bf16),
            pltpu.VMEM((n, max(1, narrow // 2 - 1), share, cols), bf16),
            dma((3,)),
        ]
        + [dma((n, chunks))] * 5
        + [dma((n, wo_chunks))] * 5
        + [dma((2,))]
        + [dma((n, narrow // 2))] * 2
        + [dma((n, max(1, narrow // 2 - 1)))] * 2,
        compiler_params=pltpu.CompilerParams(
            collective_id=0, has_side_effects=True, vmem_limit_bytes=58 * 1024 * 1024
        ),
    )(hidden, wq, wo, seg_q, seg_k)


def per_device(hidden, w_qkv, w_out, seg_ids, shift_heads):
    tok_rows = hidden.shape[0]
    local_f = w_qkv.shape[2]
    heads_here = local_f // HEAD_DIM
    blocks = tok_rows // SHIFT
    narrow = lax.axis_size("narrow")
    first_tok = lax.axis_index("wide") * tok_rows
    shifted = lax.dynamic_slice_in_dim(shift_heads, lax.axis_index("narrow") * heads_here, heads_here) > 0

    doubled = jnp.concatenate([seg_ids[-SHIFT:], seg_ids], 0)
    seg_here = lax.dynamic_slice_in_dim(doubled, first_tok, tok_rows + SHIFT)
    seg_q = seg_here[SHIFT:, None]
    windows = jnp.stack([seg_here[b * SHIFT : (b + 2) * SHIFT] for b in range(blocks)])
    odd = (jnp.arange(blocks) % 2 == 1)[None, :, None]
    reaches = (shifted[:, None, None] != odd) | (jnp.arange(2 * SHIFT) >= SHIFT)[None, None, :]
    seg_k = jnp.where(reaches, windows[None], -1)[:, :, None, :]

    wq = w_qkv.transpose(1, 0, 2)
    wo = w_out.reshape(narrow, 2, local_f // 2, -1)
    return layer(hidden, wq, wo, seg_q, seg_k)


def hub_kernel(
    row_chunks, direct,
    hidden_ref, wq_ref, wo_ref, seg_ref, shift_ref, out_ref,
    wbuf, hid, acc, q_buf, kv_buf, att, wo_buf, stage, early, seg_col,
    own_sem, sends, joint, he_r, hx_r, wm_r, we_r, wy_r, w0_r, kv_r, om_r, oe_r, od_r, ax_r, ae_r,
):
    n, narrow = lax.axis_size("wide"), lax.axis_size("narrow")
    me = lax.axis_index("wide")
    y = lax.axis_index("groups")
    spot = lax.axis_index("narrow")
    opp = 1 - y
    side = me // (n // 2)
    inner, outer = n // 2 - 1 + side, side * (n - 1)
    far_inner, far_outer = n - 1 - inner, n - 1 - outer
    is_inner, is_outer = me == inner, me == outer
    high, low = spot // 2, lax.rem(spot, 2)
    core_n, x_n = high * 2 + 1 - low, (1 - high) * 2 + low
    diag_n = (1 - high) * 2 + 1 - low
    depth = wq_ref.shape[1]
    tok = hidden_ref.shape[0]
    heads = wbuf.shape[0]
    chunks = 2 * row_chunks
    rows = depth // row_chunks
    wo_chunks = 8
    sub = wo_chunks // 4
    quarter = tok // narrow
    span = 2 * tok
    blocks = span // SHIFT
    own_pos = 1 - side
    own_row = pl.multiple_of(own_pos * tok, tok)
    far_row = pl.multiple_of(side * tok, tok)
    wo_half, wo_cols = wo_buf.shape[2], wo_buf.shape[3]
    wo_rows, wo_lanes = wo_half // (2 * sub), wo_cols // 2
    cols = wo_ref.shape[1]
    to_core, to_x, to_y = {"narrow": core_n}, {"narrow": x_n}, {"groups": opp}
    to_far, to_inner, to_outer = {"wide": far_inner}, {"wide": inner}, {"wide": outer}
    my_pos = jnp.where(is_inner, own_pos, side)

    def remote(src, dst, send, recv, device):
        return pltpu.make_async_remote_copy(
            src_ref=src, dst_ref=dst, send_sem=send, recv_sem=recv,
            device_id=device, device_id_type=MESH,
        )

    def arrived(place, ref):
        remote(ref, ref, sends.at[0], joint.at[place], to_core).wait_recv()

    def sent(place, ref):
        remote(ref, ref, sends.at[place], joint.at[0], to_core).wait_send()

    def w_at(shard, part, c):
        start = pl.multiple_of(shard * depth + lax.rem(c, row_chunks) * rows, rows)
        return wbuf.at[c // row_chunks * 2 + part, :, pl.ds(start, rows)]

    def wq_at(part, c):
        start = pl.multiple_of(lax.rem(c, row_chunks) * rows, rows)
        lane = pl.multiple_of((c // row_chunks * 2 + part) * HEAD_DIM, HEAD_DIM)
        return wq_ref.at[:, pl.ds(start, rows), pl.ds(lane, HEAD_DIM)]

    def o_at(shard, part, c):
        start = pl.multiple_of(lax.rem(c, 2 * sub) * wo_rows, wo_rows)
        lane = pl.multiple_of(c // (2 * sub) * wo_lanes, wo_lanes)
        return wo_buf.at[shard, part, pl.ds(start, wo_rows), pl.ds(lane, wo_lanes)]

    def wo_at(part, c):
        start = pl.multiple_of(part * wo_half + lax.rem(c, 2 * sub) * wo_rows, wo_rows)
        lane = pl.multiple_of(spot * wo_cols + c // (2 * sub) * wo_lanes, wo_lanes)
        return wo_ref.at[pl.ds(start, wo_rows), pl.ds(lane, wo_lanes)]

    def h_at(row_n, k):
        start = pl.multiple_of(far_row + row_n * quarter, quarter)
        return hid.at[pl.ds(start, quarter), pl.ds(pl.multiple_of(k * depth, depth), depth)]

    def h_end(k):
        src = hidden_ref.at[
            pl.ds(pl.multiple_of(spot * quarter, quarter), quarter), pl.ds(pl.multiple_of(k * depth, depth), depth)
        ]
        return remote(src, h_at(spot, k), sends.at[0], he_r.at[k], to_inner)

    def h_x(k, row_n):
        return remote(h_at(row_n, k), h_at(row_n, k), sends.at[0], hx_r.at[k], to_x)

    def h_core(k, row_n):
        return remote(h_at(row_n, k), h_at(row_n, k), sends.at[0], joint.at[0], to_core)

    def w_end(j, c):
        part = y if j == 0 else opp
        return remote(wq_at(part, c), w_at(outer, part, c), sends.at[1], we_r.at[j, c], to_inner)

    def w_mid_send(s, c):
        if s == 0:
            return remote(wq_at(y, c), w_at(inner, y, c), sends.at[1], wm_r.at[s, c], to_far)
        return remote(w_at(outer, y, c), w_at(outer, y, c), sends.at[1], wm_r.at[s, c], to_far)

    def far_shard(s):
        return jnp.where(s == 0, far_inner, far_outer)

    def w_mid_recv(s, c):
        ref = w_at(far_shard(s), y, c)
        return remote(ref, ref, sends.at[1], wm_r.at[s, c], to_far)

    def w_y(s, c, part):
        ref = w_at(far_shard(s), part, c)
        return remote(ref, ref, sends.at[1], wy_r.at[s, c], to_y)

    def w_y_outer(c, part):
        ref = w_at(outer, part, c)
        return remote(ref, ref, sends.at[2], w0_r.at[c], to_y)

    def o_end(j, c):
        part = y if j == 0 else opp
        return remote(wo_at(part, c), o_at(outer, part, c), sends.at[4], oe_r.at[c] if j == 0 else joint.at[4 + c // 4 * (1 + 7 * lax.rem(c // 2, 2))], to_inner)

    def o_mid_send(s, c):
        if s == 0:
            return remote(wo_at(y, c), o_at(inner, y, c), sends.at[4], om_r.at[s, c], to_far)
        return remote(o_at(outer, y, c), o_at(outer, y, c), sends.at[4], om_r.at[s, c], to_far)

    def o_mid_direct(c):
        ref = o_at(outer, opp, c)
        return remote(ref, ref, sends.at[4], joint.at[13], to_far)

    def o_mid_recv(s, c):
        ref = o_at(far_shard(s), y, c)
        return remote(ref, ref, sends.at[4], om_r.at[s, c], to_far)

    def o_down(c):
        return remote(wo_at(y, c), o_at(inner, y, c), sends.at[5], od_r.at[c], to_outer)

    def o_y(s, c, part):
        ref = o_at(inner if s == 2 else far_shard(s), part, c)
        place = (1, 2 + c // (2 * sub), 6)[s]
        return remote(ref, ref, sends.at[5 if s == 2 else 4], joint.at[place], to_y)

    def att_at(row_n, g, b):
        return att.at[row_n, g, pl.ds(pl.multiple_of(b * SHIFT, SHIFT), SHIFT)]

    def att_x(g, b, row_n):
        ref = att_at(row_n, g, b)
        return remote(ref, ref, sends.at[6], ax_r.at[g, b], to_x)

    def att_core(g, b, row_n):
        ref = att_at(row_n, g, b)
        return remote(ref, ref, sends.at[6], joint.at[8 + b], to_core)

    def att_end(g, b):
        ref = att_at(spot, g, b)
        return remote(ref, ref, sends.at[7], ae_r.at[g, b], to_outer)

    def share(g, b):
        att_x(g, b, spot).start()
        att_core(g, b, spot).start()

    def relay(g, b):
        att_x(g, b, x_n).wait_recv()
        att_core(g, b, x_n).start()

    def gathered(b):
        arrived(8 + b, att.at[pl.ds(0, narrow // 2), :, pl.ds(pl.multiple_of(b * SHIFT, SHIFT), SHIFT)])

    shards = (inner, far_inner, outer, far_outer)
    slots = ((0, 0, wo_cols), (1, 0, wo_cols)) + tuple((s, k * wo_lanes, wo_lanes) for s in (2, 3) for k in range(2))
    slots += ((2, 0, wo_cols),)

    def res_cols(slot, row_n):
        order, lane, size = slots[slot]
        return pl.ds(pl.multiple_of(shards[order] * cols + row_n * wo_cols + lane, size), size)

    def result(slot, pos, to_n):
        order, lane, size = slots[slot]
        return remote(
            stage.at[order, pl.ds(pl.multiple_of(pos * tok + to_n * quarter, quarter), quarter), lane : lane + size],
            out_ref.at[:, res_cols(slot, spot)],
            sends.at[8], joint.at[7],
            {"wide": side * (n // 2) + pos, "narrow": to_n},
        )

    def product(slot, b, firsts):
        order, lane, size = slots[slot]
        mine = pl.ds(pl.multiple_of(b * SHIFT, SHIFT), SHIFT)
        a_cols = att.shape[3]
        total = None
        for row_half in firsts:
            for p in range(narrow // 2):
                for g in range(2):
                    start = (p * 2 + g) * a_cols
                    term = jnp.dot(
                        att[row_half * (narrow // 2) + p, g, mine],
                        wo_buf[shards[order], row_half, start : start + a_cols, lane : lane + size],
                        preferred_element_type=jnp.float32,
                    )
                    total = term if total is None else total + term
        return total

    def emit(slot, b, total):
        order, lane, size = slots[slot]
        mine = pl.ds(pl.multiple_of(b * SHIFT, SHIFT), SHIFT)
        done = total.astype(jnp.bfloat16)
        stage[order, mine, lane : lane + size] = done
        pos = b // (blocks // 2)
        for k in range(SHIFT // quarter):
            to_n = lax.rem(b, blocks // 2) * (SHIFT // quarter) + k
            here = jnp.logical_and(pos == my_pos, spot == to_n)

            @pl.when(here)
            def _():
                out_ref[:, res_cols(slot, spot)] = done[k * quarter : (k + 1) * quarter]

            @pl.when(jnp.logical_not(here))
            def _():
                result(slot, pos, to_n).start()

    def multiply(slot, b):
        emit(slot, b, product(slot, b, (0, 1)))

    def kv_copy(g):
        return remote(
            kv_buf.at[pl.ds(2 * g, 2), :, pl.ds(span, SHIFT)], kv_buf.at[pl.ds(2 * g, 2), :, pl.ds(0, SHIFT)],
            sends.at[3], kv_r.at[g], to_far,
        )

    barrier = pltpu.get_barrier_semaphore()
    beside = [{"narrow": core_n}, {"narrow": x_n}, {"narrow": diag_n}, to_y]

    def greet(peers):
        for device in peers:
            pl.semaphore_signal(barrier, inc=1, device_id=device, device_id_type=MESH)
        pl.semaphore_wait(barrier, len(peers))

    def own_wo(h):
        return pltpu.make_async_copy(
            wo_ref.at[pl.ds(h * wo_half, wo_half), pl.ds(pl.multiple_of(spot * wo_cols, wo_cols), wo_cols)],
            wo_buf.at[me, h],
            own_sem.at[2 + h],
        )


    @pl.when(is_outer)
    def _():
        greet(beside + [{"wide": inner, "narrow": p} for p in range(narrow)])

        @pl.loop(0, n)
        def _(k):
            h_end(k).start()

        def each_end(act):
            @pl.loop(0, chunks)
            def _(c):
                act(w_end(0, c))

            @pl.loop(0, direct)
            def _(c):
                act(w_end(1, c))

            @pl.loop(row_chunks, chunks)
            def _(c):
                act(w_end(1, c))

            for j, from_c, to_c in ((0, 0, wo_chunks), (1, 6, 8), (1, 4, 6), (1, 0, 4)):
                @pl.loop(from_c, to_c)
                def _(c):
                    act(o_end(j, c))

        each_end(lambda copy: copy.start())
        for h in range(2):
            own_wo(h).start()

        @pl.loop(0, wo_chunks)
        def _(c):
            o_down(c).wait_recv()
            o_y(2, c, y).start()

        arrived(6, wo_buf.at[inner, opp])
        for h in range(2):
            own_wo(h).wait()

        def take(g, b):
            att_end(g, b).wait_recv()
            share(g, b)

        first_b, second_b = side + 1, 3 * side
        take(0, first_b)
        relay(0, first_b)
        take(0, second_b)
        relay(0, second_b)
        take(1, first_b)

        @pl.when(side == 1)
        def _():
            take(1, second_b)

        relay(1, first_b)

        @pl.when(side == 0)
        def _():
            take(1, second_b)

        gathered(first_b)
        multiply(0, first_b)
        multiply(6, first_b)
        relay(1, second_b)
        gathered(second_b)
        multiply(0, second_b)
        multiply(6, second_b)

        sent(0, hid.at[pl.ds(0, quarter)])
        sent(1, wbuf.at[0, :, pl.ds(0, (chunks + direct + row_chunks) * rows)])
        sent(4, wo_buf.at[0])
        sent(5, wo_buf.at[0, 0])
        sent(6, att.at[pl.ds(0, 3), 0])
        sent(8, stage.at[0, pl.ds(0, 2 * (narrow - 1) * quarter)])
        arrived(7, out_ref.at[:, pl.ds(0, (4 * narrow - 2) * wo_cols)])

    @pl.when(is_inner)
    def _():
        own = [
            pltpu.make_async_copy(
                wq_ref.at[:, :, pl.ds(h * HEAD_DIM, HEAD_DIM)],
                wbuf.at[h, :, pl.ds(pl.multiple_of(inner * depth, depth), depth)],
                own_sem.at[0],
            )
            for h in range(heads)
        ]
        own.append(pltpu.make_async_copy(hidden_ref, hid.at[pl.ds(own_row, tok)], own_sem.at[1]))
        for copy in own:
            copy.start()
        for h in range(2):
            own_wo(h).start()
        greet(beside + [to_far] + [{"wide": outer, "narrow": p} for p in range(narrow)])

        @pl.loop(0, chunks)
        def _(c):
            w_mid_send(0, c).start()

        @pl.loop(0, wo_chunks)
        def _(c):
            o_down(c).start()

        acc[...] = jnp.zeros_like(acc)
        seg_rows = seg_ref.shape[0]
        lanes = seg_ref.shape[1]
        seg_first = side * (span // lanes)
        for k in range(span // lanes):
            line = seg_ref[pl.ds(seg_first + k, 1), :]
            seg_col[k * lanes : (k + 1) * lanes, :] = jnp.broadcast_to(line, (lanes, lanes)).T

        def add(row, size, shard, part, c):
            start = pl.multiple_of(shard * depth + lax.rem(c, row_chunks) * rows, rows)
            head = c // row_chunks * 2 + part
            here = pl.ds(row, size)
            piece = hid[here, pl.ds(start, rows)]
            both = jnp.concatenate([wbuf[head, i, pl.ds(start, rows)] for i in range(2)], axis=1)
            found = jnp.dot(piece, both, preferred_element_type=jnp.float32)
            acc[head, 0, here] += found[:, :HEAD_DIM]
            acc[head, 1, here] += found[:, HEAD_DIM:]
            acc[head, 2, here] += jnp.dot(piece, wbuf[head, 2, pl.ds(start, rows)], preferred_element_type=jnp.float32)

        def add_all(shard, part, c):
            add(0, span, shard, part, c)

        def add_at(t, shard, part, c):
            @pl.when(t < chunks)
            def _():
                add(own_row, tok, shard, part, c)

            @pl.when(t >= chunks)
            def _():
                add_all(shard, part, c)

        pltpu.make_async_copy(
            wbuf.at[:, :, pl.ds(0, depth)],
            wbuf.at[:, :, pl.ds(pl.multiple_of(inner * depth, depth), depth)],
            own_sem.at[0],
        ).wait()
        own[heads].wait()

        @pl.loop(0, 2 * chunks)
        def _(u):
            add(own_row, tok, inner, u // chunks, lax.rem(u, chunks))

        def own_mid(first, last):
            @pl.loop(first, last)
            def _(c):
                o_mid_send(0, c).start()

        lag = row_chunks
        lead = chunks - 2
        catch_up = 4 * chunks - lag

        @pl.loop(0, 2 * chunks)
        def _(t):
            s, c = t // chunks, lax.rem(t, chunks)
            q = t - lead

            @pl.when(jnp.logical_and(q >= 0, q < chunks))
            def _():
                w_end(0, q).wait_recv()
                w_mid_send(1, q).start()

            @pl.when(jnp.logical_and(q >= direct, q < row_chunks))
            def _():
                w_y_outer(q, y).start()

            w_mid_recv(s, c).wait_recv()
            w_y(s, c, y).start()

            @pl.when(jnp.logical_and(t >= 1, t < 1 + n))
            def _():
                h_end(t - 1).wait_recv()
                h_x(t - 1, spot).start()
                h_core(t - 1, spot).start()

            @pl.when(jnp.logical_and(t >= 4, t < 4 + n))
            def _():
                h_x(t - 4, x_n).wait_recv()
                h_core(t - 4, x_n).start()

            @pl.when(t == chunks)
            def _():
                arrived(0, hid.at[pl.ds(far_row, narrow // 2 * quarter)])

            @pl.when(t == lead + chunks)
            def _():
                own_mid(0, 2)

            add_at(t, far_shard(s), y, c)

            @pl.when(t >= lag)
            def _():
                v = t - lag
                w_y(v // chunks, lax.rem(v, chunks), opp).wait_recv()
                add_at(t, far_shard(v // chunks), opp, lax.rem(v, chunks))

            @pl.when(t >= chunks)
            def _():
                add_all(outer, y, t - chunks)
                u0 = 4 * (t - chunks)

                @pl.loop(u0, jnp.minimum(u0 + 4, catch_up))
                def _(u):
                    turn = u // row_chunks
                    near = lax.rem(turn, 4) < 2
                    part = jnp.where(near, lax.rem(turn, 2), jnp.where(lax.rem(turn, 2) == 0, y, opp))
                    c = lax.rem(u, row_chunks) + turn // 4 * row_chunks
                    add(far_row, tok, jnp.where(near, inner, far_inner), part, c)

            @pl.when(t >= chunks + row_chunks)
            def _():
                k = lax.rem(t - chunks - row_chunks + direct, row_chunks)

                @pl.when(k < direct)
                def _():
                    w_end(1, k).wait_recv()

                @pl.when(k >= direct)
                def _():
                    w_y_outer(k, opp).wait_recv()

                add_all(outer, opp, k)

        causal = lax.broadcasted_iota(jnp.int32, (SHIFT, 2 * SHIFT), 1) <= (
            lax.broadcasted_iota(jnp.int32, (SHIFT, 2 * SHIFT), 0) + SHIFT
        )
        per_block = SHIFT // lanes

        def seg_line(b):
            at = [lax.rem(seg_first + b * per_block + k + seg_rows, seg_rows) for k in range(per_block)]
            return jnp.concatenate([seg_ref[pl.ds(i, 1), :] for i in at], axis=1)

        def attend(g, b):
            mine, seen = slice(b * SHIFT, (b + 1) * SHIFT), slice(b * SHIFT, (b + 2) * SHIFT)
            seg_q = jnp.concatenate([seg_col[mine, :]] * (2 * per_block), axis=1)
            near, prior = seg_line(b), seg_line(b - 1)
            for k in range(2):
                h = 2 * g + k
                reach = shift_ref[spot * heads + h]
                if b % 2 == 1:
                    reach = 1 - reach
                seg_k = jnp.concatenate([prior * reach + (reach - 1), near], axis=1)
                scores = lax.dot_general(
                    q_buf[h, mine], kv_buf[h, 0, seen], (((1,), (1,)), ((), ())),
                    preferred_element_type=jnp.float32,
                ) * (1.0 / math.sqrt(HEAD_DIM))
                allowed = causal & (seg_q == seg_k)
                scores = jnp.where(allowed, scores, masked_out)
                exponent = jnp.exp(scores - jnp.max(scores, axis=-1, keepdims=True))
                weights = exponent / jnp.sum(exponent, axis=-1, keepdims=True)
                att[spot, g, mine, k * HEAD_DIM : (k + 1) * HEAD_DIM] = jnp.dot(
                    weights.astype(jnp.bfloat16), kv_buf[h, 1, seen], preferred_element_type=jnp.float32
                ).astype(jnp.bfloat16)
            share(g, b)

            @pl.when(b // (blocks // 2) == side)
            def _():
                att_end(g, b).start()

        def settle(g):
            for h in (2 * g, 2 * g + 1):
                for i in range(2):
                    kv_buf[h, i, SHIFT:] = acc[h, 1 + i].astype(jnp.bfloat16)
            kv_copy(g).start()
            for h in (2 * g, 2 * g + 1):
                q_buf[h] = acc[h, 0].astype(jnp.bfloat16)

        def multiply_these(slot, first, count):
            @pl.loop(0, count)
            def _(k):
                multiply(slot, lax.rem(first + k, blocks))

        def multiply_own(slot, b):
            @pl.when(b // (blocks // 2) == own_pos)
            def _():
                multiply(slot, b)

        def relay_wo(arrival, *onward):
            def act(i, count):
                @pl.loop(i, i + count)
                def _(c):
                    arrival(c).wait_recv()
                    for copy in onward:
                        copy(c).start()

            return act

        near_wo = relay_wo(lambda c: o_mid_recv(0, c), lambda c: o_y(0, c, y))
        far_wo = relay_wo(lambda c: o_mid_recv(1, c), lambda c: o_y(1, c, y))
        pass_wo = relay_wo(lambda c: o_end(0, c), lambda c: o_mid_send(1, c))

        def half_of(shard, lane_half):
            return wo_buf.at[shard, opp, :, lane_half * wo_lanes : (lane_half + 1) * wo_lanes]

        def corner(shard, row):
            return wo_buf.at[shard, opp, row * 2 * wo_rows : (row + 1) * 2 * wo_rows, wo_lanes:]

        def last_y(c):
            w_y(1, c, opp).wait_recv()
            add_all(far_outer, opp, c)

        def last_end(c):
            w_end(1, c).wait_recv()
            add_all(outer, opp, c)

        settle(0)
        own_mid(2, 7)
        attend(0, 1)
        last_y(row_chunks)
        attend(0, 2)
        last_y(row_chunks + 1)
        attend(0, 3)

        @pl.loop(row_chunks, chunks - 2)
        def _(c):
            last_end(c)

        relay(0, 1)
        kv_copy(0).wait_recv()
        attend(0, 0)
        relay(0, 2)
        last_y(row_chunks + 2)
        last_end(chunks - 2)
        relay(0, 3)
        last_end(chunks - 1)
        near_wo(0, 2)
        last_y(row_chunks + 3)
        settle(1)
        near_wo(2, 2)
        own_mid(7, 8)
        attend(1, 1)
        near_wo(4, 2)
        attend(1, 2)
        relay(0, 0)
        pass_wo(0, 2)
        attend(1, 3)
        near_wo(6, 1)
        for h in range(2):
            own_wo(h).wait()
        pass_wo(2, 2)
        relay(1, 1)
        gathered(1)
        multiply_own(0, 1)
        pass_wo(4, 2)
        kv_copy(1).wait_recv()
        attend(1, 0)
        near_wo(7, 1)
        pass_wo(6, 2)
        relay(1, 2)
        gathered(2)
        multiply_own(0, 2)
        far_wo(0, 2)
        relay(1, 3)
        gathered(3)
        multiply_own(0, 3)
        arrived(1, wo_buf.at[far_inner, opp])
        multiply(1, side + 1)
        far_wo(2, 1)
        relay(1, 0)
        multiply(1, 3)
        far_wo(3, 2)
        gathered(0)
        arrived(12, corner(outer, 1))
        for c in range(wo_chunks - 2, wo_chunks):
            o_mid_direct(c).start()
        multiply(1, 0)
        far_wo(5, 1)
        multiply(1, own_pos + 1)
        multiply_own(0, 0)
        first = side * (blocks // 2)
        arrived(5, corner(outer, 0))
        multiply_these(3, own_pos * (blocks // 2), blocks // 2)
        arrived(2, half_of(far_outer, 0))
        multiply_these(4, first, blocks)
        for c in range(wo_chunks - 2, wo_chunks):
            o_mid_recv(1, c).wait_recv()

        @pl.loop(0, blocks)
        def _(b):
            early[b] = product(5, b, (y,))

        arrived(3, corner(far_outer, 0))
        arrived(13, corner(far_outer, 1))

        def last_piece(begin):
            @pl.loop(0, blocks // 2)
            def _(turn):
                b = begin + turn
                emit(5, b, early[b] + product(5, b, (opp,)))

        last_piece(first)
        arrived(4, half_of(outer, 0))
        multiply_these(2, own_pos * (blocks // 2), blocks // 2)
        last_piece(own_pos * (blocks // 2))

        sent(0, hid.at[pl.ds(0, 3 * quarter)])
        sent(1, wbuf.at[pl.ds(0, 2)])
        sent(2, wbuf.at[0, :, pl.ds(0, (row_chunks - direct) * rows)])
        sent(3, kv_buf.at[:, :, pl.ds(0, SHIFT)])
        sent(4, wo_buf.at[pl.ds(0, 2)])
        sent(5, wo_buf.at[0, 0])
        sent(6, att.at[pl.ds(0, 3)])
        sent(7, att.at[0, 0])
        pieces = 4 * (narrow - 1) + 2 * narrow
        sent(8, hid.at[pl.ds(0, pieces * quarter * wo_cols // hid.shape[1])])
        arrived(7, out_ref.at[:, pl.ds(0, 4 * (narrow - 1) * wo_cols)])


def hub_layer(hidden, wq, wo, seg, shift_heads):
    n, narrow = lax.axis_size("wide"), lax.axis_size("narrow")
    tok, width = hidden.shape
    heads = wq.shape[2] // HEAD_DIM
    row_chunks = wq.shape[1] // HUB_ROWS
    chunks, wo_chunks = 2 * row_chunks, 8
    cols = wo.shape[1]
    wo_half, wo_cols = wo.shape[0] // 2, cols // narrow
    quarter, span = tok // narrow, 2 * tok
    blocks = span // SHIFT
    vmem = pl.BlockSpec(memory_space=pltpu.VMEM)
    smem = pl.BlockSpec(memory_space=pltpu.SMEM)
    hbm = pl.BlockSpec(memory_space=pl.ANY)
    dma = pltpu.SemaphoreType.DMA
    bf16 = jnp.bfloat16
    return pl.pallas_call(
        functools.partial(hub_kernel, row_chunks, DIRECT),
        out_shape=pltpu.VMEM((quarter, n * cols), bf16),
        in_specs=[hbm, hbm, hbm, vmem, smem],
        out_specs=vmem,
        scratch_shapes=[
            pltpu.VMEM((heads, 3, width, HEAD_DIM), bf16),
            pltpu.VMEM((span, width), bf16),
            pltpu.VMEM((heads, 3, span, HEAD_DIM), jnp.float32),
            pltpu.VMEM((heads, span, HEAD_DIM), bf16),
            pltpu.VMEM((heads, 2, span + SHIFT, HEAD_DIM), bf16),
            pltpu.VMEM((narrow, 2, span, 2 * HEAD_DIM), bf16),
            pltpu.VMEM((n, 2, wo_half, wo_cols), bf16),
            pltpu.VMEM((n, span, wo_cols), bf16),
            pltpu.VMEM((blocks, SHIFT, wo_cols // 2), jnp.float32),
            pltpu.VMEM((span, seg.shape[1]), jnp.int32),
            dma((4,)),
            dma((9,)),
            dma((10 + blocks,)),
        ]
        + [dma((n,))] * 2
        + [dma((2, chunks))] * 3
        + [dma((row_chunks,)), dma((2,)), dma((2, wo_chunks)), dma((wo_chunks,)), dma((wo_chunks,))]
        + [dma((2, blocks))] * 2,
        compiler_params=pltpu.CompilerParams(
            collective_id=0, has_side_effects=True, vmem_limit_bytes=58 * 1024 * 1024
        ),
    )(hidden, wq, wo, seg, shift_heads)


def hub_per_device(hidden, w_qkv, w_out, seg_ids, shift_heads):
    return hub_layer(hidden, w_qkv.transpose(1, 0, 2), w_out, seg_ids.reshape(-1, 128), shift_heads)


def solution(mesh):
    placed = (
        P(("groups", "wide"), None),
        P("wide", None, "narrow"),
        P(None, "wide"),
        P("groups"),
        P(),
    )
    shape = mesh.shape
    hub = shape["groups"] == 2 and shape["wide"] == 4 and shape["narrow"] == 4
    return jax.shard_map(
        hub_per_device if hub else per_device,
        mesh=mesh,
        in_specs=placed,
        out_specs=P(("groups", "wide", "narrow"), None),
        check_vma=False,
    )
```

```python
import functools
import math

import jax
import jax.numpy as jnp
from jax import lax
from jax.experimental import pallas as pl
from jax.experimental.pallas import tpu as pltpu
from jax.sharding import PartitionSpec as P

HEAD_DIM = 128
GROUP = 512
SHIFT = 256

masked_out = -1e30
MESH = pl.DeviceIdType.MESH
ROWS = 128
WO_CHUNKS = 4
HUB_ROWS = 256
DIRECT = 2


def layer_kernel(
    n, narrow, chunks, wo_chunks,
    hidden_ref, wq_ref, wo_ref, segq_ref, segk_ref, out_ref,
    wbuf, acc, wo_buf, q_buf, kv_buf, att, part, pair_in, pair_sum, far_in,
    own_sem,
    qs_r, qs_l, qr, qs_y, qr_y,
    os_r, os_l, o_r, os_y, or_y,
    kv_sem, pair_s, pair_r, far_s, far_r,
):
    me = lax.axis_index("wide")
    y = lax.axis_index("groups")
    spot = lax.axis_index("narrow")
    other = 1 - y
    across_n = narrow // 2
    high, low = spot // 2, lax.rem(spot, 2)
    depth = wq_ref.shape[1]
    half = wbuf.shape[3]
    tok = hidden_ref.shape[0]
    rows = depth // chunks
    steps = (n - 1) * chunks
    wo_rows = wo_buf.shape[2] // wo_chunks
    cols = wo_buf.shape[3]
    blocks = tok // SHIFT
    per_half = half // HEAD_DIM
    has_left, has_right = me > 0, me < n - 1
    right, left = {"wide": me + 1}, {"wide": me - 1}
    after, before = {"wide": lax.rem(me + 1, n)}, {"wide": lax.rem(me + n - 1, n)}
    opposite = {"groups": other}
    pair = {"narrow": high * 2 + 1 - low}
    far = [{"narrow": lax.rem(high + d, across_n) * 2 + low} for d in range(1, across_n)]
    far_from = [{"narrow": lax.rem(high + across_n - d, across_n) * 2 + low} for d in range(1, across_n)]

    barrier = pltpu.get_barrier_semaphore()
    greeted = [after, before, opposite, pair] + far
    for device in greeted:
        pl.semaphore_signal(barrier, inc=1, device_id=device, device_id_type=MESH)

    def w_at(shard, part_of, c):
        start = pl.multiple_of(shard * depth + c * rows, rows)
        return wbuf.at[part_of, :, pl.ds(start, rows)]

    def wq_own(c):
        return wq_ref.at[
            :, pl.ds(pl.multiple_of(c * rows, rows), rows), pl.ds(pl.multiple_of(y * half, half), half)
        ]

    def o_at(shard, part_of, c):
        return wo_buf.at[shard, part_of, pl.ds(pl.multiple_of(c * wo_rows, wo_rows), wo_rows)]

    def wo_own(c):
        return wo_ref.at[spot, y, pl.ds(pl.multiple_of(c * wo_rows, wo_rows), wo_rows)]

    def remote(src, dst, send, recv, device):
        return pltpu.make_async_remote_copy(
            src_ref=src, dst_ref=dst, send_sem=send, recv_sem=recv,
            device_id=device, device_id_type=MESH,
        )

    def q_right(shard, c, src=None):
        dst = w_at(shard, y, c)
        return remote(dst if src is None else src, dst, qs_r.at[shard, c], qr.at[shard, c], right)

    def q_left(shard, c, src=None):
        dst = w_at(shard, y, c)
        return remote(dst if src is None else src, dst, qs_l.at[shard, c], qr.at[shard, c], left)

    def q_across(shard, c, part_of):
        ref = w_at(shard, part_of, c)
        return remote(ref, ref, qs_y.at[shard, c], qr_y.at[shard, c], opposite)

    def o_right(shard, c, src=None):
        dst = o_at(shard, y, c)
        return remote(dst if src is None else src, dst, os_r.at[shard, c], o_r.at[shard, c], right)

    def o_left(shard, c, src=None):
        dst = o_at(shard, y, c)
        return remote(dst if src is None else src, dst, os_l.at[shard, c], o_r.at[shard, c], left)

    def o_across(shard, c, part_of):
        ref = o_at(shard, part_of, c)
        return remote(ref, ref, os_y.at[shard, c], or_y.at[shard, c], opposite)

    own = [
        pltpu.make_async_copy(
            wq_ref.at[:, :, pl.ds(h * half, half)],
            wbuf.at[h, :, pl.ds(pl.multiple_of(me * depth, depth), depth)],
            own_sem.at[h],
        )
        for h in range(2)
    ]
    own.append(pltpu.make_async_copy(wo_ref.at[spot], wo_buf.at[me], own_sem.at[2]))
    for copy in own:
        copy.start()
    pl.semaphore_wait(barrier, len(greeted))

    @pl.loop(0, chunks)
    def _(c):
        @pl.when(has_right)
        def _():
            q_right(me, c, wq_own(c)).start()

        @pl.when(has_left)
        def _():
            q_left(me, c, wq_own(c)).start()

    acc[...] = jnp.zeros_like(acc)
    own[0].wait()
    own[1].wait()

    def add(shard, part_of, c):
        start = pl.multiple_of(shard * depth + c * rows, rows)
        piece = hidden_ref[:, pl.ds(start, rows)]
        for i in range(3):
            acc[part_of, i] += jnp.dot(
                piece, wbuf[part_of, i, pl.ds(start, rows)], preferred_element_type=jnp.float32
            )

    @pl.loop(0, 2 * chunks)
    def _(i):
        add(me, i // chunks, lax.rem(i, chunks))

    def add_across(t):
        s, c = t // chunks, lax.rem(t, chunks)
        for there, shard in ((me - 1 - s >= 0, me - 1 - s), (me + 1 + s <= n - 1, me + 1 + s)):
            @pl.when(there)
            def _():
                q_across(shard, c, other).wait_recv()
                add(shard, other, c)

    def send_own_wo():
        @pl.loop(0, wo_chunks)
        def _(c):
            @pl.when(has_right)
            def _():
                o_right(me, c, wo_own(c)).start()

            @pl.when(has_left)
            def _():
                o_left(me, c, wo_own(c)).start()

    @pl.loop(0, steps)
    def _(t):
        s, c = t // chunks, lax.rem(t, chunks)

        @pl.when(t == steps - chunks)
        def _():
            send_own_wo()

        @pl.when(me - 1 - s >= 0)
        def _():
            q_right(me - 1 - s, c).wait_recv()

            @pl.when(has_right)
            def _():
                q_right(me - 1 - s, c).start()

            q_across(me - 1 - s, c, y).start()

        @pl.when(me + 1 + s <= n - 1)
        def _():
            q_left(me + 1 + s, c).wait_recv()

            @pl.when(has_left)
            def _():
                q_left(me + 1 + s, c).start()

            q_across(me + 1 + s, c, y).start()

        for there, shard in ((me - 1 - s >= 0, me - 1 - s), (me + 1 + s <= n - 1, me + 1 + s)):
            @pl.when(there)
            def _():
                add(shard, y, c)

        @pl.when(t > 0)
        def _():
            add_across(t - 1)

    add_across(steps - 1)
    for h in range(2):
        q_buf[h] = acc[h, 0].astype(jnp.bfloat16)
        for i in range(2):
            kv_buf[h, i, SHIFT:] = acc[h, 1 + i].astype(jnp.bfloat16)

    kv_copy = remote(
        kv_buf.at[:, :, pl.ds(tok, SHIFT)], kv_buf.at[:, :, pl.ds(0, SHIFT)],
        kv_sem.at[0], kv_sem.at[1], after,
    )
    kv_copy.start()

    causal = lax.broadcasted_iota(jnp.int32, (SHIFT, 2 * SHIFT), 1) <= (
        lax.broadcasted_iota(jnp.int32, (SHIFT, 2 * SHIFT), 0) + SHIFT
    )

    def attend(h, b):
        lanes = slice((h % per_half) * HEAD_DIM, (h % per_half + 1) * HEAD_DIM)
        mine, seen = slice(b * SHIFT, (b + 1) * SHIFT), slice(b * SHIFT, (b + 2) * SHIFT)
        keys, values = kv_buf.at[h // per_half, 0], kv_buf.at[h // per_half, 1]
        scores = lax.dot_general(
            q_buf[h // per_half, mine, lanes], keys[seen, lanes], (((1,), (1,)), ((), ())),
            preferred_element_type=jnp.float32,
        ) * (1.0 / math.sqrt(HEAD_DIM))
        allowed = causal & (segq_ref[mine, :] == segk_ref[h, b])
        scores = jnp.where(allowed, scores, masked_out)
        exponent = jnp.exp(scores - jnp.max(scores, axis=-1, keepdims=True))
        weights = exponent / jnp.sum(exponent, axis=-1, keepdims=True)
        att[mine, h * HEAD_DIM : (h + 1) * HEAD_DIM] = jnp.dot(
            weights.astype(jnp.bfloat16), values[seen, lanes], preferred_element_type=jnp.float32
        ).astype(jnp.bfloat16)

    least = jnp.minimum(me, n - 1 - me)

    def block_of(k):
        turn = (k + 1) // 2
        near = jnp.where(lax.rem(k, 2) == 1, me - turn, me + turn)
        rest = jnp.where(me > least, me - (k - least), me + (k - least))
        return jnp.where(k <= 2 * least, near, rest)

    def pass_on(k):
        shard = block_of(k)

        @pl.loop(0, wo_chunks)
        def _(c):
            o_right(shard, c).wait_recv()

            @pl.when(jnp.logical_and(shard < me, has_right))
            def _():
                o_right(shard, c).start()

            @pl.when(jnp.logical_and(shard > me, has_left))
            def _():
                o_left(shard, c).start()

            o_across(shard, c, y).start()

    def pair_copy(shard, a):
        return remote(
            part.at[shard, a * 2 + 1 - low], pair_in.at[shard, a],
            pair_s.at[shard, a], pair_r.at[shard, a], pair,
        )

    def far_copy(shard, d):
        a = lax.rem(high + d, across_n)
        return remote(
            pair_sum.at[shard, a], far_in.at[shard, d - 1],
            far_s.at[shard, d - 1], far_r.at[shard, d - 1], far[d - 1],
        )

    def far_arrival(shard, d):
        return remote(
            pair_sum.at[shard, high], far_in.at[shard, d - 1],
            far_s.at[shard, d - 1], far_r.at[shard, d - 1], far_from[d - 1],
        )

    def multiply(k):
        shard = block_of(k)
        width = att.shape[1] // 2
        share = tok // narrow
        for p in range(narrow):
            a_rows = att[p * share : (p + 1) * share, :]
            total = jnp.dot(a_rows[:, :width], wo_buf[shard, 0], preferred_element_type=jnp.float32)
            total += jnp.dot(a_rows[:, width:], wo_buf[shard, 1], preferred_element_type=jnp.float32)
            part[shard, p] = total.astype(jnp.bfloat16)
        for a in range(across_n):
            pair_copy(shard, a).start()

    def sum_pair(k):
        shard = block_of(k)
        for a in range(across_n):
            pair_copy(shard, a).wait_recv()
            total = part[shard, a * 2 + low].astype(jnp.float32) + pair_in[shard, a].astype(jnp.float32)
            pair_sum[shard, a] = total.astype(jnp.bfloat16)
        for d in range(1, across_n):
            far_copy(shard, d).start()

    def finish(k):
        shard = block_of(k)
        total = part[shard, high * 2 + low].astype(jnp.float32) + pair_in[shard, high].astype(jnp.float32)
        for d in range(1, across_n):
            far_arrival(shard, d).wait_recv()
            total += far_in[shard, d - 1].astype(jnp.float32)
        out_ref[:, pl.ds(pl.multiple_of(shard * cols, cols), cols)] = total.astype(out_ref.dtype)

    heads = 2 * per_half
    for b in range(1, blocks):
        for h in range(heads):
            attend(h, b)
    pass_on(1)
    pass_on(2)
    kv_copy.wait_recv()
    for h in range(heads):
        attend(h, 0)
    own[2].wait()
    multiply(0)

    @pl.loop(1, n)
    def _(k):
        @pl.when(k > 2)
        def _():
            pass_on(k)

        sum_pair(k - 1)

        @pl.when(k > 1)
        def _():
            finish(k - 2)

        shard = block_of(k)

        @pl.loop(0, wo_chunks)
        def _(c):
            o_across(shard, c, other).wait_recv()

        multiply(k)

    sum_pair(n - 1)
    finish(n - 2)
    finish(n - 1)

    kv_copy.wait_send()

    @pl.loop(0, n)
    def _(shard):
        for a in range(across_n):
            pair_copy(shard, a).wait_send()
        for d in range(1, across_n):
            far_copy(shard, d).wait_send()
        goes_right = jnp.logical_and(shard <= me, has_right)
        goes_left = jnp.logical_and(shard >= me, has_left)
        for count, to_right, to_left, to_other in (
            (chunks, q_right, q_left, q_across), (wo_chunks, o_right, o_left, o_across)
        ):
            @pl.loop(0, count)
            def _(c):
                @pl.when(goes_right)
                def _():
                    to_right(shard, c).wait_send()

                @pl.when(goes_left)
                def _():
                    to_left(shard, c).wait_send()

                @pl.when(shard != me)
                def _():
                    to_other(shard, c, y).wait_send()


def layer(hidden, wq, wo, seg_q, seg_k):
    n, narrow = lax.axis_size("wide"), lax.axis_size("narrow")
    tok, width = hidden.shape
    half = wq.shape[2] // 2
    chunks = max(1, wq.shape[1] // ROWS)
    wo_chunks = WO_CHUNKS
    cols = wo.shape[3]
    share = tok // narrow
    vmem = pl.BlockSpec(memory_space=pltpu.VMEM)
    hbm = pl.BlockSpec(memory_space=pl.ANY)
    dma = pltpu.SemaphoreType.DMA
    bf16 = jnp.bfloat16
    return pl.pallas_call(
        functools.partial(layer_kernel, n, narrow, chunks, wo_chunks),
        out_shape=jax.ShapeDtypeStruct((share, n * cols), bf16),
        in_specs=[vmem, hbm, hbm, vmem, vmem],
        out_specs=vmem,
        scratch_shapes=[
            pltpu.VMEM((2, 3, width, half), bf16),
            pltpu.VMEM((2, 3, tok, half), jnp.float32),
            pltpu.VMEM((n,) + wo.shape[1:], bf16),
            pltpu.VMEM((2, tok, half), bf16),
            pltpu.VMEM((2, 2, tok + SHIFT, half), bf16),
            pltpu.VMEM((tok, 2 * half), bf16),
            pltpu.VMEM((n, narrow, share, cols), bf16),
            pltpu.VMEM((n, narrow // 2, share, cols), bf16),
            pltpu.VMEM((n, narrow // 2, share, cols), bf16),
            pltpu.VMEM((n, max(1, narrow // 2 - 1), share, cols), bf16),
            dma((3,)),
        ]
        + [dma((n, chunks))] * 5
        + [dma((n, wo_chunks))] * 5
        + [dma((2,))]
        + [dma((n, narrow // 2))] * 2
        + [dma((n, max(1, narrow // 2 - 1)))] * 2,
        compiler_params=pltpu.CompilerParams(
            collective_id=0, has_side_effects=True, vmem_limit_bytes=58 * 1024 * 1024
        ),
    )(hidden, wq, wo, seg_q, seg_k)


def per_device(hidden, w_qkv, w_out, seg_ids, shift_heads):
    tok_rows = hidden.shape[0]
    local_f = w_qkv.shape[2]
    heads_here = local_f // HEAD_DIM
    blocks = tok_rows // SHIFT
    narrow = lax.axis_size("narrow")
    first_tok = lax.axis_index("wide") * tok_rows
    shifted = lax.dynamic_slice_in_dim(shift_heads, lax.axis_index("narrow") * heads_here, heads_here) > 0

    doubled = jnp.concatenate([seg_ids[-SHIFT:], seg_ids], 0)
    seg_here = lax.dynamic_slice_in_dim(doubled, first_tok, tok_rows + SHIFT)
    seg_q = seg_here[SHIFT:, None]
    windows = jnp.stack([seg_here[b * SHIFT : (b + 2) * SHIFT] for b in range(blocks)])
    odd = (jnp.arange(blocks) % 2 == 1)[None, :, None]
    reaches = (shifted[:, None, None] != odd) | (jnp.arange(2 * SHIFT) >= SHIFT)[None, None, :]
    seg_k = jnp.where(reaches, windows[None], -1)[:, :, None, :]

    wq = w_qkv.transpose(1, 0, 2)
    wo = w_out.reshape(narrow, 2, local_f // 2, -1)
    return layer(hidden, wq, wo, seg_q, seg_k)


def hub_kernel(
    row_chunks, direct,
    hidden_ref, wq_ref, wo_ref, seg_hbm, shift_hbm, out_ref,
    wbuf, hid, acc, q_buf, kv_buf, att, wo_buf, stage, early, seg_col, seg_ref, shift_ref,
    own_sem, sends, joint, he_r, hx_r, wm_r, we_r, wy_r, w0_r, kv_r, om_r, oe_r, od_r, ax_r, ae_r,
):
    n, narrow = lax.axis_size("wide"), lax.axis_size("narrow")
    me = lax.axis_index("wide")
    y = lax.axis_index("groups")
    spot = lax.axis_index("narrow")
    opp = 1 - y
    side = me // (n // 2)
    inner, outer = n // 2 - 1 + side, side * (n - 1)
    far_inner, far_outer = n - 1 - inner, n - 1 - outer
    is_inner, is_outer = me == inner, me == outer
    high, low = spot // 2, lax.rem(spot, 2)
    core_n, x_n = high * 2 + 1 - low, (1 - high) * 2 + low
    diag_n = (1 - high) * 2 + 1 - low
    depth = wq_ref.shape[1]
    tok = hidden_ref.shape[0]
    heads = wbuf.shape[0]
    chunks = 2 * row_chunks
    rows = depth // row_chunks
    wo_chunks = 8
    sub = wo_chunks // 4
    quarter = tok // narrow
    span = 2 * tok
    blocks = span // SHIFT
    own_pos = 1 - side
    own_row = pl.multiple_of(own_pos * tok, tok)
    far_row = pl.multiple_of(side * tok, tok)
    wo_half, wo_cols = wo_buf.shape[2], wo_buf.shape[3]
    wo_rows, wo_lanes = wo_half // (2 * sub), wo_cols // 2
    cols = wo_ref.shape[1]
    to_core, to_x, to_y = {"narrow": core_n}, {"narrow": x_n}, {"groups": opp}
    to_far, to_inner, to_outer = {"wide": far_inner}, {"wide": inner}, {"wide": outer}
    my_pos = jnp.where(is_inner, own_pos, side)

    def remote(src, dst, send, recv, device):
        return pltpu.make_async_remote_copy(
            src_ref=src, dst_ref=dst, send_sem=send, recv_sem=recv,
            device_id=device, device_id_type=MESH,
        )

    def arrived(place, ref):
        remote(ref, ref, sends.at[0], joint.at[place], to_core).wait_recv()

    def sent(place, ref):
        remote(ref, ref, sends.at[place], joint.at[0], to_core).wait_send()

    def w_at(shard, part, c):
        start = pl.multiple_of(shard * depth + lax.rem(c, row_chunks) * rows, rows)
        return wbuf.at[c // row_chunks * 2 + part, :, pl.ds(start, rows)]

    def wq_at(part, c):
        start = pl.multiple_of(lax.rem(c, row_chunks) * rows, rows)
        lane = pl.multiple_of((c // row_chunks * 2 + part) * HEAD_DIM, HEAD_DIM)
        return wq_ref.at[:, pl.ds(start, rows), pl.ds(lane, HEAD_DIM)]

    def o_at(shard, part, c):
        start = pl.multiple_of(lax.rem(c, 2 * sub) * wo_rows, wo_rows)
        lane = pl.multiple_of(c // (2 * sub) * wo_lanes, wo_lanes)
        return wo_buf.at[shard, part, pl.ds(start, wo_rows), pl.ds(lane, wo_lanes)]

    def wo_at(part, c):
        start = pl.multiple_of(part * wo_half + lax.rem(c, 2 * sub) * wo_rows, wo_rows)
        lane = pl.multiple_of(spot * wo_cols + c // (2 * sub) * wo_lanes, wo_lanes)
        return wo_ref.at[pl.ds(start, wo_rows), pl.ds(lane, wo_lanes)]

    def h_at(row_n, k):
        start = pl.multiple_of(far_row + row_n * quarter, quarter)
        return hid.at[pl.ds(start, quarter), pl.ds(pl.multiple_of(k * depth, depth), depth)]

    def h_end(k):
        src = hidden_ref.at[
            pl.ds(pl.multiple_of(spot * quarter, quarter), quarter), pl.ds(pl.multiple_of(k * depth, depth), depth)
        ]
        return remote(src, h_at(spot, k), sends.at[0], he_r.at[k], to_inner)

    def h_x(k, row_n):
        return remote(h_at(row_n, k), h_at(row_n, k), sends.at[0], hx_r.at[k], to_x)

    def h_core(k, row_n):
        return remote(h_at(row_n, k), h_at(row_n, k), sends.at[0], joint.at[0], to_core)

    def w_end(j, c):
        part = y if j == 0 else opp
        return remote(wq_at(part, c), w_at(outer, part, c), sends.at[1], we_r.at[j, c], to_inner)

    def w_mid_send(s, c):
        if s == 0:
            return remote(wq_at(y, c), w_at(inner, y, c), sends.at[1], wm_r.at[s, c], to_far)
        return remote(w_at(outer, y, c), w_at(outer, y, c), sends.at[1], wm_r.at[s, c], to_far)

    def far_shard(s):
        return jnp.where(s == 0, far_inner, far_outer)

    def w_mid_recv(s, c):
        ref = w_at(far_shard(s), y, c)
        return remote(ref, ref, sends.at[1], wm_r.at[s, c], to_far)

    def w_y(s, c, part):
        ref = w_at(far_shard(s), part, c)
        return remote(ref, ref, sends.at[1], wy_r.at[s, c], to_y)

    def w_y_outer(c, part):
        ref = w_at(outer, part, c)
        return remote(ref, ref, sends.at[2], w0_r.at[c], to_y)

    def o_end(j, c):
        part = y if j == 0 else opp
        return remote(wo_at(part, c), o_at(outer, part, c), sends.at[4], oe_r.at[c] if j == 0 else joint.at[4 + c // 4 * (1 + 7 * lax.rem(c // 2, 2))], to_inner)

    def o_mid_send(s, c):
        if s == 0:
            return remote(wo_at(y, c), o_at(inner, y, c), sends.at[4], om_r.at[s, c], to_far)
        return remote(o_at(outer, y, c), o_at(outer, y, c), sends.at[4], om_r.at[s, c], to_far)

    def o_mid_direct(c):
        ref = o_at(outer, opp, c)
        return remote(ref, ref, sends.at[4], joint.at[13], to_far)

    def o_mid_recv(s, c):
        ref = o_at(far_shard(s), y, c)
        return remote(ref, ref, sends.at[4], om_r.at[s, c], to_far)

    def o_down(c):
        return remote(wo_at(y, c), o_at(inner, y, c), sends.at[5], od_r.at[c], to_outer)

    def o_y(s, c, part):
        ref = o_at(inner if s == 2 else far_shard(s), part, c)
        place = (1, 2 + c // (2 * sub), 6)[s]
        return remote(ref, ref, sends.at[5 if s == 2 else 4], joint.at[place], to_y)

    def att_at(row_n, g, b):
        return att.at[row_n, g, pl.ds(pl.multiple_of(b * SHIFT, SHIFT), SHIFT)]

    def att_x(g, b, row_n):
        ref = att_at(row_n, g, b)
        return remote(ref, ref, sends.at[6], ax_r.at[g, b], to_x)

    def att_core(g, b, row_n):
        ref = att_at(row_n, g, b)
        return remote(ref, ref, sends.at[6], joint.at[8 + b], to_core)

    def att_end(g, b):
        ref = att_at(spot, g, b)
        return remote(ref, ref, sends.at[7], ae_r.at[g, b], to_outer)

    def share(g, b):
        att_x(g, b, spot).start()
        att_core(g, b, spot).start()

    def relay(g, b):
        att_x(g, b, x_n).wait_recv()
        att_core(g, b, x_n).start()

    def gathered(b):
        arrived(8 + b, att.at[pl.ds(0, narrow // 2), :, pl.ds(pl.multiple_of(b * SHIFT, SHIFT), SHIFT)])

    shards = (inner, far_inner, outer, far_outer)
    slots = ((0, 0, wo_cols), (1, 0, wo_cols)) + tuple((s, k * wo_lanes, wo_lanes) for s in (2, 3) for k in range(2))
    slots += ((2, 0, wo_cols),)

    def res_cols(slot, row_n):
        order, lane, size = slots[slot]
        return pl.ds(pl.multiple_of(shards[order] * cols + row_n * wo_cols + lane, size), size)

    def result(slot, pos, to_n):
        order, lane, size = slots[slot]
        return remote(
            stage.at[order, pl.ds(pl.multiple_of(pos * tok + to_n * quarter, quarter), quarter), lane : lane + size],
            out_ref.at[:, res_cols(slot, spot)],
            sends.at[8], joint.at[7],
            {"wide": side * (n // 2) + pos, "narrow": to_n},
        )

    def product(slot, b, firsts):
        order, lane, size = slots[slot]
        mine = pl.ds(pl.multiple_of(b * SHIFT, SHIFT), SHIFT)
        a_cols = att.shape[3]
        total = None
        for row_half in firsts:
            for p in range(narrow // 2):
                for g in range(2):
                    start = (p * 2 + g) * a_cols
                    term = jnp.dot(
                        att[row_half * (narrow // 2) + p, g, mine],
                        wo_buf[shards[order], row_half, start : start + a_cols, lane : lane + size],
                        preferred_element_type=jnp.float32,
                    )
                    total = term if total is None else total + term
        return total

    def emit(slot, b, total):
        order, lane, size = slots[slot]
        mine = pl.ds(pl.multiple_of(b * SHIFT, SHIFT), SHIFT)
        done = total.astype(jnp.bfloat16)
        stage[order, mine, lane : lane + size] = done
        pos = b // (blocks // 2)
        for k in range(SHIFT // quarter):
            to_n = lax.rem(b, blocks // 2) * (SHIFT // quarter) + k
            here = jnp.logical_and(pos == my_pos, spot == to_n)

            @pl.when(here)
            def _():
                out_ref[:, res_cols(slot, spot)] = done[k * quarter : (k + 1) * quarter]

            @pl.when(jnp.logical_not(here))
            def _():
                result(slot, pos, to_n).start()

    def multiply(slot, b):
        emit(slot, b, product(slot, b, (0, 1)))

    def kv_copy(g):
        return remote(
            kv_buf.at[pl.ds(2 * g, 2), :, pl.ds(span, SHIFT)], kv_buf.at[pl.ds(2 * g, 2), :, pl.ds(0, SHIFT)],
            sends.at[3], kv_r.at[g], to_far,
        )

    barrier = pltpu.get_barrier_semaphore()
    beside = [{"narrow": core_n}, {"narrow": x_n}, {"narrow": diag_n}, to_y]

    def greet(peers):
        for device in peers:
            pl.semaphore_signal(barrier, inc=1, device_id=device, device_id_type=MESH)
        pl.semaphore_wait(barrier, len(peers))

    def own_wo(h):
        return pltpu.make_async_copy(
            wo_ref.at[pl.ds(h * wo_half, wo_half), pl.ds(pl.multiple_of(spot * wo_cols, wo_cols), wo_cols)],
            wo_buf.at[me, h],
            own_sem.at[2 + h],
        )


    @pl.when(is_outer)
    def _():
        greet(beside + [{"wide": inner, "narrow": p} for p in range(narrow)])

        @pl.loop(0, n)
        def _(k):
            h_end(k).start()

        def each_end(act):
            @pl.loop(0, chunks)
            def _(c):
                act(w_end(0, c))

            @pl.loop(0, direct)
            def _(c):
                act(w_end(1, c))

            @pl.loop(row_chunks, chunks)
            def _(c):
                act(w_end(1, c))

            for j, from_c, to_c in ((0, 0, wo_chunks), (1, 6, 8), (1, 4, 6), (1, 0, 4)):
                @pl.loop(from_c, to_c)
                def _(c):
                    act(o_end(j, c))

        each_end(lambda copy: copy.start())
        for h in range(2):
            own_wo(h).start()

        @pl.loop(0, wo_chunks)
        def _(c):
            o_down(c).wait_recv()
            o_y(2, c, y).start()

        arrived(6, wo_buf.at[inner, opp])
        for h in range(2):
            own_wo(h).wait()

        def take(g, b):
            att_end(g, b).wait_recv()
            share(g, b)

        first_b, second_b = side + 1, 3 * side
        take(0, first_b)
        relay(0, first_b)
        take(0, second_b)
        relay(0, second_b)
        take(1, first_b)

        @pl.when(side == 1)
        def _():
            take(1, second_b)

        relay(1, first_b)

        @pl.when(side == 0)
        def _():
            take(1, second_b)

        gathered(first_b)
        multiply(0, first_b)
        multiply(6, first_b)
        relay(1, second_b)
        gathered(second_b)
        multiply(0, second_b)
        multiply(6, second_b)

        sent(0, hid.at[pl.ds(0, quarter)])
        sent(1, wbuf.at[0, :, pl.ds(0, (chunks + direct + row_chunks) * rows)])
        sent(4, wo_buf.at[0])
        sent(5, wo_buf.at[0, 0])
        sent(6, att.at[pl.ds(0, 3), 0])
        sent(8, stage.at[0, pl.ds(0, 2 * (narrow - 1) * quarter)])
        arrived(7, out_ref.at[:, pl.ds(0, (4 * narrow - 2) * wo_cols)])

    @pl.when(is_inner)
    def _():
        own = [
            pltpu.make_async_copy(
                wq_ref.at[:, :, pl.ds(h * HEAD_DIM, HEAD_DIM)],
                wbuf.at[h, :, pl.ds(pl.multiple_of(inner * depth, depth), depth)],
                own_sem.at[0],
            )
            for h in range(heads)
        ]
        own.append(pltpu.make_async_copy(hidden_ref, hid.at[pl.ds(own_row, tok)], own_sem.at[1]))
        small = [
            pltpu.make_async_copy(seg_hbm, seg_ref, own_sem.at[4]),
            pltpu.make_async_copy(shift_hbm, shift_ref, own_sem.at[5]),
        ]
        for copy in own + small:
            copy.start()
        for h in range(2):
            own_wo(h).start()
        greet(beside + [to_far] + [{"wide": outer, "narrow": p} for p in range(narrow)])

        @pl.loop(0, chunks)
        def _(c):
            w_mid_send(0, c).start()

        @pl.loop(0, wo_chunks)
        def _(c):
            o_down(c).start()

        acc[...] = jnp.zeros_like(acc)
        for copy in small:
            copy.wait()
        seg_rows = seg_ref.shape[0]
        lanes = seg_ref.shape[1]
        seg_first = side * (span // lanes)
        for k in range(span // lanes):
            line = seg_ref[pl.ds(seg_first + k, 1), :]
            seg_col[k * lanes : (k + 1) * lanes, :] = jnp.broadcast_to(line, (lanes, lanes)).T

        def add(row, size, shard, part, c):
            start = pl.multiple_of(shard * depth + lax.rem(c, row_chunks) * rows, rows)
            head = c // row_chunks * 2 + part
            here = pl.ds(row, size)
            piece = hid[here, pl.ds(start, rows)]
            both = jnp.concatenate([wbuf[head, i, pl.ds(start, rows)] for i in range(2)], axis=1)
            found = jnp.dot(piece, both, preferred_element_type=jnp.float32)
            acc[head, 0, here] += found[:, :HEAD_DIM]
            acc[head, 1, here] += found[:, HEAD_DIM:]
            acc[head, 2, here] += jnp.dot(piece, wbuf[head, 2, pl.ds(start, rows)], preferred_element_type=jnp.float32)

        def add_all(shard, part, c):
            add(0, span, shard, part, c)

        def add_at(t, shard, part, c):
            @pl.when(t < chunks)
            def _():
                add(own_row, tok, shard, part, c)

            @pl.when(t >= chunks)
            def _():
                add_all(shard, part, c)

        pltpu.make_async_copy(
            wbuf.at[:, :, pl.ds(0, depth)],
            wbuf.at[:, :, pl.ds(pl.multiple_of(inner * depth, depth), depth)],
            own_sem.at[0],
        ).wait()
        own[heads].wait()

        @pl.loop(0, 2 * chunks)
        def _(u):
            add(own_row, tok, inner, u // chunks, lax.rem(u, chunks))

        def own_mid(first, last):
            @pl.loop(first, last)
            def _(c):
                o_mid_send(0, c).start()

        lag = row_chunks
        lead = chunks - 2
        catch_up = 4 * chunks - lag

        @pl.loop(0, 2 * chunks)
        def _(t):
            s, c = t // chunks, lax.rem(t, chunks)
            q = t - lead

            @pl.when(jnp.logical_and(q >= 0, q < chunks))
            def _():
                w_end(0, q).wait_recv()
                w_mid_send(1, q).start()

            @pl.when(jnp.logical_and(q >= direct, q < row_chunks))
            def _():
                w_y_outer(q, y).start()

            w_mid_recv(s, c).wait_recv()
            w_y(s, c, y).start()

            @pl.when(jnp.logical_and(t >= 1, t < 1 + n))
            def _():
                h_end(t - 1).wait_recv()
                h_x(t - 1, spot).start()
                h_core(t - 1, spot).start()

            @pl.when(jnp.logical_and(t >= 4, t < 4 + n))
            def _():
                h_x(t - 4, x_n).wait_recv()
                h_core(t - 4, x_n).start()

            @pl.when(t == chunks)
            def _():
                arrived(0, hid.at[pl.ds(far_row, narrow // 2 * quarter)])

            @pl.when(t == lead + chunks)
            def _():
                own_mid(0, 2)

            add_at(t, far_shard(s), y, c)

            @pl.when(t >= lag)
            def _():
                v = t - lag
                w_y(v // chunks, lax.rem(v, chunks), opp).wait_recv()
                add_at(t, far_shard(v // chunks), opp, lax.rem(v, chunks))

            @pl.when(t >= chunks)
            def _():
                add_all(outer, y, t - chunks)
                u0 = 4 * (t - chunks)

                @pl.loop(u0, jnp.minimum(u0 + 4, catch_up))
                def _(u):
                    turn = u // row_chunks
                    near = lax.rem(turn, 4) < 2
                    part = jnp.where(near, lax.rem(turn, 2), jnp.where(lax.rem(turn, 2) == 0, y, opp))
                    c = lax.rem(u, row_chunks) + turn // 4 * row_chunks
                    add(far_row, tok, jnp.where(near, inner, far_inner), part, c)

            @pl.when(t >= chunks + row_chunks)
            def _():
                k = lax.rem(t - chunks - row_chunks + direct, row_chunks)

                @pl.when(k < direct)
                def _():
                    w_end(1, k).wait_recv()

                @pl.when(k >= direct)
                def _():
                    w_y_outer(k, opp).wait_recv()

                add_all(outer, opp, k)

        causal = lax.broadcasted_iota(jnp.int32, (SHIFT, 2 * SHIFT), 1) <= (
            lax.broadcasted_iota(jnp.int32, (SHIFT, 2 * SHIFT), 0) + SHIFT
        )
        per_block = SHIFT // lanes

        def seg_line(b):
            at = [lax.rem(seg_first + b * per_block + k + seg_rows, seg_rows) for k in range(per_block)]
            return jnp.concatenate([seg_ref[pl.ds(i, 1), :] for i in at], axis=1)

        def attend(g, b):
            mine, seen = slice(b * SHIFT, (b + 1) * SHIFT), slice(b * SHIFT, (b + 2) * SHIFT)
            seg_q = jnp.concatenate([seg_col[mine, :]] * (2 * per_block), axis=1)
            near, prior = seg_line(b), seg_line(b - 1)
            for k in range(2):
                h = 2 * g + k
                reach = shift_ref[spot * heads + h]
                if b % 2 == 1:
                    reach = 1 - reach
                seg_k = jnp.concatenate([prior * reach + (reach - 1), near], axis=1)
                scores = lax.dot_general(
                    q_buf[h, mine], kv_buf[h, 0, seen], (((1,), (1,)), ((), ())),
                    preferred_element_type=jnp.float32,
                ) * (1.0 / math.sqrt(HEAD_DIM))
                allowed = causal & (seg_q == seg_k)
                scores = jnp.where(allowed, scores, masked_out)
                exponent = jnp.exp(scores - jnp.max(scores, axis=-1, keepdims=True))
                weights = exponent / jnp.sum(exponent, axis=-1, keepdims=True)
                att[spot, g, mine, k * HEAD_DIM : (k + 1) * HEAD_DIM] = jnp.dot(
                    weights.astype(jnp.bfloat16), kv_buf[h, 1, seen], preferred_element_type=jnp.float32
                ).astype(jnp.bfloat16)
            share(g, b)

            @pl.when(b // (blocks // 2) == side)
            def _():
                att_end(g, b).start()

        def settle(g):
            for h in (2 * g, 2 * g + 1):
                for i in range(2):
                    kv_buf[h, i, SHIFT:] = acc[h, 1 + i].astype(jnp.bfloat16)
            kv_copy(g).start()
            for h in (2 * g, 2 * g + 1):
                q_buf[h] = acc[h, 0].astype(jnp.bfloat16)

        def multiply_these(slot, first, count):
            @pl.loop(0, count)
            def _(k):
                multiply(slot, lax.rem(first + k, blocks))

        def multiply_own(slot, b):
            @pl.when(b // (blocks // 2) == own_pos)
            def _():
                multiply(slot, b)

        def relay_wo(arrival, *onward):
            def act(i, count):
                @pl.loop(i, i + count)
                def _(c):
                    arrival(c).wait_recv()
                    for copy in onward:
                        copy(c).start()

            return act

        near_wo = relay_wo(lambda c: o_mid_recv(0, c), lambda c: o_y(0, c, y))
        far_wo = relay_wo(lambda c: o_mid_recv(1, c), lambda c: o_y(1, c, y))
        pass_wo = relay_wo(lambda c: o_end(0, c), lambda c: o_mid_send(1, c))

        def half_of(shard, lane_half):
            return wo_buf.at[shard, opp, :, lane_half * wo_lanes : (lane_half + 1) * wo_lanes]

        def corner(shard, row):
            return wo_buf.at[shard, opp, row * 2 * wo_rows : (row + 1) * 2 * wo_rows, wo_lanes:]

        def last_y(c):
            w_y(1, c, opp).wait_recv()
            add_all(far_outer, opp, c)

        def last_end(c):
            w_end(1, c).wait_recv()
            add_all(outer, opp, c)

        settle(0)
        own_mid(2, 7)
        attend(0, 1)
        last_y(row_chunks)
        attend(0, 2)
        last_y(row_chunks + 1)
        attend(0, 3)

        @pl.loop(row_chunks, chunks - 2)
        def _(c):
            last_end(c)

        relay(0, 1)
        kv_copy(0).wait_recv()
        attend(0, 0)
        relay(0, 2)
        last_y(row_chunks + 2)
        last_end(chunks - 2)
        relay(0, 3)
        last_end(chunks - 1)
        near_wo(0, 2)
        last_y(row_chunks + 3)
        settle(1)
        near_wo(2, 2)
        own_mid(7, 8)
        attend(1, 1)
        near_wo(4, 2)
        attend(1, 2)
        relay(0, 0)
        pass_wo(0, 2)
        attend(1, 3)
        near_wo(6, 1)
        for h in range(2):
            own_wo(h).wait()
        pass_wo(2, 2)
        relay(1, 1)
        gathered(1)
        multiply_own(0, 1)
        pass_wo(4, 2)
        kv_copy(1).wait_recv()
        attend(1, 0)
        near_wo(7, 1)
        pass_wo(6, 2)
        relay(1, 2)
        gathered(2)
        multiply_own(0, 2)
        far_wo(0, 2)
        relay(1, 3)
        gathered(3)
        multiply_own(0, 3)
        arrived(1, wo_buf.at[far_inner, opp])
        multiply(1, side + 1)
        far_wo(2, 1)
        relay(1, 0)
        multiply(1, 3)
        far_wo(3, 2)
        gathered(0)
        arrived(12, corner(outer, 1))
        for c in range(wo_chunks - 2, wo_chunks):
            o_mid_direct(c).start()
        multiply(1, 0)
        far_wo(5, 1)
        multiply(1, own_pos + 1)
        multiply_own(0, 0)
        first = side * (blocks // 2)
        arrived(5, corner(outer, 0))
        multiply_these(3, own_pos * (blocks // 2), blocks // 2)
        arrived(2, half_of(far_outer, 0))
        multiply_these(4, first, blocks)
        for c in range(wo_chunks - 2, wo_chunks):
            o_mid_recv(1, c).wait_recv()

        @pl.loop(0, blocks)
        def _(b):
            early[b] = product(5, b, (y,))

        arrived(3, corner(far_outer, 0))
        arrived(13, corner(far_outer, 1))

        def last_piece(begin):
            @pl.loop(0, blocks // 2)
            def _(turn):
                b = begin + turn
                emit(5, b, early[b] + product(5, b, (opp,)))

        last_piece(first)
        arrived(4, half_of(outer, 0))
        multiply_these(2, own_pos * (blocks // 2), blocks // 2)
        last_piece(own_pos * (blocks // 2))

        sent(0, hid.at[pl.ds(0, 3 * quarter)])
        sent(1, wbuf.at[pl.ds(0, 2)])
        sent(2, wbuf.at[0, :, pl.ds(0, (row_chunks - direct) * rows)])
        sent(3, kv_buf.at[:, :, pl.ds(0, SHIFT)])
        sent(4, wo_buf.at[pl.ds(0, 2)])
        sent(5, wo_buf.at[0, 0])
        sent(6, att.at[pl.ds(0, 3)])
        sent(7, att.at[0, 0])
        pieces = 4 * (narrow - 1) + 2 * narrow
        sent(8, hid.at[pl.ds(0, pieces * quarter * wo_cols // hid.shape[1])])
        arrived(7, out_ref.at[:, pl.ds(0, 4 * (narrow - 1) * wo_cols)])


def hub_layer(hidden, wq, wo, seg, shift_heads):
    n, narrow = lax.axis_size("wide"), lax.axis_size("narrow")
    tok, width = hidden.shape
    heads = wq.shape[2] // HEAD_DIM
    row_chunks = wq.shape[1] // HUB_ROWS
    chunks, wo_chunks = 2 * row_chunks, 8
    cols = wo.shape[1]
    wo_half, wo_cols = wo.shape[0] // 2, cols // narrow
    quarter, span = tok // narrow, 2 * tok
    blocks = span // SHIFT
    vmem = pl.BlockSpec(memory_space=pltpu.VMEM)
    hbm = pl.BlockSpec(memory_space=pl.ANY)
    dma = pltpu.SemaphoreType.DMA
    bf16 = jnp.bfloat16
    return pl.pallas_call(
        functools.partial(hub_kernel, row_chunks, DIRECT),
        out_shape=pltpu.VMEM((quarter, n * cols), bf16),
        in_specs=[hbm] * 5,
        out_specs=vmem,
        scratch_shapes=[
            pltpu.VMEM((heads, 3, width, HEAD_DIM), bf16),
            pltpu.VMEM((span, width), bf16),
            pltpu.VMEM((heads, 3, span, HEAD_DIM), jnp.float32),
            pltpu.VMEM((heads, span, HEAD_DIM), bf16),
            pltpu.VMEM((heads, 2, span + SHIFT, HEAD_DIM), bf16),
            pltpu.VMEM((narrow, 2, span, 2 * HEAD_DIM), bf16),
            pltpu.VMEM((n, 2, wo_half, wo_cols), bf16),
            pltpu.VMEM((n, span, wo_cols), bf16),
            pltpu.VMEM((blocks, SHIFT, wo_cols // 2), jnp.float32),
            pltpu.VMEM((span, seg.shape[1]), jnp.int32),
            pltpu.VMEM(seg.shape, jnp.int32),
            pltpu.SMEM(shift_heads.shape, jnp.int32),
            dma((6,)),
            dma((9,)),
            dma((10 + blocks,)),
        ]
        + [dma((n,))] * 2
        + [dma((2, chunks))] * 3
        + [dma((row_chunks,)), dma((2,)), dma((2, wo_chunks)), dma((wo_chunks,)), dma((wo_chunks,))]
        + [dma((2, blocks))] * 2,
        compiler_params=pltpu.CompilerParams(
            collective_id=0, has_side_effects=True, vmem_limit_bytes=58 * 1024 * 1024
        ),
    )(hidden, wq, wo, seg, shift_heads)


def hub_per_device(hidden, w_qkv, w_out, seg_ids, shift_heads):
    return hub_layer(hidden, w_qkv.transpose(1, 0, 2), w_out, seg_ids.reshape(-1, 128), shift_heads)


def solution(mesh):
    placed = (
        P(("groups", "wide"), None),
        P("wide", None, "narrow"),
        P(None, "wide"),
        P("groups"),
        P(),
    )
    shape = mesh.shape
    hub = shape["groups"] == 2 and shape["wide"] == 4 and shape["narrow"] == 4
    return jax.shard_map(
        hub_per_device if hub else per_device,
        mesh=mesh,
        in_specs=placed,
        out_specs=P(("groups", "wide", "narrow"), None),
        check_vma=False,
    )
```
